32 devices in a mesh: dp: 16 (over z, y, x), mp: 2 (over core).
Axes of the slice: x: 2, y: 2, z: 4, core: 2. Of those that a mesh axis runs over, the one named last changes fastest.
Arguments:
- tokens: bfloat16 [32768, 768], P('dp'), may hold values from -6 to 6
- segments: int32 [32768], P('dp'), may hold values from 0 to 32, as said below
- sentence_dest: int32 [2048, 2], P('dp'), may hold values from 0 to 15, as said below
- pair_source: int32 [2048, 2], P('dp'), may hold values from 0 to 15, as said below
- labels: int32 [1024], P('dp'), may hold values from 0 to 5
- params: float32 [2, 3541248], P('mp', 'dp'), as said below
- first: float32 [2, 3541248], P('mp', 'dp')
- second: float32 [2, 3541248], P('mp', 'dp'), as said below
- shared: float32 [6, 768], replicated, as said below
- shared_first: float32 [6, 768], replicated
- shared_second: float32 [6, 768], replicated, as said below
Outputs:
- encoded: bfloat16 [32768, 768], P('dp')
- input_grad: float32 [32768, 768], P('dp')
- grad_norm: float32 [1], replicated
- params_new: float32 [2, 3541248], P('mp', 'dp')
- first_new: float32 [2, 3541248], P('mp', 'dp')
- second_new: float32 [2, 3541248], P('mp', 'dp')
- params_low: bfloat16 [2, 3541248], P('mp', 'dp')
- shared_new: float32 [6, 768], replicated
- shared_first_new: float32 [6, 768], replicated
- shared_second_new: float32 [6, 768], replicated
- params_grad: float32 [2, 3541248], P('mp', 'dp')
- shared_grad: float32 [6, 768], replicated
The draws below stay inside these ranges and needn't reach their ends.
Inputs may be any that keep to these rules, and one draw needn't show every extreme that they name: `segments`: within each row of 512 positions ids never fall; each id 0 to 31 covers 1 to 16 positions and slot 0 exactly 16; id 32 marks the padding at a row's end. `sentence_dest`: column 0 is the scoring device, column 1 the place 0 to 7 among the sentences that this device sends there; each device sends exactly 8 or none of its sentences to each device, and each (device, place) occurs once per sender. `pair_source`: column 0 is the sending device, column 1 the place; each names a sentence whose sentence_dest points to this device and place, every sentence exactly once; items 2j and 2j+1 form pair j. `params`: laid out as the steps say. `second`: Positive. `shared`: Rows: first gain, first bias, second gain, second bias, attention output bias, feed-forward output bias. `shared_second`: Positive.
All inputs are finite; a program needn't handle non-finite values.
Results may differ from the reference program's by a relative error of at most 0.018.
Values may be sent and summed in bfloat16 or wider, within the bound.
A program may use at most 256 MiB of HBM per device.

```python
import math
import jax
import jax.numpy as jnp
from jax import lax

D = 768
HEAD_DIM = 64
FF = 3072
ROW = 512
SEG = 32
RPM = 2
MB = 2
MAXLEN = 16
HCOLS = 384
FCOLS = 1536
HEADS_DEV = 6
SENT = 128
PAIRS = 64
CAP = 8
PARAMS_HALF = 3541248
PARAMS_ALL = 7087104
TOKENS = 32768
N_DP = 16
N_MP = 2


CLIP_NORM = 0.5


FIRST_SHARE = 0.1 / 0.9


SECOND_SHARE = 0.001 / 0.999


def rough_draw(key, shape):
    return jnp.clip(jax.random.normal(key, shape, jnp.float32), -5.0, 5.0)


def region_scale(matrix_scales, bias_scale):
    cut_one = 3 * D * HCOLS
    cut_two = cut_one + HCOLS * D
    cut_three = cut_two + D * FCOLS
    cut_four = cut_three + FCOLS * D
    position_ids = jnp.arange(PARAMS_HALF)
    scaled = jnp.where(position_ids < cut_four, matrix_scales[3], bias_scale)
    scaled = jnp.where(position_ids < cut_three, matrix_scales[2], scaled)
    scaled = jnp.where(position_ids < cut_two, matrix_scales[1], scaled)
    scaled = jnp.where(position_ids < cut_one, matrix_scales[0], scaled)
    return scaled.astype(jnp.float32)[None, :]


def grad_size():
    return CLIP_NORM / math.sqrt(PARAMS_ALL)


def draw_params(key, part):
    scales = region_scale((D ** (-0.5), 3.0 * D ** (-0.5), D ** (-0.5), 1.5 * FF ** (-0.5)), 0.3)
    return rough_draw(key, (N_MP, PARAMS_HALF)) * scales


def draw_first(key, part):
    size_one = grad_size()
    scales = region_scale((size_one, size_one, size_one, size_one), 4.0 * size_one)
    return FIRST_SHARE * rough_draw(key, (N_MP, PARAMS_HALF)) * scales


def draw_second(key, part):
    size_one = grad_size()
    scales = region_scale((size_one, size_one, size_one, size_one), 4.0 * size_one)
    return jax.random.uniform(key, (N_MP, PARAMS_HALF), jnp.float32, 1.0, 4.0) * SECOND_SHARE * scales * scales


def draw_shared(key, part):
    row_ids = jnp.arange(6)[:, None]
    noise = rough_draw(key, (6, D))
    is_gain = (row_ids == 0) | (row_ids == 2)
    return jnp.where(is_gain, 1.0 + 0.1 * noise, 0.2 * noise)


def draw_shared_first(key, part):
    return FIRST_SHARE * 4.0 * grad_size() * rough_draw(key, (6, D))


def draw_shared_second(key, part):
    size_four = 4.0 * grad_size()
    return jax.random.uniform(key, (6, D), jnp.float32, 1.0, 4.0) * SECOND_SHARE * size_four * size_four


def draw_segments(key, part):
    row_count = N_DP * MB * RPM
    key_bucket, key_short, key_long = jax.random.split(key, 3)
    longer = jax.random.randint(key_bucket, (N_DP, 1, 1), 0, 2)
    longer = jnp.broadcast_to(longer, (N_DP, MB * RPM, 1)).reshape(row_count, 1)
    short_len = jax.random.randint(key_short, (row_count, SEG), 1, MAXLEN // 2 + 1)
    long_len = jax.random.randint(key_long, (row_count, SEG), MAXLEN // 2, MAXLEN + 1)
    lengths = jnp.where(longer == 1, long_len, short_len)
    lengths = lengths.at[:, 0].set(MAXLEN)
    end_pos = jnp.cumsum(lengths, axis=1)
    position_ids = jnp.arange(ROW, dtype=jnp.int32)
    segment_ids = jnp.sum((position_ids[None, :, None] >= end_pos[:, None, :]).astype(jnp.int32), axis=2)
    return segment_ids.reshape(TOKENS).astype(jnp.int32)


def shuffle_slots(sub_key):
    return jax.random.permutation(sub_key, SENT)


def route_tables(key):
    base_key = jax.random.fold_in(key, 11)
    key_offset, key_send, key_recv = jax.random.split(base_key, 3)
    groups = SENT // CAP
    ranking = jax.random.permutation(key_offset, N_DP).astype(jnp.int32)
    ranking = ranking.at[1].set(-3).at[N_DP - 1].set(-2).at[N_DP // 2].set(-1)
    offsets = jnp.argsort(ranking)[:groups].astype(jnp.int32)
    devices = jnp.arange(N_DP, dtype=jnp.int32)[:, None]
    send_perm = jax.vmap(shuffle_slots)(jax.random.split(key_send, N_DP)).astype(jnp.int32)
    position = jnp.argsort(send_perm, axis=1).astype(jnp.int32)
    target_dev = (devices + offsets[position // CAP]) % N_DP
    rank_in = position % CAP
    senders = jnp.stack([target_dev, rank_in], -1).reshape(N_DP * SENT, 2)
    recv_perm = jax.vmap(shuffle_slots)(jax.random.split(key_recv, N_DP)).astype(jnp.int32)
    source = (devices - offsets[recv_perm // CAP]) % N_DP
    receivers = jnp.stack([source, recv_perm % CAP], -1).reshape(N_DP * SENT, 2)
    return (senders.astype(jnp.int32), receivers.astype(jnp.int32))


def draw_sentence_dest(key, part):
    return route_tables(key)[0]


def draw_pair_source(key, part):
    return route_tables(key)[1]


def set_ends(drawn, stream_key, low, top_value):
    dims = drawn.shape
    spot = [jax.random.randint(jax.random.fold_in(stream_key, axis), (), 0, dims[axis]) for axis in range(len(dims))]
    drawn = drawn.at[tuple(spot)].set(low)
    longest = dims.index(max(dims))
    spot[longest] = (spot[longest] + 1) % dims[longest]
    return drawn.at[tuple(spot)].set(top_value)


def block_scale(stream_key, shape, cuts, low, top_value):
    gain = 1.0
    for axis_at, parts in cuts:
        heights = jax.random.uniform(jax.random.fold_in(jax.random.fold_in(stream_key, 6), axis_at), (parts,), jnp.float32, low / len(cuts), top_value / len(cuts))
        gain = gain * jnp.repeat(jnp.exp(heights), shape[axis_at] // parts).reshape((-1,) + (1,) * (len(shape) - 1 - axis_at))
    return gain


def gaussian(stream_key, shape, scale, most, shards=(), kind=jnp.bfloat16):
    result = jax.random.normal(stream_key, shape, jnp.float32) * scale
    if len(shards) > 0:
        result = block_scale(stream_key, shape, shards, -0.22, 0.18) * result
    return jnp.clip(result, min=-most, max=most).astype(kind)


def setup_inputs(seed: int = 0) -> dict:
    keys = jax.random.split(jax.random.key(seed), 12)
    tokens = gaussian(keys[0], (TOKENS, D), 1.0, 6.0, ((0, 16),))
    segments = draw_segments(jax.random.fold_in(keys[11], 71), 0)
    sentence_dest = draw_sentence_dest(jax.random.fold_in(keys[11], 71), 0)
    pair_source = draw_pair_source(jax.random.fold_in(keys[11], 71), 0)
    labels = set_ends(jax.random.randint(keys[4], (N_DP * PAIRS,), 0, 6), jax.random.fold_in(keys[4], 1), 0, 5).astype(jnp.int32)
    params = draw_params(jax.random.fold_in(keys[11], 71), 0)
    first = draw_first(jax.random.fold_in(keys[11], 71), 0)
    second = draw_second(jax.random.fold_in(keys[11], 71), 0)
    shared = draw_shared(jax.random.fold_in(keys[11], 71), 0)
    shared_first = draw_shared_first(jax.random.fold_in(keys[11], 71), 0)
    shared_second = draw_shared_second(jax.random.fold_in(keys[11], 71), 0)
    return dict(tokens=tokens, segments=segments, sentence_dest=sentence_dest, pair_source=pair_source, labels=labels, params=params, first=first, second=second, shared=shared, shared_first=shared_first, shared_second=shared_second)


LOSS_SCALE = 1024.0
CLIP_NORM = 0.5
LEARN_RATE = 0.1
SHARED_RATE = 0.5
BETA_ONE = 0.9
BETA_TWO = 0.999
ADAM_EPS = 1e-08
DECAY = 0.01
NORM_EPS = 1e-12
STEP_COUNT = 10.0
TOP_PRECISION = lax.Precision.HIGHEST

@jax.custom_vjp
def low(v):
    return lax.optimization_barrier(v.astype(jnp.bfloat16)).astype(jnp.float32)

@jax.custom_vjp
def low_back(v):
    return v

def low_keep(v):
    return (low(v), None)

def low_pass(kept, grad):
    return (grad,)

def back_keep(v):
    return (v, None)

def back_low(kept, grad):
    return (low(grad),)
low.defvjp(low_keep, low_pass)
low_back.defvjp(back_keep, back_low)

def matmul(left_mat, right_mat):
    return jnp.matmul(left_mat, right_mat, precision=TOP_PRECISION)

def both_round(values_in):
    return low(low_back(values_in))

def normalize(values_in, scale_vec, shift_vec):
    center = lax.optimization_barrier(jnp.mean(values_in, -1, keepdims=True))
    centered = values_in - center
    spread = lax.optimization_barrier(jnp.mean(centered * centered, -1, keepdims=True))
    return centered * lax.rsqrt(spread + NORM_EPS) * scale_vec + shift_vec

def unpack(packed):
    pieces = []
    offset = 0
    for height, extent in ((D, 3 * HCOLS), (HCOLS, D), (D, FCOLS), (FCOLS, D)):
        pieces.append(packed[offset:offset + height * extent].reshape(height, extent))
        offset = offset + height * extent
    for extent in (HCOLS, HCOLS, FCOLS):
        pieces.append(packed[offset:offset + extent])
        offset = offset + extent
    return pieces

def encode(tokens_row, segment_row, halves, shared):
    same_doc = (segment_row[:, None] == segment_row[None, :])[None]
    score_scale = HEAD_DIM ** (-0.5)
    attn_out = jnp.zeros((ROW, D), jnp.float32)
    for w_qkv, w_attn, w_in, w_out, b_query, b_value, b_in in halves:
        tokens_half = low_back(tokens_row)
        projected = matmul(tokens_half, w_qkv)
        queries = both_round(projected[:, :HCOLS] + b_query).reshape(ROW, HEADS_DEV, HEAD_DIM)
        keys_low = both_round(projected[:, HCOLS:2 * HCOLS]).reshape(ROW, HEADS_DEV, HEAD_DIM)
        values_low = both_round(projected[:, 2 * HCOLS:] + b_value).reshape(ROW, HEADS_DEV, HEAD_DIM)
        scores = low_back(jnp.einsum('qhd,khd->hqk', queries, keys_low, precision=TOP_PRECISION) * score_scale)
        scores = jnp.where(same_doc, scores, -1e+30)
        row_max = lax.optimization_barrier(jnp.max(scores, -1, keepdims=True))
        exponent = jnp.exp(scores - row_max)
        attn_probs = low(exponent / lax.optimization_barrier(jnp.sum(exponent, -1, keepdims=True)))
        mixed_heads = jnp.einsum('hqk,khd->qhd', attn_probs, values_low, precision=TOP_PRECISION)
        mixed_heads = both_round(mixed_heads.reshape(ROW, HCOLS))
        attn_out = attn_out + low(matmul(mixed_heads, w_attn))
    attn_out = low_back(attn_out + shared[4])
    hidden = normalize(tokens_row + attn_out, shared[0], shared[1])
    ffn_out = jnp.zeros((ROW, D), jnp.float32)
    for w_qkv, w_attn, w_in, w_out, b_query, b_value, b_in in halves:
        hidden_half = low_back(low(hidden))
        up_proj = low_back(matmul(hidden_half, w_in) + b_in)
        activated = low(jax.nn.gelu(up_proj, approximate=False))
        ffn_out = ffn_out + low(matmul(activated, w_out))
    ffn_out = low_back(ffn_out + shared[5])
    encoded_row = normalize(hidden + ffn_out, shared[2], shared[3])
    onehot = (segment_row[None, :] == jnp.arange(SEG, dtype=jnp.int32)[:, None]).astype(jnp.float32)
    counts = lax.optimization_barrier(jnp.sum(onehot, 1, keepdims=True))
    pooled = both_round(matmul(onehot / counts, encoded_row))
    return (encoded_row, pooled)

def pair_loss(pair_items, labels):
    first_vec = pair_items[..., 0::2, :]
    second_vec = pair_items[..., 1::2, :]
    inner_prod = lax.optimization_barrier(jnp.sum(first_vec * second_vec, -1))
    cosine = inner_prod * lax.rsqrt(lax.optimization_barrier(jnp.sum(first_vec * first_vec, -1)) + 1e-06) * lax.rsqrt(lax.optimization_barrier(jnp.sum(second_vec * second_vec, -1)) + 1e-06)
    error_term = cosine - labels.astype(jnp.float32) / 5.0
    return LOSS_SCALE * jnp.sum(error_term * error_term)

def adamw(weight, moment_one, moment_two, gradient, factor, step_count, rate):
    clipped = gradient * factor
    first_new = BETA_ONE * moment_one + (1.0 - BETA_ONE) * clipped
    second_new = BETA_TWO * moment_two + (1.0 - BETA_TWO) * clipped * clipped
    first_hat = first_new / (1.0 - BETA_ONE ** step_count)
    second_hat = second_new / (1.0 - BETA_TWO ** step_count)
    weight_new = weight - rate * (first_hat / (jnp.sqrt(second_hat) + ADAM_EPS) + DECAY * weight)
    return (weight_new, first_new, second_new)

def reference(tokens, segments, sentence_dest, pair_source, labels, params, first, second, shared, shared_first, shared_second):
    rows_in = tokens.astype(jnp.float32).reshape(N_DP * MB * RPM, ROW, D)
    segment_rows = segments.reshape(N_DP * MB * RPM, ROW)
    sender = jnp.repeat(jnp.arange(N_DP, dtype=jnp.int32), SENT)
    send_code = (sentence_dest[:, 0] * N_DP + sender) * CAP + sentence_dest[:, 1]
    sort_order = jnp.argsort(send_code)
    sorted_code = send_code[sort_order]
    want_code = (sender * N_DP + pair_source[:, 0]) * CAP + pair_source[:, 1]
    found_at = jnp.searchsorted(sorted_code, want_code)
    index_overall = sort_order[found_at]
    label_rows = labels.reshape(N_DP, PAIRS)

    def total_loss(inputs_f, params_f, shared_f):
        halves = [unpack(low(params_f[half_index])) for half_index in range(N_MP)]

        def one_row(pair_in):
            return encode(pair_in[0], pair_in[1], halves, shared_f)
        encoded_rows, pooled = lax.map(jax.checkpoint(one_row), (inputs_f, segment_rows))
        pair_items = pooled.reshape(N_DP * SENT, D)[index_overall].reshape(N_DP, SENT, D)
        return (pair_loss(pair_items, label_rows), encoded_rows)
    loss_value, back_fn, encoded_rows = jax.vjp(total_loss, rows_in, params, shared, has_aux=True)
    grad_rows, grad_params, grad_shared = back_fn(jnp.ones_like(loss_value))
    grad_params = grad_params / LOSS_SCALE
    grad_shared = grad_shared / LOSS_SCALE
    norm_value = jnp.sqrt(jnp.sum(grad_params * grad_params) + jnp.sum(grad_shared * grad_shared))
    factor = jnp.minimum(1.0, CLIP_NORM / norm_value)
    step_count = STEP_COUNT
    params_new, first_new, second_new = adamw(params, first, second, grad_params, factor, step_count, LEARN_RATE)
    shared_new, shared_first_new, shared_second_new = adamw(shared, shared_first, shared_second, grad_shared, factor, step_count, SHARED_RATE)
    grad_unit = math.sqrt(PARAMS_ALL) / CLIP_NORM
    params_grad = grad_params * factor * grad_unit
    shared_grad = grad_shared * factor * grad_unit
    return (encoded_rows.reshape(TOKENS, D).astype(jnp.bfloat16), grad_rows.reshape(TOKENS, D), norm_value.reshape(1), params_new, first_new, second_new, params_new.astype(jnp.bfloat16), shared_new, shared_first_new, shared_second_new, params_grad, shared_grad)
```

```python
from functools import partial
import math

import jax
import jax.numpy as jnp
from jax import lax
from jax.experimental import pallas as pl
from jax.experimental.pallas import tpu as pltpu
from jax.sharding import PartitionSpec as P

HEAD_DIM = 64
FF = 3072
ROW = 512
SEG = 32
RPM = 2
MB = 2
MP = 2
LANES = 128
ROWS_DEV = MB * RPM
ROWS_CORE = ROWS_DEV // MP


LOSS_SCALE = 1024.0
CLIP_NORM = 0.5
LEARN_RATE = 0.1
SHARED_RATE = 0.5
BETA_ONE = 0.9
BETA_TWO = 0.999
ADAM_EPS = 1e-08
DECAY = 0.01
NORM_EPS = 1e-12
STEP_COUNT = 10.0
TOP_PRECISION = lax.Precision.HIGHEST
MESH = pl.DeviceIdType.MESH
DMA = pltpu.SemaphoreType.DMA
VMEM_LIMIT = 60 << 20


def normalize(values_in, scale_vec, shift_vec):
    center = jnp.mean(values_in, -1, keepdims=True)
    centered = values_in - center
    spread = jnp.mean(centered * centered, -1, keepdims=True)
    return centered * lax.rsqrt(spread + NORM_EPS) * scale_vec + shift_vec


def pair_loss(pair_items, labels):
    first_vec = pair_items[..., 0::2, :]
    second_vec = pair_items[..., 1::2, :]
    inner_prod = jnp.sum(first_vec * second_vec, -1)
    cosine = (
        inner_prod
        * lax.rsqrt(jnp.sum(first_vec * first_vec, -1) + 1e-06)
        * lax.rsqrt(jnp.sum(second_vec * second_vec, -1) + 1e-06)
    )
    error_term = cosine - labels.astype(jnp.float32) / 5.0
    return LOSS_SCALE * jnp.sum(error_term * error_term)


def adamw(weight, moment_one, moment_two, gradient, factor, step_count, rate):
    clipped = gradient * factor
    first_new = BETA_ONE * moment_one + (1.0 - BETA_ONE) * clipped
    second_new = BETA_TWO * moment_two + (1.0 - BETA_TWO) * clipped * clipped
    first_hat = first_new / (1.0 - BETA_ONE**step_count)
    second_hat = second_new / (1.0 - BETA_TWO**step_count)
    weight_new = weight - rate * (first_hat / (jnp.sqrt(second_hat) + ADAM_EPS) + DECAY * weight)
    return (weight_new, first_new, second_new)


class Layout:
    def __init__(self, features, shard, dp_count):
        self.features = features
        self.shard = shard
        self.dp_count = dp_count
        self.head_cols = features // MP
        self.ffn_cols = FF // MP
        self.total = shard * dp_count
        self.lines = self.total // LANES
        assert self.lines * LANES == self.total
        self.starts = [index * shard // LANES for index in range(dp_count)]
        need = max(
            ((index + 1) * shard - 1) // LANES - index * shard // LANES + 1
            for index in range(dp_count)
        )
        self.length = -(-need // 16) * 16
        self.cut = -(-self.length // 32) * 16
        self.mats = []
        offset = 0
        for height, extent in (
            (features, 3 * self.head_cols),
            (self.head_cols, features),
            (features, self.ffn_cols),
            (self.ffn_cols, features),
        ):
            assert extent % LANES == 0 and height % LANES == 0
            self.mats.append((offset, height, extent // LANES))
            offset += height * (extent // LANES)
        self.bias_start = offset
        self.bias_lines = self.lines - offset
        self.bias_rows = -(-self.bias_lines // 8) * 8
        self.flat_rows = -(-(self.starts[-1] + self.length) // 8) * 8


def weight_specs(lay):
    specs = [
        pl.BlockSpec((lay.features, 3 * lay.head_cols), lambda half: (0, half)),
        pl.BlockSpec((lay.head_cols, lay.features), lambda half: (half, 0)),
        pl.BlockSpec((lay.features, lay.ffn_cols), lambda half: (0, half)),
        pl.BlockSpec((lay.ffn_cols, lay.features), lambda half: (half, 0)),
        pl.BlockSpec((1, lay.bias_rows, LANES), lambda half: (half, 0, 0)),
    ]
    shapes = [
        (lay.features, MP * 3 * lay.head_cols),
        (MP * lay.head_cols, lay.features),
        (lay.features, MP * lay.ffn_cols),
        (MP * lay.ffn_cols, lay.features),
    ]
    return specs, shapes


def unpack_kernel(lay, lines_ref, qkv_ref, attn_ref, in_ref, out_ref, bias_ref, flat):
    for index in range(lay.dp_count):
        start = lay.starts[index]
        if index > 0:
            kept = flat[start : start + 1, :]
        flat[start : start + lay.length, :] = lines_ref[0, index].astype(jnp.float32)
        if index > 0:
            flat[start : start + 1, :] += kept
    for (offset, height, cols), ref in zip(lay.mats, (qkv_ref, attn_ref, in_ref, out_ref)):

        def body(step, carry, offset=offset, cols=cols, ref=ref):
            row = pl.multiple_of(step * LANES, LANES)
            for col in range(cols):
                block = flat[pl.ds(offset + row * cols + col, LANES, stride=cols), :]
                ref[pl.ds(row, LANES), col * LANES : (col + 1) * LANES] = block.astype(
                    jnp.bfloat16
                )
            return carry

        lax.fori_loop(0, height // LANES, body, 0)
    bias_ref[0] = flat[lay.bias_start : lay.bias_start + lay.bias_rows, :]


def unpack_weights(lay, gathered):
    specs, shapes = weight_specs(lay)
    return pl.pallas_call(
        partial(unpack_kernel, lay),
        grid=(MP,),
        in_specs=[
            pl.BlockSpec((1, lay.dp_count, lay.length, LANES), lambda half: (half, 0, 0, 0))
        ],
        out_specs=specs,
        out_shape=[jax.ShapeDtypeStruct(s, jnp.bfloat16) for s in shapes]
        + [jax.ShapeDtypeStruct((MP, lay.bias_rows, LANES), jnp.float32)],
        scratch_shapes=[pltpu.VMEM((lay.flat_rows, LANES), jnp.float32)],
        compiler_params=pltpu.CompilerParams(vmem_limit_bytes=VMEM_LIMIT),
        name="unpack_weights",
    )(gathered)


def pack_kernel(lay, qkv_ref, attn_ref, in_ref, out_ref, bias_ref, lines_ref, flat):
    for (offset, height, cols), ref in zip(lay.mats, (qkv_ref, attn_ref, in_ref, out_ref)):

        def body(step, carry, offset=offset, cols=cols, ref=ref):
            row = pl.multiple_of(step * LANES, LANES)
            for col in range(cols):
                block = ref[pl.ds(row, LANES), col * LANES : (col + 1) * LANES]
                flat[pl.ds(offset + row * cols + col, LANES, stride=cols), :] = block.astype(
                    jnp.float32
                )
            return carry

        lax.fori_loop(0, height // LANES, body, 0)
    tail = lay.flat_rows - lay.lines
    if tail:
        flat[lay.lines :, :] = jnp.zeros((tail, LANES), jnp.float32)
    flat[lay.bias_start : lay.lines, :] = bias_ref[0, : lay.bias_lines]
    for index in range(lay.dp_count):
        start = lay.starts[index]
        lines_ref[0, index] = flat[start : start + lay.length, :].astype(jnp.bfloat16)


def pack_gradients(lay, grads, bias_grad):
    specs, _ = weight_specs(lay)
    return pl.pallas_call(
        partial(pack_kernel, lay),
        grid=(MP,),
        in_specs=specs,
        out_specs=pl.BlockSpec(
            (1, lay.dp_count, lay.length, LANES), lambda half: (half, 0, 0, 0)
        ),
        out_shape=jax.ShapeDtypeStruct((MP, lay.dp_count, lay.length, LANES), jnp.bfloat16),
        scratch_shapes=[pltpu.VMEM((lay.flat_rows, LANES), jnp.float32)],
        compiler_params=pltpu.CompilerParams(vmem_limit_bytes=VMEM_LIMIT),
        name="pack_gradients",
    )(*grads, bias_grad)


class Place:
    def __init__(self):
        self.dp = lax.axis_index("dp")
        self.half = lax.axis_index("mp")
        self.z = self.dp // 4
        self.y = (self.dp // 2) % 2
        self.x = self.dp % 2
        self.has_up = self.z < 3
        self.has_down = self.z > 0
        self.up = (jnp.minimum(self.dp + 4, 12 + self.dp % 4), self.half)
        self.down = (jnp.maximum(self.dp - 4, self.dp % 4), self.half)
        self.xn = (self.shard(self.z, self.y, 1 - self.x), self.half)
        self.yn = (self.shard(self.z, 1 - self.y, self.x), self.half)
        self.sib = (self.dp, 1 - self.half)

    def shard(self, z, y, x):
        return z * 4 + y * 2 + x

    def barrier(self):
        bar = pltpu.get_barrier_semaphore()
        for dev in (self.xn, self.yn, self.sib):
            pl.semaphore_signal(bar, inc=1, device_id=dev, device_id_type=MESH)

        @pl.when(self.has_up)
        def _():
            pl.semaphore_signal(bar, inc=1, device_id=self.up, device_id_type=MESH)

        @pl.when(self.has_down)
        def _():
            pl.semaphore_signal(bar, inc=1, device_id=self.down, device_id_type=MESH)

        pl.semaphore_wait(
            bar, 3 + jnp.where(self.has_up, 1, 0) + jnp.where(self.has_down, 1, 0)
        )


def guarded(cond, work):
    if cond is None:
        work()
    else:
        pl.when(cond)(work)


def gather_kernel(
    lay, own_ref, buf, zs_sem, zr_sem, xs_sem, xr_sem, ys_sem, yr_sem, ss_sem, sr_sem, loc_sem
):
    at = Place()
    halves = ((0, lay.cut), (lay.cut, lay.length - lay.cut))
    local = pltpu.make_async_copy(own_ref, buf.at[at.half, at.dp], loc_sem)
    local.start()
    at.barrier()
    local.wait()
    sends = []

    def remote(index, part, send_sem, recv_sem, dev):
        piece = buf.at[at.half, index, pl.ds(*halves[part])]
        return pltpu.make_async_remote_copy(
            src_ref=piece,
            dst_ref=piece,
            send_sem=send_sem,
            recv_sem=recv_sem,
            device_id=dev,
            device_id_type=MESH,
        )

    def send(index, part, send_sem, recv_sem, dev, cond=None):
        guarded(cond, lambda: remote(index, part, send_sem, recv_sem, dev).start())
        sends.append((cond, lambda: remote(index, part, send_sem, recv_sem, dev).wait_send()))

    def wait(index, part, send_sem, recv_sem, dev, cond=None):
        guarded(cond, lambda: remote(index, part, send_sem, recv_sem, dev).wait_recv())

    def share(index, part, cond=None):
        send(index, part, ss_sem.at[index, part], sr_sem.at[index, part], at.sib, cond)

    for part in range(2):
        send(at.dp, part, zs_sem.at[0, 0, part], zr_sem.at[0, 1, part], at.up, at.has_up)
        send(at.dp, part, zs_sem.at[1, 0, part], zr_sem.at[1, 1, part], at.down, at.has_down)
        send(at.dp, part, xs_sem.at[at.z, part], xr_sem.at[at.z, part], at.xn)
        send(at.dp, part, ys_sem.at[at.z, part], yr_sem.at[at.z, part], at.yn)
        share(at.dp, part)

    def chain(dist):
        for part in range(2):
            for down in range(2):
                src = at.z + dist if down else at.z - dist
                ok = (src <= 3) if down else (src >= 0)
                src = jnp.clip(src, 0, 3)
                index = at.shard(src, at.y, at.x)
                dev = at.down if down else at.up
                onward = at.has_down if down else at.has_up
                wait(
                    index, part, zs_sem.at[down, 0, part], zr_sem.at[down, dist, part], dev, ok
                )
                if dist < 3:
                    send(
                        index,
                        part,
                        zs_sem.at[down, dist, part],
                        zr_sem.at[down, dist + 1, part],
                        dev,
                        ok & onward,
                    )
                send(index, part, xs_sem.at[src, part], xr_sem.at[src, part], at.xn, ok)
                send(index, part, ys_sem.at[src, part], yr_sem.at[src, part], at.yn, ok)
                share(index, part, ok)

    def sources(dist):
        if dist == 0:
            return [(at.z, None)]
        return [
            (jnp.clip(at.z - dist, 0, 3), at.z - dist >= 0),
            (jnp.clip(at.z + dist, 0, 3), at.z + dist <= 3),
        ]

    def plane(dist):
        for src, ok in sources(dist):
            for part in range(2):
                from_x = at.shard(src, at.y, 1 - at.x)
                from_y = at.shard(src, 1 - at.y, at.x)
                wait(from_x, part, xs_sem.at[src, part], xr_sem.at[src, part], at.xn, ok)
                if part == 0:
                    send(from_x, 0, ys_sem.at[src, 2], yr_sem.at[src, 2], at.yn, ok)
                share(from_x, part, ok)
                wait(from_y, part, ys_sem.at[src, part], yr_sem.at[src, part], at.yn, ok)
                if part == 1:
                    send(from_y, 1, xs_sem.at[src, 2], xr_sem.at[src, 2], at.xn, ok)
                share(from_y, part, ok)

    def diagonal(dist):
        for src, ok in sources(dist):
            index = at.shard(src, 1 - at.y, 1 - at.x)
            wait(index, 0, ys_sem.at[src, 2], yr_sem.at[src, 2], at.yn, ok)
            wait(index, 1, xs_sem.at[src, 2], xr_sem.at[src, 2], at.xn, ok)
            for part in range(2):
                share(index, part, ok)

    chain(1)
    plane(0)
    chain(2)
    plane(1)
    diagonal(0)
    chain(3)
    plane(2)
    diagonal(1)
    plane(3)
    diagonal(2)
    diagonal(3)
    for index in range(16):
        for part in range(2):
            piece = buf.at[1 - at.half, index, pl.ds(*halves[part])]
            pltpu.make_async_remote_copy(
                src_ref=piece,
                dst_ref=piece,
                send_sem=ss_sem.at[index, part],
                recv_sem=sr_sem.at[index, part],
                device_id=at.sib,
                device_id_type=MESH,
            ).wait_recv()
    for cond, work in sends:
        guarded(cond, work)


def gather_lines(lay, own):
    if lay.dp_count != 16:
        gathered = lax.all_gather(own, ("mp", "dp"), axis=0, tiled=True)
        return gathered.reshape(MP, lay.dp_count, lay.length, LANES)
    return pl.pallas_call(
        partial(gather_kernel, lay),
        out_shape=jax.ShapeDtypeStruct((MP, 16, lay.length, LANES), jnp.bfloat16),
        in_specs=[pl.BlockSpec(memory_space=pl.ANY)],
        out_specs=pl.BlockSpec(memory_space=pltpu.VMEM),
        scratch_shapes=[
            DMA((2, 4, 2)),
            DMA((2, 4, 2)),
            DMA((4, 3)),
            DMA((4, 3)),
            DMA((4, 3)),
            DMA((4, 3)),
            DMA((16, 2)),
            DMA((16, 2)),
            DMA,
        ],
        compiler_params=pltpu.CompilerParams(
            collective_id=0, has_side_effects=True, vmem_limit_bytes=VMEM_LIMIT
        ),
        name="gather_lines",
    )(own)


def scatter_kernel(
    lay,
    part_ref,
    out_ref,
    part,
    from_sib,
    from_x,
    from_y,
    diag_x,
    diag_y,
    from_z,
    acc_z,
    load_sem,
    ss_sem,
    sr_sem,
    xs_sem,
    xr_sem,
    ys_sem,
    yr_sem,
    zs_sem,
    zr_sem,
):
    at = Place()
    halves = ((0, lay.cut), (lay.cut, lay.length - lay.cut))
    my_part = part.at[at.half]

    def load(index):
        return [
            pltpu.make_async_copy(
                part_ref.at[half, index], part.at[half, index], load_sem.at[half, index]
            )
            for half in (0, 1)
        ]

    columns = (
        (1 - at.y, 1 - at.x),
        (at.y, 1 - at.x),
        (1 - at.y, at.x),
        (at.y, at.x),
    )
    order_z = (3, 0, 2, 1)
    order = [(z, col) for col in columns for z in order_z]
    for z, (y, x) in order:
        for copy in load(at.shard(z, y, x)):
            copy.start()
    at.barrier()
    sends = []

    def remote(src, dst, send_sem, recv_sem, dev):
        return pltpu.make_async_remote_copy(
            src_ref=src,
            dst_ref=dst,
            send_sem=send_sem,
            recv_sem=recv_sem,
            device_id=dev,
            device_id_type=MESH,
        )

    def send(copy, cond=None):
        guarded(cond, lambda: copy().start())
        sends.append((cond, lambda: copy().wait_send()))

    for z, (y, x) in order:
        index = at.shard(z, y, x)
        for copy in load(index):
            copy.wait()
        send(
            lambda index=index: remote(
                part.at[1 - at.half, index],
                from_sib.at[index],
                ss_sem.at[index],
                sr_sem.at[index],
                at.sib,
            )
        )

    def wait_sib(index):
        remote(
            my_part.at[index], from_sib.at[index], ss_sem.at[index], sr_sem.at[index], at.sib
        ).wait_recv()

    def wide(ref, span):
        return ref[pl.ds(*span), :].astype(jnp.float32)

    step_rows = 16 * math.gcd(lay.cut // 16, (lay.length - lay.cut) // 16)

    def add_into(dst, terms, span):
        def body(step, carry):
            rows = (pl.multiple_of(span[0] + step * step_rows, 16), step_rows)
            total = wide(terms[0], rows)
            for term in terms[1:]:
                total = total + wide(term, rows)
            dst[pl.ds(*rows), :] = total.astype(dst.dtype)
            return carry

        lax.fori_loop(0, span[1] // step_rows, body, 0)

    whole = (0, lay.length)
    for z in order_z:
        index = at.shard(z, 1 - at.y, 1 - at.x)
        wait_sib(index)
        mine = my_part.at[index]
        add_into(mine, [mine, from_sib.at[index]], whole)
        send(
            lambda z=z, mine=mine: remote(
                mine.at[pl.ds(*halves[0])], diag_y.at[z], ys_sem.at[z, 1], yr_sem.at[z, 1], at.yn
            )
        )
        send(
            lambda z=z, mine=mine: remote(
                mine.at[pl.ds(*halves[1])], diag_x.at[z], xs_sem.at[z, 1], xr_sem.at[z, 1], at.xn
            )
        )
    for z in order_z:
        index = at.shard(z, at.y, 1 - at.x)
        wait_sib(index)
        mine = my_part.at[index]
        remote(
            mine.at[pl.ds(*halves[0])], diag_y.at[z], ys_sem.at[z, 1], yr_sem.at[z, 1], at.yn
        ).wait_recv()
        add_into(mine, [mine, from_sib.at[index], diag_y.at[z]], halves[0])
        add_into(mine, [mine, from_sib.at[index]], halves[1])
        send(
            lambda z=z, mine=mine: remote(
                mine, from_x.at[z], xs_sem.at[z, 0], xr_sem.at[z, 0], at.xn
            )
        )
        index = at.shard(z, 1 - at.y, at.x)
        wait_sib(index)
        mine = my_part.at[index]
        remote(
            mine.at[pl.ds(*halves[1])], diag_x.at[z], xs_sem.at[z, 1], xr_sem.at[z, 1], at.xn
        ).wait_recv()
        add_into(mine, [mine, from_sib.at[index]], halves[0])
        shifted = diag_x.at[z]

        def body(step, carry, mine=mine, index=index, shifted=shifted):
            rows = pl.ds(pl.multiple_of(halves[1][0] + step * step_rows, 16), step_rows)
            base = pl.ds(pl.multiple_of(step * step_rows, 16), step_rows)
            total = (
                mine[rows, :].astype(jnp.float32)
                + from_sib[index, rows, :].astype(jnp.float32)
                + shifted[base, :].astype(jnp.float32)
            )
            mine[rows, :] = total.astype(jnp.bfloat16)
            return carry

        lax.fori_loop(0, halves[1][1] // step_rows, body, 0)
        send(
            lambda z=z, mine=mine: remote(
                mine, from_y.at[z], ys_sem.at[z, 0], yr_sem.at[z, 0], at.yn
            )
        )

    for z in order_z:
        index = at.shard(z, at.y, at.x)
        wait_sib(index)
        mine = my_part.at[index]
        remote(mine, from_x.at[z], xs_sem.at[z, 0], xr_sem.at[z, 0], at.xn).wait_recv()
        remote(mine, from_y.at[z], ys_sem.at[z, 0], yr_sem.at[z, 0], at.yn).wait_recv()
        base = [mine, from_sib.at[index], from_x.at[z], from_y.at[z]]

        for down in range(2):
            dev = at.down if down else at.up
            passes = (at.z > z) if down else (at.z < z)
            gets = (at.z < 3) if down else (at.z > 0)

            def arrive(z=z, mine=mine, down=down, dev=dev):
                remote(
                    mine, from_z.at[down, z], zs_sem.at[down, z], zr_sem.at[down, z], dev
                ).wait_recv()

            @pl.when(passes & gets)
            def _():
                arrive()
                add_into(acc_z.at[down, z], base + [from_z.at[down, z]], whole)

            @pl.when(passes & jnp.logical_not(gets))
            def _():
                add_into(acc_z.at[down, z], base, whole)

            send(
                lambda z=z, down=down, dev=dev: remote(
                    acc_z.at[down, z],
                    from_z.at[down, z],
                    zs_sem.at[down, z],
                    zr_sem.at[down, z],
                    dev,
                ),
                passes,
            )

    index = at.dp
    mine = my_part.at[index]
    base = [mine, from_sib.at[index], from_x.at[at.z], from_y.at[at.z]]
    add_into(out_ref, base, whole)
    for down in range(2):

        @pl.when((at.z < 3) if down else (at.z > 0))
        def _(down=down):
            arrived = from_z.at[down, at.z]
            dev = at.down if down else at.up
            remote(
                mine, arrived, zs_sem.at[down, at.z], zr_sem.at[down, at.z], dev
            ).wait_recv()
            add_into(out_ref, [out_ref, arrived], whole)

    for cond, work in sends:
        guarded(cond, work)


def scatter_lines(lay, packed):
    if lay.dp_count != 16:
        flat = packed.reshape(MP * lay.dp_count * lay.length, LANES)
        return lax.psum_scatter(
            flat, ("mp", "dp"), scatter_dimension=0, tiled=True
        ).astype(jnp.float32)
    size = (lay.length, LANES)
    low = jnp.bfloat16
    return pl.pallas_call(
        partial(scatter_kernel, lay),
        out_shape=jax.ShapeDtypeStruct(size, jnp.float32),
        in_specs=[pl.BlockSpec(memory_space=pl.ANY)],
        out_specs=pl.BlockSpec(memory_space=pltpu.VMEM),
        scratch_shapes=[
            pltpu.VMEM((MP, 16) + size, low),
            pltpu.VMEM((16,) + size, low),
            pltpu.VMEM((4,) + size, low),
            pltpu.VMEM((4,) + size, low),
            pltpu.VMEM((4, lay.length - lay.cut, LANES), low),
            pltpu.VMEM((4, lay.cut, LANES), low),
            pltpu.VMEM((2, 4) + size, low),
            pltpu.VMEM((2, 4) + size, low),
            DMA((MP, 16)),
            DMA((16,)),
            DMA((16,)),
            DMA((4, 2)),
            DMA((4, 2)),
            DMA((4, 2)),
            DMA((4, 2)),
            DMA((2, 4)),
            DMA((2, 4)),
        ],
        compiler_params=pltpu.CompilerParams(
            collective_id=1, has_side_effects=True, vmem_limit_bytes=VMEM_LIMIT
        ),
        name="scatter_lines",
    )(packed)


SCORE_SCALE = HEAD_DIM ** (-0.5)
LAST = (((1,), (1,)), ((), ()))
FIRST = (((0,), (0,)), ((), ()))


def attend_kernel(heads, qkv_ref, seg_col_ref, seg_row_ref, out_ref, log_ref):
    width = heads * HEAD_DIM
    same = seg_col_ref[...] == seg_row_ref[0]
    logs = []
    for head in range(heads):
        low = head * HEAD_DIM
        queries = qkv_ref[:, low : low + HEAD_DIM]
        keys = qkv_ref[:, width + low : width + low + HEAD_DIM]
        values = qkv_ref[:, 2 * width + low : 2 * width + low + HEAD_DIM]
        scores = lax.dot_general(queries, keys, LAST, preferred_element_type=jnp.float32)
        scores = jnp.where(same, scores * SCORE_SCALE, -1e30)
        row_max = jnp.max(scores, -1, keepdims=True)
        exponent = jnp.exp(scores - row_max)
        row_total = jnp.sum(exponent, -1, keepdims=True)
        probs = (exponent * (1.0 / row_total)).astype(jnp.bfloat16)
        mixed = jnp.dot(probs, values, preferred_element_type=jnp.float32)
        out_ref[:, low : low + HEAD_DIM] = mixed.astype(jnp.bfloat16)
        logs.append(row_max + jnp.log(row_total))
    log_ref[0] = jnp.concatenate(logs + [logs[0]] * (8 - heads), 1)


def attend(qkv, seg_col, seg_row, head_cols):
    heads = head_cols // HEAD_DIM
    rows = qkv.shape[0] // ROW
    return pl.pallas_call(
        partial(attend_kernel, heads),
        grid=(rows, MP),
        in_specs=[
            pl.BlockSpec((ROW, 3 * head_cols), lambda r, m: (r, m)),
            pl.BlockSpec((ROW, 1), lambda r, m: (r, 0)),
            pl.BlockSpec((1, 1, ROW), lambda r, m: (r, 0, 0)),
        ],
        out_specs=[
            pl.BlockSpec((ROW, head_cols), lambda r, m: (r, m)),
            pl.BlockSpec((1, ROW, 8), lambda r, m: (m, r, 0)),
        ],
        out_shape=[
            jax.ShapeDtypeStruct((rows * ROW, MP * head_cols), jnp.bfloat16),
            jax.ShapeDtypeStruct((MP, rows * ROW, 8), jnp.float32),
        ],
        compiler_params=pltpu.CompilerParams(vmem_limit_bytes=VMEM_LIMIT),
        name="attend",
    )(qkv, seg_col, seg_row)


def attend_back_kernel(heads, qkv_ref, grad_ref, log_ref, seg_col_ref, seg_row_ref, out_ref):
    width = heads * HEAD_DIM
    same = seg_col_ref[...] == seg_row_ref[0]
    for head in range(heads):
        low = head * HEAD_DIM
        queries = qkv_ref[:, low : low + HEAD_DIM]
        keys = qkv_ref[:, width + low : width + low + HEAD_DIM]
        values = qkv_ref[:, 2 * width + low : 2 * width + low + HEAD_DIM]
        mixed_grad = grad_ref[:, low : low + HEAD_DIM]
        scores = lax.dot_general(queries, keys, LAST, preferred_element_type=jnp.float32)
        scores = jnp.where(same, scores * SCORE_SCALE, -1e30)
        probs = jnp.exp(scores - log_ref[0, :, head : head + 1])
        prob_grad = lax.dot_general(
            mixed_grad, values, LAST, preferred_element_type=jnp.float32
        )
        row_inner = jnp.sum(prob_grad * probs, -1, keepdims=True)
        score_grad = (probs * (prob_grad - row_inner)).astype(jnp.bfloat16)
        value_grad = lax.dot_general(
            probs.astype(jnp.bfloat16), mixed_grad, FIRST, preferred_element_type=jnp.float32
        )
        query_grad = (
            jnp.dot(score_grad, keys, preferred_element_type=jnp.float32) * SCORE_SCALE
        )
        key_grad = (
            lax.dot_general(score_grad, queries, FIRST, preferred_element_type=jnp.float32)
            * SCORE_SCALE
        )
        for place, value in enumerate((query_grad, key_grad, value_grad)):
            start = place * width + low
            out_ref[:, start : start + HEAD_DIM] = value.astype(jnp.bfloat16)


def attend_back(qkv, mixed_grad, logs, seg_col, seg_row, head_cols):
    heads = head_cols // HEAD_DIM
    rows = qkv.shape[0] // ROW
    return pl.pallas_call(
        partial(attend_back_kernel, heads),
        grid=(rows, MP),
        in_specs=[
            pl.BlockSpec((ROW, 3 * head_cols), lambda r, m: (r, m)),
            pl.BlockSpec((ROW, head_cols), lambda r, m: (r, m)),
            pl.BlockSpec((1, ROW, 8), lambda r, m: (m, r, 0)),
            pl.BlockSpec((ROW, 1), lambda r, m: (r, 0)),
            pl.BlockSpec((1, 1, ROW), lambda r, m: (r, 0, 0)),
        ],
        out_specs=pl.BlockSpec((ROW, 3 * head_cols), lambda r, m: (r, m)),
        out_shape=jax.ShapeDtypeStruct(qkv.shape, jnp.bfloat16),
        compiler_params=pltpu.CompilerParams(vmem_limit_bytes=VMEM_LIMIT),
        name="attend_back",
    )(qkv, mixed_grad, logs, seg_col, seg_row)


def back_norm(values_in, scale_vec, grad):
    center = jnp.mean(values_in, -1, keepdims=True)
    centered = values_in - center
    inverse = lax.rsqrt(jnp.mean(centered * centered, -1, keepdims=True) + NORM_EPS)
    unit = centered * inverse
    scaled = grad * scale_vec
    out = inverse * (
        scaled
        - jnp.mean(scaled, -1, keepdims=True)
        - unit * jnp.mean(scaled * unit, -1, keepdims=True)
    )
    return out, jnp.sum(grad * unit, 0), jnp.sum(grad, 0)


def per_device(
    tokens,
    segments,
    sentence_dest,
    pair_source,
    labels,
    params,
    first,
    second,
    shared,
    shared_first,
    shared_second,
):
    features = tokens.shape[1]
    dp_count = lax.axis_size("dp")
    dp_index = lax.axis_index("dp")
    mp_index = lax.axis_index("mp")
    shard = params.shape[1]
    lay = Layout(features, shard, dp_count)
    head_cols = lay.head_cols
    sent_slots = ROWS_DEV * SEG
    slot_capacity = max(2, sent_slots // dp_count)
    params_total = MP * shard * dp_count + 6 * features
    core_rows = ROWS_CORE * ROW

    phase = (dp_index * shard) % LANES
    own = lax.dynamic_update_slice(
        jnp.zeros((lay.length * LANES,), jnp.bfloat16),
        params.astype(jnp.bfloat16).reshape(-1),
        (phase,),
    ).reshape(lay.length, LANES)
    w_qkv, w_attn, w_in, w_out, biases = unpack_weights(lay, gather_lines(lay, own))
    head_lines = head_cols // LANES
    b_query = biases[:, :head_lines].reshape(MP, head_cols)
    b_value = biases[:, head_lines : 2 * head_lines].reshape(MP, head_cols)
    b_in = biases[:, 2 * head_lines : lay.bias_lines].reshape(MP * lay.ffn_cols)
    b_qkv = jnp.concatenate([b_query, jnp.zeros_like(b_query), b_value], 1).reshape(-1)

    tokens_core = lax.dynamic_slice_in_dim(tokens, mp_index * core_rows, core_rows, 0)
    segments_core = lax.dynamic_slice_in_dim(segments, mp_index * core_rows, core_rows, 0)
    seg_col = segments_core.reshape(core_rows, 1)
    seg_row = segments_core.reshape(ROWS_CORE, 1, ROW)

    qkv = (jnp.dot(tokens_core, w_qkv, preferred_element_type=jnp.float32) + b_qkv).astype(
        jnp.bfloat16
    )
    mixed, logs = attend(qkv, seg_col, seg_row, head_cols)
    attn_out = jnp.dot(mixed, w_attn, preferred_element_type=jnp.float32) + shared[4]
    resid_one = tokens_core.astype(jnp.float32) + attn_out
    hidden = normalize(resid_one, shared[0], shared[1])
    hidden_low = hidden.astype(jnp.bfloat16)
    up_proj = jnp.dot(hidden_low, w_in, preferred_element_type=jnp.float32) + b_in
    cdf = 0.5 * (1.0 + lax.erf(up_proj * (0.5**0.5)))
    activated = (up_proj * cdf).astype(jnp.bfloat16)
    slope = (
        cdf + up_proj * jnp.exp(-0.5 * up_proj * up_proj) * ((2.0 * math.pi) ** -0.5)
    ).astype(jnp.bfloat16)
    ffn_out = jnp.dot(activated, w_out, preferred_element_type=jnp.float32) + shared[5]
    resid_two = hidden + ffn_out
    encoded_core = normalize(resid_two, shared[2], shared[3])
    encoded = lax.all_gather(encoded_core.astype(jnp.bfloat16), "mp", axis=0, tiled=True)

    slot_ids = jnp.arange(SEG, dtype=jnp.int32)
    onehot = (seg_row == slot_ids[None, :, None]).astype(jnp.float32)
    weight = onehot / jnp.sum(onehot, 2, keepdims=True)
    pooled_core = jnp.einsum(
        "kvf,kfo->kvo",
        weight,
        encoded_core.reshape(ROWS_CORE, ROW, features),
        precision=TOP_PRECISION,
    ).astype(jnp.bfloat16)
    pooled_flat = lax.all_gather(
        pooled_core.reshape(ROWS_CORE * SEG, features), "mp", axis=0, tiled=True
    )
    code_ids = jnp.arange(dp_count * slot_capacity, dtype=jnp.int32)
    send_code = sentence_dest[:, 0] * slot_capacity + sentence_dest[:, 1]
    send_map = (code_ids[:, None] == send_code[None, :]).astype(jnp.bfloat16)
    outgoing = jnp.dot(send_map, pooled_flat, preferred_element_type=jnp.float32).astype(
        jnp.bfloat16
    )
    outgoing = outgoing.reshape(dp_count, slot_capacity, features)
    incoming = lax.all_to_all(outgoing, "dp", split_axis=0, concat_axis=0, tiled=True).reshape(
        dp_count * slot_capacity, features
    )
    take_code = pair_source[:, 0] * slot_capacity + pair_source[:, 1]
    take_map = (take_code[:, None] == code_ids[None, :]).astype(jnp.bfloat16)
    pair_items = jnp.dot(take_map, incoming, preferred_element_type=jnp.float32)
    item_grad = jax.grad(pair_loss)(pair_items, labels).astype(jnp.bfloat16)
    returning = jnp.dot(take_map.T, item_grad, preferred_element_type=jnp.float32).astype(
        jnp.bfloat16
    )
    returning = returning.reshape(dp_count, slot_capacity, features)
    arrived = lax.all_to_all(returning, "dp", split_axis=0, concat_axis=0, tiled=True).reshape(
        dp_count * slot_capacity, features
    )
    core_map = lax.dynamic_slice_in_dim(send_map, mp_index * ROWS_CORE * SEG, ROWS_CORE * SEG, 1)
    pooled_grad = jnp.dot(core_map.T, arrived, preferred_element_type=jnp.float32)

    encoded_grad = jnp.einsum(
        "jix,jip->jxp",
        weight,
        pooled_grad.reshape(ROWS_CORE, SEG, features),
        precision=TOP_PRECISION,
    ).reshape(core_rows, features)
    resid_two_grad, scale_two, shift_two = back_norm(resid_two, shared[2], encoded_grad)
    ffn_grad = resid_two_grad.astype(jnp.bfloat16)
    act_grad = lax.dot_general(ffn_grad, w_out, LAST, preferred_element_type=jnp.float32)
    up_grad = (act_grad * slope.astype(jnp.float32)).astype(jnp.bfloat16)
    w_out_grad = lax.dot_general(activated, ffn_grad, FIRST, preferred_element_type=jnp.float32)
    w_in_grad = lax.dot_general(hidden_low, up_grad, FIRST, preferred_element_type=jnp.float32)
    hidden_term = lax.dot_general(up_grad, w_in, LAST, preferred_element_type=jnp.float32)
    hidden_grad = resid_two_grad + hidden_term
    resid_one_grad, scale_one, shift_one = back_norm(resid_one, shared[0], hidden_grad)
    attn_grad = resid_one_grad.astype(jnp.bfloat16)
    w_attn_grad = lax.dot_general(mixed, attn_grad, FIRST, preferred_element_type=jnp.float32)
    mixed_grad = lax.dot_general(
        attn_grad, w_attn, LAST, preferred_element_type=jnp.float32
    ).astype(jnp.bfloat16)
    qkv_grad = attend_back(qkv, mixed_grad, logs, seg_col, seg_row, head_cols)
    w_qkv_grad = lax.dot_general(
        tokens_core, qkv_grad, FIRST, preferred_element_type=jnp.float32
    )
    input_term = lax.dot_general(qkv_grad, w_qkv, LAST, preferred_element_type=jnp.float32)
    input_core = resid_one_grad + input_term
    input_grad = lax.all_gather(input_core, "mp", axis=0, tiled=True)

    qkv_sums = jnp.sum(qkv_grad.astype(jnp.float32), 0).reshape(MP, 3, head_lines, LANES)
    in_sums = jnp.sum(up_grad.astype(jnp.float32), 0).reshape(MP, -1, LANES)
    bias_grad = jnp.concatenate([qkv_sums[:, 0], qkv_sums[:, 2], in_sums], 1)
    bias_grad = jnp.pad(bias_grad, ((0, 0), (0, lay.bias_rows - lay.bias_lines), (0, 0)))
    packed = pack_gradients(
        lay,
        [g.astype(jnp.bfloat16) for g in (w_qkv_grad, w_attn_grad, w_in_grad, w_out_grad)],
        bias_grad,
    )
    grad_lines = scatter_lines(lay, packed)
    flat_grad = lax.dynamic_slice(grad_lines.reshape(-1), (phase,), (shard,))[None]
    flat_grad = flat_grad / LOSS_SCALE
    shared_step = jnp.stack(
        [
            scale_one,
            shift_one,
            scale_two,
            shift_two,
            jnp.sum(attn_grad.astype(jnp.float32), 0),
            jnp.sum(ffn_grad.astype(jnp.float32), 0),
        ]
    )
    shared_grad = lax.psum(shared_step, ("dp", "mp")) / LOSS_SCALE
    local_squares = jnp.sum(flat_grad * flat_grad)
    total_squares = lax.psum(local_squares, ("dp", "mp"))
    norm_value = jnp.sqrt(total_squares + jnp.sum(shared_grad * shared_grad))
    factor = jnp.minimum(1.0, CLIP_NORM / norm_value)
    step_count = STEP_COUNT
    params_new, first_new, second_new = adamw(
        params, first, second, flat_grad, factor, step_count, LEARN_RATE
    )
    shared_new, shared_first_new, shared_second_new = adamw(
        shared, shared_first, shared_second, shared_grad, factor, step_count, SHARED_RATE
    )
    grad_unit = math.sqrt(params_total) / CLIP_NORM
    params_grad = flat_grad * factor * grad_unit
    shared_grad_out = shared_grad * factor * grad_unit
    return (
        encoded,
        input_grad,
        norm_value.reshape(1),
        params_new,
        first_new,
        second_new,
        params_new.astype(jnp.bfloat16),
        shared_new,
        shared_first_new,
        shared_second_new,
        params_grad,
        shared_grad_out,
    )


def solution(mesh):
    in_specs = (
        P("dp", None),
        P("dp"),
        P("dp", None),
        P("dp", None),
        P("dp"),
        P("mp", "dp"),
        P("mp", "dp"),
        P("mp", "dp"),
        P(),
        P(),
        P(),
    )
    out_specs = (
        P("dp", None),
        P("dp", None),
        P(),
        P("mp", "dp"),
        P("mp", "dp"),
        P("mp", "dp"),
        P("mp", "dp"),
        P(),
        P(),
        P(),
        P("mp", "dp"),
        P(),
    )
    return jax.shard_map(
        per_device, mesh=mesh, in_specs=in_specs, out_specs=out_specs, check_vma=False
    )
```

```python
from functools import partial
import math

import jax
import jax.numpy as jnp
from jax import lax
from jax.experimental import pallas as pl
from jax.experimental.pallas import tpu as pltpu
from jax.sharding import PartitionSpec as P

HEAD_DIM = 64
FF = 3072
ROW = 512
SEG = 32
RPM = 2
MB = 2
MP = 2
LANES = 128
ROWS_DEV = MB * RPM
ROWS_CORE = ROWS_DEV // MP


LOSS_SCALE = 1024.0
CLIP_NORM = 0.5
LEARN_RATE = 0.1
SHARED_RATE = 0.5
BETA_ONE = 0.9
BETA_TWO = 0.999
ADAM_EPS = 1e-08
DECAY = 0.01
NORM_EPS = 1e-12
STEP_COUNT = 10.0
TOP_PRECISION = lax.Precision.HIGHEST
MESH = pl.DeviceIdType.MESH
DMA = pltpu.SemaphoreType.DMA
VMEM_LIMIT = 60 << 20


def normalize(values_in, scale_vec, shift_vec):
    center = jnp.mean(values_in, -1, keepdims=True)
    centered = values_in - center
    spread = jnp.mean(centered * centered, -1, keepdims=True)
    return centered * lax.rsqrt(spread + NORM_EPS) * scale_vec + shift_vec


def pair_loss(pair_items, labels):
    first_vec = pair_items[..., 0::2, :]
    second_vec = pair_items[..., 1::2, :]
    inner_prod = jnp.sum(first_vec * second_vec, -1)
    cosine = (
        inner_prod
        * lax.rsqrt(jnp.sum(first_vec * first_vec, -1) + 1e-06)
        * lax.rsqrt(jnp.sum(second_vec * second_vec, -1) + 1e-06)
    )
    error_term = cosine - labels.astype(jnp.float32) / 5.0
    return LOSS_SCALE * jnp.sum(error_term * error_term)


def adamw(weight, moment_one, moment_two, gradient, factor, step_count, rate):
    clipped = gradient * factor
    first_new = BETA_ONE * moment_one + (1.0 - BETA_ONE) * clipped
    second_new = BETA_TWO * moment_two + (1.0 - BETA_TWO) * clipped * clipped
    first_hat = first_new / (1.0 - BETA_ONE**step_count)
    second_hat = second_new / (1.0 - BETA_TWO**step_count)
    weight_new = weight - rate * (first_hat / (jnp.sqrt(second_hat) + ADAM_EPS) + DECAY * weight)
    return (weight_new, first_new, second_new)


class Layout:
    def __init__(self, features, shard, dp_count):
        self.features = features
        self.shard = shard
        self.dp_count = dp_count
        self.head_cols = features // MP
        self.ffn_cols = FF // MP
        self.total = shard * dp_count
        self.lines = self.total // LANES
        assert self.lines * LANES == self.total
        self.starts = [index * shard // LANES for index in range(dp_count)]
        need = max(
            ((index + 1) * shard - 1) // LANES - index * shard // LANES + 1
            for index in range(dp_count)
        )
        self.need = need
        self.length = -(-(need + 2) // 32) * 32
        self.cut = self.length // 2
        self.step = max(
            rows for rows in range(16, 257, 16) if self.cut % rows == 0
        )
        self.mats = []
        offset = 0
        for height, extent in (
            (features, 3 * self.head_cols),
            (self.head_cols, features),
            (features, self.ffn_cols),
            (self.ffn_cols, features),
        ):
            assert extent % LANES == 0 and height % LANES == 0
            self.mats.append((offset, height, extent // LANES))
            offset += height * (extent // LANES)
        self.bias_start = offset
        self.bias_lines = self.lines - offset
        self.bias_rows = -(-self.bias_lines // 8) * 8
        self.flat_rows = -(-(self.starts[-1] + self.length) // 8) * 8


def weight_specs(lay):
    specs = [
        pl.BlockSpec((lay.features, 3 * lay.head_cols), lambda half: (0, half)),
        pl.BlockSpec((lay.head_cols, lay.features), lambda half: (half, 0)),
        pl.BlockSpec((lay.features, lay.ffn_cols), lambda half: (0, half)),
        pl.BlockSpec((lay.ffn_cols, lay.features), lambda half: (half, 0)),
        pl.BlockSpec((1, lay.bias_rows, LANES), lambda half: (half, 0, 0)),
    ]
    shapes = [
        (lay.features, MP * 3 * lay.head_cols),
        (MP * lay.head_cols, lay.features),
        (lay.features, MP * lay.ffn_cols),
        (MP * lay.ffn_cols, lay.features),
    ]
    return specs, shapes


def unpack_kernel(lay, lines_ref, qkv_ref, attn_ref, in_ref, out_ref, bias_ref, flat):
    for index in range(lay.dp_count):
        start = lay.starts[index]
        if index > 0:
            kept = flat[start : start + 1, :]
        flat[start : start + lay.length, :] = lines_ref[0, index].astype(jnp.float32)
        if index > 0:
            flat[start : start + 1, :] += kept
    for (offset, height, cols), ref in zip(lay.mats, (qkv_ref, attn_ref, in_ref, out_ref)):

        def body(step, carry, offset=offset, cols=cols, ref=ref):
            row = pl.multiple_of(step * LANES, LANES)
            for col in range(cols):
                block = flat[pl.ds(offset + row * cols + col, LANES, stride=cols), :]
                ref[pl.ds(row, LANES), col * LANES : (col + 1) * LANES] = block.astype(
                    jnp.bfloat16
                )
            return carry

        lax.fori_loop(0, height // LANES, body, 0)
    bias_ref[0] = flat[lay.bias_start : lay.bias_start + lay.bias_rows, :]


def unpack_weights(lay, gathered):
    specs, shapes = weight_specs(lay)
    return pl.pallas_call(
        partial(unpack_kernel, lay),
        grid=(MP,),
        in_specs=[
            pl.BlockSpec((1, lay.dp_count, lay.length, LANES), lambda half: (half, 0, 0, 0))
        ],
        out_specs=specs,
        out_shape=[jax.ShapeDtypeStruct(s, jnp.bfloat16) for s in shapes]
        + [jax.ShapeDtypeStruct((MP, lay.bias_rows, LANES), jnp.float32)],
        scratch_shapes=[pltpu.VMEM((lay.flat_rows, LANES), jnp.float32)],
        compiler_params=pltpu.CompilerParams(vmem_limit_bytes=VMEM_LIMIT),
        name="unpack_weights",
    )(gathered)


def pack_kernel(lay, qkv_ref, attn_ref, in_ref, out_ref, bias_ref, lines_ref, flat):
    for (offset, height, cols), ref in zip(lay.mats, (qkv_ref, attn_ref, in_ref, out_ref)):

        def body(step, carry, offset=offset, cols=cols, ref=ref):
            row = pl.multiple_of(step * LANES, LANES)
            for col in range(cols):
                block = ref[pl.ds(row, LANES), col * LANES : (col + 1) * LANES]
                flat[pl.ds(offset + row * cols + col, LANES, stride=cols), :] = block.astype(
                    jnp.float32
                )
            return carry

        lax.fori_loop(0, height // LANES, body, 0)
    tail = lay.flat_rows - lay.lines
    if tail:
        flat[lay.lines :, :] = jnp.zeros((tail, LANES), jnp.float32)
    flat[lay.bias_start : lay.lines, :] = bias_ref[0, : lay.bias_lines]
    for index in range(lay.dp_count):
        start = lay.starts[index]
        lines_ref[0, index] = flat[start : start + lay.length, :].astype(jnp.bfloat16)


def pack_gradients(lay, grads, bias_grad):
    specs, _ = weight_specs(lay)
    return pl.pallas_call(
        partial(pack_kernel, lay),
        grid=(MP,),
        in_specs=specs,
        out_specs=pl.BlockSpec(
            (1, lay.dp_count, lay.length, LANES), lambda half: (half, 0, 0, 0)
        ),
        out_shape=jax.ShapeDtypeStruct((MP, lay.dp_count, lay.length, LANES), jnp.bfloat16),
        scratch_shapes=[pltpu.VMEM((lay.flat_rows, LANES), jnp.float32)],
        compiler_params=pltpu.CompilerParams(vmem_limit_bytes=VMEM_LIMIT),
        name="pack_gradients",
    )(*grads, bias_grad)


class Place:
    def __init__(self):
        self.dp = lax.axis_index("dp")
        self.half = lax.axis_index("mp")
        self.z = self.dp // 4
        self.y = (self.dp // 2) % 2
        self.x = self.dp % 2
        self.has_up = self.z < 3
        self.has_down = self.z > 0
        self.up = (jnp.minimum(self.dp + 4, 12 + self.dp % 4), self.half)
        self.down = (jnp.maximum(self.dp - 4, self.dp % 4), self.half)
        self.xn = (self.shard(self.z, self.y, 1 - self.x), self.half)
        self.yn = (self.shard(self.z, 1 - self.y, self.x), self.half)
        self.sib = (self.dp, 1 - self.half)

    def shard(self, z, y, x):
        return z * 4 + y * 2 + x

    def barrier(self):
        bar = pltpu.get_barrier_semaphore()
        for dev in (self.xn, self.yn, self.sib):
            pl.semaphore_signal(bar, inc=1, device_id=dev, device_id_type=MESH)

        @pl.when(self.has_up)
        def _():
            pl.semaphore_signal(bar, inc=1, device_id=self.up, device_id_type=MESH)

        @pl.when(self.has_down)
        def _():
            pl.semaphore_signal(bar, inc=1, device_id=self.down, device_id_type=MESH)

        pl.semaphore_wait(
            bar, 3 + jnp.where(self.has_up, 1, 0) + jnp.where(self.has_down, 1, 0)
        )


def guarded(cond, work):
    if cond is None:
        work()
    else:
        pl.when(cond)(work)


def lane_ids(rows):
    return lax.broadcasted_iota(jnp.int32, (rows, LANES), 1)


def shift_into_lines(lay, own_ref, rolled, put):
    phase = lax.rem(lax.axis_index("dp") * lay.shard, LANES)
    rows = lay.length
    rolled[0:8, :] = jnp.zeros((8, LANES), jnp.float32)
    rolled[8 : 8 + rows, :] = pltpu.roll(own_ref[...], phase, 1)
    late = rolled[7 : 7 + rows, :]
    put(jnp.where(lane_ids(rows) < phase, late, rolled[8 : 8 + rows, :]))


def gather_kernel(
    lay, own_ref, buf, rolled, zs_sem, zr_sem, xs_sem, xr_sem, ys_sem, yr_sem, ss_sem, sr_sem
):
    at = Place()
    halves = ((0, lay.cut), (lay.cut, lay.length - lay.cut))

    def put(lines):
        buf[at.half, at.dp] = lines.astype(jnp.bfloat16)

    shift_into_lines(lay, own_ref, rolled, put)
    at.barrier()
    sends = []

    def remote(index, part, send_sem, recv_sem, dev):
        piece = buf.at[at.half, index, pl.ds(*halves[part])]
        return pltpu.make_async_remote_copy(
            src_ref=piece,
            dst_ref=piece,
            send_sem=send_sem,
            recv_sem=recv_sem,
            device_id=dev,
            device_id_type=MESH,
        )

    def send(index, part, send_sem, recv_sem, dev, cond=None):
        guarded(cond, lambda: remote(index, part, send_sem, recv_sem, dev).start())
        sends.append((cond, lambda: remote(index, part, send_sem, recv_sem, dev).wait_send()))

    def wait(index, part, send_sem, recv_sem, dev, cond=None):
        guarded(cond, lambda: remote(index, part, send_sem, recv_sem, dev).wait_recv())

    def share(index, part, cond=None):
        send(index, part, ss_sem.at[index, part], sr_sem.at[index, part], at.sib, cond)

    for part in range(2):
        send(at.dp, part, zs_sem.at[0, 0, part], zr_sem.at[0, 1, part], at.up, at.has_up)
        send(at.dp, part, zs_sem.at[1, 0, part], zr_sem.at[1, 1, part], at.down, at.has_down)
        send(at.dp, part, xs_sem.at[at.z, part], xr_sem.at[at.z, part], at.xn)
        send(at.dp, part, ys_sem.at[at.z, part], yr_sem.at[at.z, part], at.yn)
        share(at.dp, part)

    def chain(dist):
        for part in range(2):
            for down in range(2):
                src = at.z + dist if down else at.z - dist
                ok = (src <= 3) if down else (src >= 0)
                src = jnp.clip(src, 0, 3)
                index = at.shard(src, at.y, at.x)
                dev = at.down if down else at.up
                onward = at.has_down if down else at.has_up
                wait(
                    index, part, zs_sem.at[down, 0, part], zr_sem.at[down, dist, part], dev, ok
                )
                if dist < 3:
                    send(
                        index,
                        part,
                        zs_sem.at[down, dist, part],
                        zr_sem.at[down, dist + 1, part],
                        dev,
                        ok & onward,
                    )
                send(index, part, xs_sem.at[src, part], xr_sem.at[src, part], at.xn, ok)
                send(index, part, ys_sem.at[src, part], yr_sem.at[src, part], at.yn, ok)
                share(index, part, ok)

    def sources(dist):
        if dist == 0:
            return [(at.z, None)]
        return [
            (jnp.clip(at.z - dist, 0, 3), at.z - dist >= 0),
            (jnp.clip(at.z + dist, 0, 3), at.z + dist <= 3),
        ]

    def plane(dist):
        for src, ok in sources(dist):
            for part in range(2):
                from_x = at.shard(src, at.y, 1 - at.x)
                from_y = at.shard(src, 1 - at.y, at.x)
                wait(from_x, part, xs_sem.at[src, part], xr_sem.at[src, part], at.xn, ok)
                if part == 0:
                    send(from_x, 0, ys_sem.at[src, 2], yr_sem.at[src, 2], at.yn, ok)
                share(from_x, part, ok)
                wait(from_y, part, ys_sem.at[src, part], yr_sem.at[src, part], at.yn, ok)
                if part == 1:
                    send(from_y, 1, xs_sem.at[src, 2], xr_sem.at[src, 2], at.xn, ok)
                share(from_y, part, ok)

    def diagonal(dist):
        for src, ok in sources(dist):
            index = at.shard(src, 1 - at.y, 1 - at.x)
            wait(index, 0, ys_sem.at[src, 2], yr_sem.at[src, 2], at.yn, ok)
            wait(index, 1, xs_sem.at[src, 2], xr_sem.at[src, 2], at.xn, ok)
            for part in range(2):
                share(index, part, ok)

    chain(1)
    plane(0)
    chain(2)
    plane(1)
    diagonal(0)
    chain(3)
    plane(2)
    diagonal(1)
    plane(3)
    diagonal(2)
    diagonal(3)
    for index in range(16):
        for part in range(2):
            piece = buf.at[1 - at.half, index, pl.ds(*halves[part])]
            pltpu.make_async_remote_copy(
                src_ref=piece,
                dst_ref=piece,
                send_sem=ss_sem.at[index, part],
                recv_sem=sr_sem.at[index, part],
                device_id=at.sib,
                device_id_type=MESH,
            ).wait_recv()
    for cond, work in sends:
        guarded(cond, work)


def gather_lines(lay, own):
    if lay.dp_count != 16:
        flat = own.reshape(-1)
        phase = (lax.axis_index("dp") * lay.shard) % LANES
        own = jnp.roll(flat, phase).reshape(lay.length, LANES).astype(jnp.bfloat16)
        gathered = lax.all_gather(own, ("mp", "dp"), axis=0, tiled=True)
        return gathered.reshape(MP, lay.dp_count, lay.length, LANES)
    return pl.pallas_call(
        partial(gather_kernel, lay),
        out_shape=jax.ShapeDtypeStruct((MP, 16, lay.length, LANES), jnp.bfloat16),
        in_specs=[pl.BlockSpec(memory_space=pltpu.VMEM)],
        out_specs=pl.BlockSpec(memory_space=pltpu.VMEM),
        scratch_shapes=[
            pltpu.VMEM((lay.length + 8, LANES), jnp.float32),
            DMA((2, 4, 2)),
            DMA((2, 4, 2)),
            DMA((4, 3)),
            DMA((4, 3)),
            DMA((4, 3)),
            DMA((4, 3)),
            DMA((16, 2)),
            DMA((16, 2)),
        ],
        compiler_params=pltpu.CompilerParams(
            collective_id=0, has_side_effects=True, vmem_limit_bytes=VMEM_LIMIT
        ),
        name="gather_lines",
    )(own)


STAT_ROWS = 8


def scatter_kernel(
    lay,
    qkv_hbm,
    attn_hbm,
    in_hbm,
    out_hbm,
    bias_ref,
    tail_ref,
    grad_ref,
    norm_ref,
    shared_ref,
    staged_qkv,
    staged_attn,
    staged_in,
    staged_out,
    flat,
    part,
    from_sib,
    from_x,
    from_y,
    diag_x,
    diag_y,
    from_z,
    acc_z,
    total,
    stats,
    load_sem,
    ss_sem,
    sr_sem,
    xs_sem,
    xr_sem,
    ys_sem,
    yr_sem,
    zs_sem,
    zr_sem,
    bs_sem,
    br_sem,
):
    at = Place()
    halves = ((0, lay.cut), (lay.cut, lay.length - lay.cut))
    my_part = part.at[at.half]
    staged = (staged_qkv, staged_attn, staged_in, staged_out)

    def load(which, half):
        source = (qkv_hbm, attn_hbm, in_hbm, out_hbm)[which]
        rows, cols = staged[which].shape
        if which % 2 == 0:
            piece = source.at[:, pl.ds(pl.multiple_of(half * cols, LANES), cols)]
        else:
            piece = source.at[pl.ds(pl.multiple_of(half * rows, LANES), rows), :]
        return pltpu.make_async_copy(piece, staged[which], load_sem.at[which])

    for which in range(4):
        load(which, 1 - at.half).start()

    bar = pltpu.get_barrier_semaphore()
    me = at.dp * MP + at.half
    count = 16 * MP

    def peer(step):
        other = lax.rem(me + step, count)
        return (other // MP, lax.rem(other, MP))

    def greet(step, carry):
        pl.semaphore_signal(bar, inc=1, device_id=peer(step), device_id_type=MESH)
        return carry

    lax.fori_loop(1, count, greet, 0)
    sends = []

    def remote(src, dst, send_sem, recv_sem, dev):
        return pltpu.make_async_remote_copy(
            src_ref=src,
            dst_ref=dst,
            send_sem=send_sem,
            recv_sem=recv_sem,
            device_id=dev,
            device_id_type=MESH,
        )

    def send(copy, cond=None):
        guarded(cond, lambda: copy().start())
        sends.append((cond, lambda: copy().wait_send()))

    tail_from = lay.need // 16 * 16
    tail_rows = lax.broadcasted_iota(jnp.int32, (16, LANES), 0)
    for turn in range(2):
        half = at.half if turn else 1 - at.half
        emitted = 0
        for which, (offset, height, cols) in enumerate(lay.mats):
            ref = staged[which]
            load(which, half).wait()

            def body(step, carry, offset=offset, cols=cols, ref=ref):
                row = pl.multiple_of(step * LANES, LANES)
                for col in range(cols):
                    block = ref[pl.ds(row, LANES), col * LANES : (col + 1) * LANES]
                    flat[pl.ds(offset + row * cols + col, LANES, stride=cols), :] = block.astype(
                        jnp.float32
                    )
                return carry

            lax.fori_loop(0, height // LANES, body, 0)
            if turn == 0:
                load(which, at.half).start()
            done = offset + height * cols
            if which == 3:
                rows = lay.flat_rows - lay.lines
                if rows:
                    flat[lay.lines :, :] = jnp.zeros((rows, LANES), jnp.float32)
                flat[lay.bias_start : lay.lines, :] = bias_ref[half, : lay.bias_lines]
                done = lay.flat_rows
            while emitted < lay.dp_count and lay.starts[emitted] + lay.length <= done:
                index, start = emitted, lay.starts[emitted]
                part[half, index, :tail_from] = flat[start : start + tail_from, :].astype(
                    jnp.bfloat16
                )
                last = flat[start + tail_from : start + tail_from + 16, :]
                last = jnp.where(tail_rows < lay.need - tail_from, last, tail_ref[half, index])
                part[half, index, tail_from : tail_from + 16] = last.astype(jnp.bfloat16)
                if lay.length > tail_from + 16:
                    part[half, index, tail_from + 16 :] = jnp.zeros(
                        (lay.length - tail_from - 16, LANES), jnp.bfloat16
                    )
                if turn == 0:
                    if index == 0:
                        pl.semaphore_wait(bar, count - 1)
                    send(
                        lambda index=index: remote(
                            part.at[1 - at.half, index],
                            from_sib.at[index],
                            ss_sem.at[index],
                            sr_sem.at[index],
                            at.sib,
                        )
                    )
                emitted += 1
        assert emitted == lay.dp_count

    order_z = (3, 0, 2, 1)

    def wait_sib(index):
        remote(
            my_part.at[index], from_sib.at[index], ss_sem.at[index], sr_sem.at[index], at.sib
        ).wait_recv()

    def wide(ref, span):
        return ref[pl.ds(*span), :].astype(jnp.float32)

    step_rows = lay.step

    def add_into(dst, terms, span):
        def body(step, carry):
            rows = (pl.multiple_of(span[0] + step * step_rows, 16), step_rows)
            total = wide(terms[0], rows)
            for term in terms[1:]:
                total = total + wide(term, rows)
            dst[pl.ds(*rows), :] = total.astype(dst.dtype)
            return carry

        lax.fori_loop(0, span[1] // step_rows, body, 0)

    whole = (0, lay.length)
    for z in order_z:
        index = at.shard(z, 1 - at.y, 1 - at.x)
        wait_sib(index)
        mine = my_part.at[index]
        add_into(mine, [mine, from_sib.at[index]], whole)
        send(
            lambda z=z, mine=mine: remote(
                mine.at[pl.ds(*halves[0])], diag_y.at[z], ys_sem.at[z, 1], yr_sem.at[z, 1], at.yn
            )
        )
        send(
            lambda z=z, mine=mine: remote(
                mine.at[pl.ds(*halves[1])], diag_x.at[z], xs_sem.at[z, 1], xr_sem.at[z, 1], at.xn
            )
        )
    for z in order_z:
        index = at.shard(z, at.y, 1 - at.x)
        wait_sib(index)
        mine = my_part.at[index]
        remote(
            mine.at[pl.ds(*halves[0])], diag_y.at[z], ys_sem.at[z, 1], yr_sem.at[z, 1], at.yn
        ).wait_recv()
        add_into(mine, [mine, from_sib.at[index], diag_y.at[z]], halves[0])
        add_into(mine, [mine, from_sib.at[index]], halves[1])
        send(
            lambda z=z, mine=mine: remote(
                mine, from_x.at[z], xs_sem.at[z, 0], xr_sem.at[z, 0], at.xn
            )
        )
        index = at.shard(z, 1 - at.y, at.x)
        wait_sib(index)
        mine = my_part.at[index]
        remote(
            mine.at[pl.ds(*halves[1])], diag_x.at[z], xs_sem.at[z, 1], xr_sem.at[z, 1], at.xn
        ).wait_recv()
        add_into(mine, [mine, from_sib.at[index]], halves[0])
        shifted = diag_x.at[z]

        def body(step, carry, mine=mine, index=index, shifted=shifted):
            rows = pl.ds(pl.multiple_of(halves[1][0] + step * step_rows, 16), step_rows)
            base = pl.ds(pl.multiple_of(step * step_rows, 16), step_rows)
            total = (
                mine[rows, :].astype(jnp.float32)
                + from_sib[index, rows, :].astype(jnp.float32)
                + shifted[base, :].astype(jnp.float32)
            )
            mine[rows, :] = total.astype(jnp.bfloat16)
            return carry

        lax.fori_loop(0, halves[1][1] // step_rows, body, 0)
        send(
            lambda z=z, mine=mine: remote(
                mine, from_y.at[z], ys_sem.at[z, 0], yr_sem.at[z, 0], at.yn
            )
        )

    for z in order_z:
        index = at.shard(z, at.y, at.x)
        wait_sib(index)
        mine = my_part.at[index]
        remote(mine, from_x.at[z], xs_sem.at[z, 0], xr_sem.at[z, 0], at.xn).wait_recv()
        remote(mine, from_y.at[z], ys_sem.at[z, 0], yr_sem.at[z, 0], at.yn).wait_recv()
        base = [mine, from_sib.at[index], from_x.at[z], from_y.at[z]]

        for down in range(2):
            dev = at.down if down else at.up
            passes = (at.z > z) if down else (at.z < z)
            gets = (at.z < 3) if down else (at.z > 0)

            def arrive(z=z, mine=mine, down=down, dev=dev):
                remote(
                    mine, from_z.at[down, z], zs_sem.at[down, z], zr_sem.at[down, z], dev
                ).wait_recv()

            @pl.when(passes & gets)
            def _():
                arrive()
                add_into(acc_z.at[down, z], base + [from_z.at[down, z]], whole)

            @pl.when(passes & jnp.logical_not(gets))
            def _():
                add_into(acc_z.at[down, z], base, whole)

            send(
                lambda z=z, down=down, dev=dev: remote(
                    acc_z.at[down, z],
                    from_z.at[down, z],
                    zs_sem.at[down, z],
                    zr_sem.at[down, z],
                    dev,
                ),
                passes,
            )

    index = at.dp
    mine = my_part.at[index]
    base = [mine, from_sib.at[index], from_x.at[at.z], from_y.at[at.z]]
    add_into(total, base, whole)
    for down in range(2):

        @pl.when((at.z < 3) if down else (at.z > 0))
        def _(down=down):
            arrived = from_z.at[down, at.z]
            dev = at.down if down else at.up
            remote(
                mine, arrived, zs_sem.at[down, at.z], zr_sem.at[down, at.z], dev
            ).wait_recv()
            add_into(total, [total, arrived], whole)

    rows = lay.length - 16
    scale = 1.0 / LOSS_SCALE
    phase = lax.rem(lax.axis_index("dp") * lay.shard, LANES)
    back = lax.rem(LANES - phase, LANES)
    spare = lay.need - tail_from
    extra = total[tail_from : tail_from + 16, :] * scale
    stats[me] = jnp.zeros((STAT_ROWS, LANES), jnp.float32)
    stats[me, 1:3] = extra[spare : spare + 2]
    turned = pltpu.roll(total[...] * scale, back, 1)
    total[...] = turned
    lanes = lane_ids(lay.length - 8)
    lines = jnp.where(
        lanes < LANES - phase, total[: lay.length - 8, :], total[1 : lay.length - 7, :]
    )
    spots = lax.broadcasted_iota(jnp.int32, (lay.length - 8, LANES), 0) * LANES + lanes
    lines = jnp.where(spots < lay.shard, lines, 0.0)
    grad_ref[: lay.length - 8, :] = lines
    grad_ref[lay.length - 8 :, :] = jnp.zeros((8, LANES), jnp.float32)
    stats[me, 0:1] = jnp.sum(lines * lines, 0, keepdims=True)

    def tell(step):
        return remote(stats.at[me], stats.at[me], bs_sem.at[step], br_sem.at[step], peer(step))

    def hear(step):
        other = lax.rem(me + count - step, count)
        return remote(
            stats.at[other], stats.at[other], bs_sem.at[step], br_sem.at[step], peer(step)
        )

    def start_tell(step, carry):
        tell(step).start()
        return carry

    def finish(step, carry):
        hear(step).wait_recv()
        tell(step).wait_send()
        return carry

    lax.fori_loop(1, count, start_tell, 0)
    for cond, work in sends:
        guarded(cond, work)
    lax.fori_loop(1, count, finish, 0)
    everyone = stats[...]
    squares = jnp.sum(everyone[:, 0]) + jnp.sum(everyone[:, 1] * everyone[:, 1])
    squares = squares + jnp.sum(everyone[:, 2] * everyone[:, 2])
    norm_ref[...] = jnp.full((1, LANES), squares, jnp.float32)
    across = lay.features // LANES
    lines_half = 6 * across // MP
    for line in range(6 * across):
        half, place = line // lines_half, line % lines_half
        slot = (place // 2) * MP + half
        row, col = line // across, line % across
        shared_ref[row : row + 1, col * LANES : (col + 1) * LANES] = everyone[
            slot, 1 + place % 2 : 2 + place % 2
        ]


def scatter_gradients(lay, grads, bias_grad, shared_step):
    phase = (lax.axis_index("dp") * lay.shard) % LANES
    if lay.dp_count != 16:
        packed = pack_gradients(lay, grads, bias_grad)
        flat = packed.reshape(MP * lay.dp_count * lay.length, LANES)
        lines = lax.psum_scatter(flat, ("mp", "dp"), scatter_dimension=0, tiled=True)
        lines = lines.astype(jnp.float32).reshape(-1) / LOSS_SCALE
        lines = jnp.roll(lines, -phase)
        lines = jnp.where(jnp.arange(lines.size) < lay.shard, lines, 0.0)
        shared_grad = lax.psum(shared_step, ("dp", "mp")) / LOSS_SCALE
        squares = lax.psum(jnp.sum(lines * lines), ("dp", "mp"))
        squares = squares + jnp.sum(shared_grad * shared_grad)
        return lines.reshape(1, -1), squares, shared_grad
    tail_from = lay.need // 16 * 16
    spare = lay.need - tail_from
    assert spare + 2 <= 16
    across = lay.features // LANES
    lines_half = 6 * across // MP
    assert lines_half <= 32 and lay.length * LANES - lay.shard >= 8 * LANES
    tail = jnp.pad(
        shared_step.reshape(MP, lines_half, LANES), ((0, 0), (0, 32 - lines_half), (0, 0))
    )
    tail = jnp.pad(tail.reshape(MP, 16, 2, LANES), ((0, 0), (0, 0), (spare, 14 - spare), (0, 0)))
    size = (lay.length, LANES)
    low = jnp.bfloat16
    vmem = pl.BlockSpec(memory_space=pltpu.VMEM)
    anywhere = pl.BlockSpec(memory_space=pl.ANY)
    lines, squares, shared_grad = pl.pallas_call(
        partial(scatter_kernel, lay),
        out_shape=[
            jax.ShapeDtypeStruct(size, jnp.float32),
            jax.ShapeDtypeStruct((1, LANES), jnp.float32),
            jax.ShapeDtypeStruct(shared_step.shape, jnp.float32),
        ],
        in_specs=[anywhere] * 4 + [vmem] * 2,
        out_specs=[vmem] * 3,
        scratch_shapes=[
            pltpu.VMEM((lay.features, 3 * lay.head_cols), low),
            pltpu.VMEM((lay.head_cols, lay.features), low),
            pltpu.VMEM((lay.features, lay.ffn_cols), low),
            pltpu.VMEM((lay.ffn_cols, lay.features), low),
            pltpu.VMEM((lay.flat_rows, LANES), jnp.float32),
            pltpu.VMEM((MP, 16) + size, low),
            pltpu.VMEM((16,) + size, low),
            pltpu.VMEM((4,) + size, low),
            pltpu.VMEM((4,) + size, low),
            pltpu.VMEM((4, lay.length - lay.cut, LANES), low),
            pltpu.VMEM((4, lay.cut, LANES), low),
            pltpu.VMEM((2, 4) + size, low),
            pltpu.VMEM((2, 4) + size, low),
            pltpu.VMEM(size, jnp.float32),
            pltpu.VMEM((16 * MP, STAT_ROWS, LANES), jnp.float32),
            DMA((4,)),
            DMA((16,)),
            DMA((16,)),
            DMA((4, 2)),
            DMA((4, 2)),
            DMA((4, 2)),
            DMA((4, 2)),
            DMA((2, 4)),
            DMA((2, 4)),
            DMA((16 * MP,)),
            DMA((16 * MP,)),
        ],
        compiler_params=pltpu.CompilerParams(
            collective_id=1, has_side_effects=True, vmem_limit_bytes=VMEM_LIMIT
        ),
        name="scatter_gradients",
    )(*grads, bias_grad, tail)
    return lines.reshape(1, -1), squares[0, 0], shared_grad


def exchange_kernel(
    pooled_ref,
    codes_ref,
    labels_ref,
    grad_ref,
    pooled,
    outgoing,
    incoming,
    returning,
    arrived,
    sib_sem,
    go_send,
    go_recv,
    back_send,
    back_recv,
):
    dp = lax.axis_index("dp")
    half = lax.axis_index("mp")
    sib = (dp, 1 - half)
    slots, capacity, features = outgoing.shape
    codes = slots * capacity
    core_sents = pooled_ref.shape[0]

    def peer(step):
        return (lax.rem(dp + step, slots), half)

    bar = pltpu.get_barrier_semaphore()
    pl.semaphore_signal(bar, inc=1, device_id=sib, device_id_type=MESH)
    for step in range(1, slots):
        pl.semaphore_signal(bar, inc=1, device_id=peer(step), device_id_type=MESH)
    pooled[half] = pooled_ref[...]
    pl.semaphore_wait(bar, slots)
    share = pltpu.make_async_remote_copy(
        src_ref=pooled_ref,
        dst_ref=pooled.at[half],
        send_sem=sib_sem.at[0],
        recv_sem=sib_sem.at[1],
        device_id=sib,
        device_id_type=MESH,
    )
    share.start()

    code_ids = lax.broadcasted_iota(jnp.int32, (codes, codes), 0)
    send_map = (code_ids == codes_ref[0:1, :]).astype(jnp.bfloat16)
    pairs = codes // 2
    even_map = (code_ids[:, :pairs] == codes_ref[1:2, :pairs]).astype(jnp.bfloat16)
    odd_map = (code_ids[:, :pairs] == codes_ref[2:3, :pairs]).astype(jnp.bfloat16)
    share.wait()
    everything = jnp.concatenate([pooled[0], pooled[1]], 0)
    out = jnp.dot(send_map, everything, preferred_element_type=jnp.float32)
    outgoing[...] = out.reshape(outgoing.shape).astype(jnp.bfloat16)

    def copy(src, dst, send_sem, recv_sem, step):
        return pltpu.make_async_remote_copy(
            src_ref=src,
            dst_ref=dst,
            send_sem=send_sem.at[step],
            recv_sem=recv_sem.at[step],
            device_id=peer(step),
            device_id_type=MESH,
        )

    def all_to_all(src, dst, send_sem, recv_sem):
        for step in range(1, slots):
            copy(src.at[lax.rem(dp + step, slots)], dst.at[dp], send_sem, recv_sem, step).start()
        dst[dp] = src[dp]
        for step in range(1, slots):
            sender = lax.rem(dp + slots - step, slots)
            copy(src.at[sender], dst.at[sender], send_sem, recv_sem, step).wait()

    all_to_all(outgoing, incoming, go_send, go_recv)
    items = incoming[...].astype(jnp.float32).reshape(codes, features).astype(jnp.bfloat16)
    left = lax.dot_general(even_map, items, FIRST, preferred_element_type=jnp.float32)
    right = lax.dot_general(odd_map, items, FIRST, preferred_element_type=jnp.float32)
    inner = jnp.sum(left * right, -1, keepdims=True)
    left_inv = lax.rsqrt(jnp.sum(left * left, -1, keepdims=True) + 1e-06)
    right_inv = lax.rsqrt(jnp.sum(right * right, -1, keepdims=True) + 1e-06)
    both = left_inv * right_inv
    cosine = inner * both
    square = (pairs, pairs)
    eye = lax.broadcasted_iota(jnp.int32, square, 0) == lax.broadcasted_iota(
        jnp.int32, square, 1
    )
    target = jnp.sum(
        jnp.where(eye, labels_ref[0:1, :pairs].astype(jnp.float32), 0.0), 1, keepdims=True
    )
    slope = (2.0 * LOSS_SCALE) * (cosine - target / 5.0)
    left_grad = slope * (both * right - (cosine * left_inv * left_inv) * left)
    right_grad = slope * (both * left - (cosine * right_inv * right_inv) * right)
    back = jnp.dot(
        even_map, left_grad.astype(jnp.bfloat16), preferred_element_type=jnp.float32
    ) + jnp.dot(odd_map, right_grad.astype(jnp.bfloat16), preferred_element_type=jnp.float32)
    returning[...] = back.reshape(returning.shape).astype(jnp.bfloat16)
    all_to_all(returning, arrived, back_send, back_recv)
    items = arrived[...].astype(jnp.float32).reshape(codes, features).astype(jnp.bfloat16)
    grads = lax.dot_general(send_map, items, FIRST, preferred_element_type=jnp.float32)
    grad_ref[...] = jnp.where(half == 0, grads[:core_sents], grads[core_sents:])


def exchange(pooled_core, sentence_dest, pair_source, labels, dp_count, capacity):
    core_sents, features = pooled_core.shape
    codes = dp_count * capacity
    send_code = sentence_dest[:, 0] * capacity + sentence_dest[:, 1]
    take_code = pair_source[:, 0] * capacity + pair_source[:, 1]
    if dp_count == 16 and codes == send_code.shape[0] == 2 * core_sents:
        pairs = take_code.reshape(-1, 2).T
        pairs = jnp.pad(pairs, ((0, 0), (0, codes - pairs.shape[1])))
        table = jnp.concatenate([send_code[None], pairs, jnp.zeros((5, codes), jnp.int32)], 0)
        wide = (dp_count, capacity, features)
        low = jnp.bfloat16
        vmem = pl.BlockSpec(memory_space=pltpu.VMEM)
        return pl.pallas_call(
            exchange_kernel,
            out_shape=jax.ShapeDtypeStruct((core_sents, features), jnp.float32),
            in_specs=[vmem] * 3,
            out_specs=vmem,
            scratch_shapes=[pltpu.VMEM((MP, core_sents, features), low)]
            + [pltpu.VMEM(wide, low)] * 4
            + [DMA((2,))]
            + [DMA((dp_count,))] * 4,
            compiler_params=pltpu.CompilerParams(
                collective_id=2, has_side_effects=True, vmem_limit_bytes=VMEM_LIMIT
            ),
            name="exchange_pairs",
        )(pooled_core, table, labels[None])
    mp_index = lax.axis_index("mp")
    pooled_flat = lax.all_gather(pooled_core, "mp", axis=0, tiled=True)
    code_ids = jnp.arange(codes, dtype=jnp.int32)
    send_map = (code_ids[:, None] == send_code[None, :]).astype(jnp.bfloat16)
    outgoing = jnp.dot(send_map, pooled_flat, preferred_element_type=jnp.float32).astype(
        jnp.bfloat16
    )
    outgoing = outgoing.reshape(dp_count, capacity, features)
    incoming = lax.all_to_all(outgoing, "dp", split_axis=0, concat_axis=0, tiled=True).reshape(
        codes, features
    )
    take_map = (take_code[:, None] == code_ids[None, :]).astype(jnp.bfloat16)
    pair_items = jnp.dot(take_map, incoming, preferred_element_type=jnp.float32)
    item_grad = jax.grad(pair_loss)(pair_items, labels).astype(jnp.bfloat16)
    returning = jnp.dot(take_map.T, item_grad, preferred_element_type=jnp.float32).astype(
        jnp.bfloat16
    )
    returning = returning.reshape(dp_count, capacity, features)
    arrived = lax.all_to_all(returning, "dp", split_axis=0, concat_axis=0, tiled=True).reshape(
        codes, features
    )
    core_map = lax.dynamic_slice_in_dim(send_map, mp_index * core_sents, core_sents, 1)
    return jnp.dot(core_map.T, arrived, preferred_element_type=jnp.float32)


SCORE_SCALE = HEAD_DIM ** (-0.5)
LAST = (((1,), (1,)), ((), ()))
FIRST = (((0,), (0,)), ((), ()))


def low_lanes(rows):
    return lax.broadcasted_iota(jnp.int32, (rows, LANES), 1) < HEAD_DIM


def one_head(tile, odd):
    mask = low_lanes(tile.shape[0])
    if odd:
        return jnp.where(mask, jnp.zeros_like(tile), tile)
    return jnp.where(mask, tile, jnp.zeros_like(tile))


def attend_kernel(tiles, qkv_ref, seg_col_ref, seg_row_ref, out_ref, log_ref):
    width = tiles * LANES
    bias = jnp.where(seg_col_ref[...] == seg_row_ref[0], 0.0, -1e30)
    logs = []
    for tile in range(tiles):
        cols = slice(tile * LANES, (tile + 1) * LANES)
        queries = qkv_ref[:, cols] * SCORE_SCALE
        keys = qkv_ref[:, width + tile * LANES : width + (tile + 1) * LANES]
        values = qkv_ref[:, 2 * width + tile * LANES : 2 * width + (tile + 1) * LANES]
        mixed = []
        for odd in range(2):
            scores = lax.dot_general(
                one_head(queries, odd), keys, LAST, preferred_element_type=jnp.float32
            )
            scores = scores + bias
            row_max = jnp.max(scores, -1, keepdims=True)
            exponent = jnp.exp(scores - row_max)
            row_total = jnp.sum(exponent, -1, keepdims=True)
            probs = exponent.astype(jnp.bfloat16)
            mixed.append(
                jnp.dot(probs, values, preferred_element_type=jnp.float32) * (1.0 / row_total)
            )
            logs.append(row_max + jnp.log(row_total))
        both = jnp.where(low_lanes(ROW), mixed[0], mixed[1])
        out_ref[:, cols] = both.astype(jnp.bfloat16)
    log_ref[0] = jnp.concatenate(logs + [logs[0]] * (8 - 2 * tiles), 1)


def attend(qkv, seg_col, seg_row, head_cols):
    rows = qkv.shape[0] // ROW
    return pl.pallas_call(
        partial(attend_kernel, head_cols // LANES),
        grid=(rows, MP),
        in_specs=[
            pl.BlockSpec((ROW, 3 * head_cols), lambda r, m: (r, m)),
            pl.BlockSpec((ROW, 1), lambda r, m: (r, 0)),
            pl.BlockSpec((1, 1, ROW), lambda r, m: (r, 0, 0)),
        ],
        out_specs=[
            pl.BlockSpec((ROW, head_cols), lambda r, m: (r, m)),
            pl.BlockSpec((1, ROW, 8), lambda r, m: (m, r, 0)),
        ],
        out_shape=[
            jax.ShapeDtypeStruct((rows * ROW, MP * head_cols), jnp.bfloat16),
            jax.ShapeDtypeStruct((MP, rows * ROW, 8), jnp.float32),
        ],
        compiler_params=pltpu.CompilerParams(vmem_limit_bytes=VMEM_LIMIT),
        name="attend",
    )(qkv, seg_col, seg_row)


def attend_back_kernel(
    tiles, qkv_ref, grad_ref, log_ref, seg_col_ref, seg_wide_ref, out_ref, key_acc, value_acc
):
    width = tiles * LANES
    block, window = LANES, 2 * LANES
    key_acc[...] = jnp.zeros_like(key_acc)
    value_acc[...] = jnp.zeros_like(value_acc)
    for step in range(ROW // block):
        start = min(max(step * block - block // 2, 0), ROW - window)
        rows = slice(step * block, (step + 1) * block)
        span = slice(start, start + window)
        bias = jnp.where(seg_col_ref[rows, :] == seg_wide_ref[0, step], 0.0, -1e30)
        for tile in range(tiles):
            cols = slice(tile * LANES, (tile + 1) * LANES)
            queries = qkv_ref[rows, cols] * SCORE_SCALE
            keys = qkv_ref[span, width + tile * LANES : width + (tile + 1) * LANES]
            values = qkv_ref[span, 2 * width + tile * LANES : 2 * width + (tile + 1) * LANES]
            mixed_grad = grad_ref[rows, cols]
            query_grad = key_grad = value_grad = 0.0
            for odd in range(2):
                head = 2 * tile + odd
                query_one = one_head(queries, odd)
                grad_one = one_head(mixed_grad, odd)
                scores = lax.dot_general(
                    query_one, keys, LAST, preferred_element_type=jnp.float32
                )
                probs = jnp.exp((scores + bias) - log_ref[0, rows, head : head + 1])
                prob_grad = lax.dot_general(
                    grad_one, values, LAST, preferred_element_type=jnp.float32
                )
                row_inner = jnp.sum(prob_grad * probs, -1, keepdims=True)
                score_grad = (probs * (prob_grad - row_inner)).astype(jnp.bfloat16)
                value_grad += lax.dot_general(
                    probs.astype(jnp.bfloat16),
                    grad_one,
                    FIRST,
                    preferred_element_type=jnp.float32,
                )
                query_grad += jnp.dot(
                    score_grad, one_head(keys, odd), preferred_element_type=jnp.float32
                )
                key_grad += lax.dot_general(
                    score_grad, query_one, FIRST, preferred_element_type=jnp.float32
                )
            out_ref[rows, cols] = (query_grad * SCORE_SCALE).astype(jnp.bfloat16)
            key_acc[span, cols] += key_grad
            value_acc[span, cols] += value_grad
    out_ref[:, width : 2 * width] = key_acc[...].astype(jnp.bfloat16)
    out_ref[:, 2 * width :] = value_acc[...].astype(jnp.bfloat16)


def attend_back(qkv, mixed_grad, logs, seg_col, seg_row, head_cols):
    rows = qkv.shape[0] // ROW
    window = 2 * LANES
    starts = [
        min(max(step * LANES - LANES // 2, 0), ROW - window) for step in range(ROW // LANES)
    ]
    seg_wide = jnp.stack([seg_row[:, :, start : start + window] for start in starts], 1)
    return pl.pallas_call(
        partial(attend_back_kernel, head_cols // LANES),
        grid=(rows, MP),
        in_specs=[
            pl.BlockSpec((ROW, 3 * head_cols), lambda r, m: (r, m)),
            pl.BlockSpec((ROW, head_cols), lambda r, m: (r, m)),
            pl.BlockSpec((1, ROW, 8), lambda r, m: (m, r, 0)),
            pl.BlockSpec((ROW, 1), lambda r, m: (r, 0)),
            pl.BlockSpec((1, ROW // LANES, 1, window), lambda r, m: (r, 0, 0, 0)),
        ],
        out_specs=pl.BlockSpec((ROW, 3 * head_cols), lambda r, m: (r, m)),
        out_shape=jax.ShapeDtypeStruct(qkv.shape, jnp.bfloat16),
        scratch_shapes=[pltpu.VMEM((ROW, head_cols), jnp.float32)] * 2,
        compiler_params=pltpu.CompilerParams(vmem_limit_bytes=VMEM_LIMIT),
        name="attend_back",
    )(qkv, mixed_grad, logs, seg_col, seg_wide)


def back_norm(values_in, scale_vec, grad):
    center = jnp.mean(values_in, -1, keepdims=True)
    centered = values_in - center
    inverse = lax.rsqrt(jnp.mean(centered * centered, -1, keepdims=True) + NORM_EPS)
    unit = centered * inverse
    scaled = grad * scale_vec
    out = inverse * (
        scaled
        - jnp.mean(scaled, -1, keepdims=True)
        - unit * jnp.mean(scaled * unit, -1, keepdims=True)
    )
    return out, jnp.sum(grad * unit, 0), jnp.sum(grad, 0)


def per_device(
    tokens,
    segments,
    sentence_dest,
    pair_source,
    labels,
    params,
    first,
    second,
    shared,
    shared_first,
    shared_second,
):
    features = tokens.shape[1]
    dp_count = lax.axis_size("dp")
    dp_index = lax.axis_index("dp")
    mp_index = lax.axis_index("mp")
    shard = params.shape[1]
    lay = Layout(features, shard, dp_count)
    head_cols = lay.head_cols
    sent_slots = ROWS_DEV * SEG
    slot_capacity = max(2, sent_slots // dp_count)
    params_total = MP * shard * dp_count + 6 * features
    core_rows = ROWS_CORE * ROW

    own = jnp.pad(params, ((0, 0), (0, lay.length * LANES - shard))).reshape(lay.length, LANES)
    w_qkv, w_attn, w_in, w_out, biases = unpack_weights(lay, gather_lines(lay, own))
    head_lines = head_cols // LANES
    b_query = biases[:, :head_lines].reshape(MP, head_cols)
    b_value = biases[:, head_lines : 2 * head_lines].reshape(MP, head_cols)
    b_in = biases[:, 2 * head_lines : lay.bias_lines].reshape(MP * lay.ffn_cols)
    b_qkv = jnp.concatenate([b_query, jnp.zeros_like(b_query), b_value], 1).reshape(-1)

    tokens_core = lax.dynamic_slice_in_dim(tokens, mp_index * core_rows, core_rows, 0)
    segments_core = lax.dynamic_slice_in_dim(segments, mp_index * core_rows, core_rows, 0)
    seg_col = segments_core.reshape(core_rows, 1)
    seg_row = segments_core.reshape(ROWS_CORE, 1, ROW)

    qkv = (jnp.dot(tokens_core, w_qkv, preferred_element_type=jnp.float32) + b_qkv).astype(
        jnp.bfloat16
    )
    mixed, logs = attend(qkv, seg_col, seg_row, head_cols)
    attn_out = jnp.dot(mixed, w_attn, preferred_element_type=jnp.float32) + shared[4]
    resid_one = tokens_core.astype(jnp.float32) + attn_out
    hidden = normalize(resid_one, shared[0], shared[1])
    hidden_low = hidden.astype(jnp.bfloat16)
    up_proj = jnp.dot(hidden_low, w_in, preferred_element_type=jnp.float32) + b_in
    cdf = 0.5 * (1.0 + lax.erf(up_proj * (0.5**0.5)))
    activated = (up_proj * cdf).astype(jnp.bfloat16)
    slope = (
        cdf + up_proj * jnp.exp(-0.5 * up_proj * up_proj) * ((2.0 * math.pi) ** -0.5)
    ).astype(jnp.bfloat16)
    ffn_out = jnp.dot(activated, w_out, preferred_element_type=jnp.float32) + shared[5]
    resid_two = hidden + ffn_out
    encoded_core = normalize(resid_two, shared[2], shared[3])
    encoded = lax.all_gather(encoded_core.astype(jnp.bfloat16), "mp", axis=0, tiled=True)

    slot_ids = jnp.arange(SEG, dtype=jnp.int32)
    onehot = (seg_row == slot_ids[None, :, None]).astype(jnp.float32)
    weight = onehot / jnp.sum(onehot, 2, keepdims=True)
    pooled_core = jnp.einsum(
        "kvf,kfo->kvo",
        weight,
        encoded_core.reshape(ROWS_CORE, ROW, features),
        precision=TOP_PRECISION,
    ).astype(jnp.bfloat16)
    pooled_grad = exchange(
        pooled_core.reshape(ROWS_CORE * SEG, features),
        sentence_dest,
        pair_source,
        labels,
        dp_count,
        slot_capacity,
    )

    encoded_grad = jnp.einsum(
        "jix,jip->jxp",
        weight,
        pooled_grad.reshape(ROWS_CORE, SEG, features),
        precision=TOP_PRECISION,
    ).reshape(core_rows, features)
    resid_two_grad, scale_two, shift_two = back_norm(resid_two, shared[2], encoded_grad)
    ffn_grad = resid_two_grad.astype(jnp.bfloat16)
    act_grad = lax.dot_general(ffn_grad, w_out, LAST, preferred_element_type=jnp.float32)
    up_grad = (act_grad * slope.astype(jnp.float32)).astype(jnp.bfloat16)
    w_out_grad = lax.dot_general(activated, ffn_grad, FIRST, preferred_element_type=jnp.float32)
    w_in_grad = lax.dot_general(hidden_low, up_grad, FIRST, preferred_element_type=jnp.float32)
    hidden_term = lax.dot_general(up_grad, w_in, LAST, preferred_element_type=jnp.float32)
    hidden_grad = resid_two_grad + hidden_term
    resid_one_grad, scale_one, shift_one = back_norm(resid_one, shared[0], hidden_grad)
    attn_grad = resid_one_grad.astype(jnp.bfloat16)
    w_attn_grad = lax.dot_general(mixed, attn_grad, FIRST, preferred_element_type=jnp.float32)
    mixed_grad = lax.dot_general(
        attn_grad, w_attn, LAST, preferred_element_type=jnp.float32
    ).astype(jnp.bfloat16)
    qkv_grad = attend_back(qkv, mixed_grad, logs, seg_col, seg_row, head_cols)
    w_qkv_grad = lax.dot_general(
        tokens_core, qkv_grad, FIRST, preferred_element_type=jnp.float32
    )
    input_term = lax.dot_general(qkv_grad, w_qkv, LAST, preferred_element_type=jnp.float32)
    input_core = resid_one_grad + input_term
    input_grad = lax.all_gather(input_core, "mp", axis=0, tiled=True)

    qkv_sums = jnp.sum(qkv_grad.astype(jnp.float32), 0).reshape(MP, 3, head_lines, LANES)
    in_sums = jnp.sum(up_grad.astype(jnp.float32), 0).reshape(MP, -1, LANES)
    bias_grad = jnp.concatenate([qkv_sums[:, 0], qkv_sums[:, 2], in_sums], 1)
    bias_grad = jnp.pad(bias_grad, ((0, 0), (0, lay.bias_rows - lay.bias_lines), (0, 0)))
    shared_step = jnp.stack(
        [
            scale_one,
            shift_one,
            scale_two,
            shift_two,
            jnp.sum(attn_grad.astype(jnp.float32), 0),
            jnp.sum(ffn_grad.astype(jnp.float32), 0),
        ]
    )
    grad_lines, total_squares, shared_grad = scatter_gradients(
        lay,
        [g.astype(jnp.bfloat16) for g in (w_qkv_grad, w_attn_grad, w_in_grad, w_out_grad)],
        bias_grad,
        shared_step,
    )
    flat_grad = grad_lines[:, :shard]
    norm_value = jnp.sqrt(total_squares)
    factor = jnp.minimum(1.0, CLIP_NORM / norm_value)
    step_count = STEP_COUNT
    params_new, first_new, second_new = adamw(
        params, first, second, flat_grad, factor, step_count, LEARN_RATE
    )
    shared_new, shared_first_new, shared_second_new = adamw(
        shared, shared_first, shared_second, shared_grad, factor, step_count, SHARED_RATE
    )
    grad_unit = math.sqrt(params_total) / CLIP_NORM
    params_grad = flat_grad * factor * grad_unit
    shared_grad_out = shared_grad * factor * grad_unit
    return (
        encoded,
        input_grad,
        norm_value.reshape(1),
        params_new,
        first_new,
        second_new,
        params_new.astype(jnp.bfloat16),
        shared_new,
        shared_first_new,
        shared_second_new,
        params_grad,
        shared_grad_out,
    )


def solution(mesh):
    in_specs = (
        P("dp", None),
        P("dp"),
        P("dp", None),
        P("dp", None),
        P("dp"),
        P("mp", "dp"),
        P("mp", "dp"),
        P("mp", "dp"),
        P(),
        P(),
        P(),
    )
    out_specs = (
        P("dp", None),
        P("dp", None),
        P(),
        P("mp", "dp"),
        P("mp", "dp"),
        P("mp", "dp"),
        P("mp", "dp"),
        P(),
        P(),
        P(),
        P("mp", "dp"),
        P(),
    )
    return jax.shard_map(
        per_device, mesh=mesh, in_specs=in_specs, out_specs=out_specs, check_vma=False
    )
```

```python
from functools import partial
import math

import jax
import jax.numpy as jnp
from jax import lax
from jax.experimental import pallas as pl
from jax.experimental.pallas import tpu as pltpu
from jax.sharding import PartitionSpec as P

HEAD_DIM = 64
FF = 3072
ROW = 512
SEG = 32
RPM = 2
MB = 2
MP = 2
LANES = 128
ROWS_DEV = MB * RPM
ROWS_CORE = ROWS_DEV // MP


LOSS_SCALE = 1024.0
CLIP_NORM = 0.5
LEARN_RATE = 0.1
SHARED_RATE = 0.5
BETA_ONE = 0.9
BETA_TWO = 0.999
ADAM_EPS = 1e-08
DECAY = 0.01
NORM_EPS = 1e-12
STEP_COUNT = 10.0
TOP_PRECISION = lax.Precision.HIGHEST
MESH = pl.DeviceIdType.MESH
DMA = pltpu.SemaphoreType.DMA
VMEM_LIMIT = 60 << 20
VMEM_MOST = 62 << 20
PIECES = 4


def normalize(values_in, scale_vec, shift_vec):
    center = jnp.mean(values_in, -1, keepdims=True)
    centered = values_in - center
    spread = jnp.mean(centered * centered, -1, keepdims=True)
    return centered * lax.rsqrt(spread + NORM_EPS) * scale_vec + shift_vec


def pair_loss(pair_items, labels):
    first_vec = pair_items[..., 0::2, :]
    second_vec = pair_items[..., 1::2, :]
    inner_prod = jnp.sum(first_vec * second_vec, -1)
    cosine = (
        inner_prod
        * lax.rsqrt(jnp.sum(first_vec * first_vec, -1) + 1e-06)
        * lax.rsqrt(jnp.sum(second_vec * second_vec, -1) + 1e-06)
    )
    error_term = cosine - labels.astype(jnp.float32) / 5.0
    return LOSS_SCALE * jnp.sum(error_term * error_term)


def adamw(weight, moment_one, moment_two, gradient, factor, step_count, rate):
    clipped = gradient * factor
    first_new = BETA_ONE * moment_one + (1.0 - BETA_ONE) * clipped
    second_new = BETA_TWO * moment_two + (1.0 - BETA_TWO) * clipped * clipped
    first_hat = first_new / (1.0 - BETA_ONE**step_count)
    second_hat = second_new / (1.0 - BETA_TWO**step_count)
    weight_new = weight - rate * (first_hat / (jnp.sqrt(second_hat) + ADAM_EPS) + DECAY * weight)
    return (weight_new, first_new, second_new)


class Layout:
    def __init__(self, features, shard, dp_count):
        self.features = features
        self.shard = shard
        self.dp_count = dp_count
        self.head_cols = features // MP
        self.ffn_cols = FF // MP
        self.total = shard * dp_count
        self.lines = self.total // LANES
        assert self.lines * LANES == self.total
        self.starts = [index * shard // LANES for index in range(dp_count)]
        need = max(
            ((index + 1) * shard - 1) // LANES - index * shard // LANES + 1
            for index in range(dp_count)
        )
        self.need = need
        self.length = -(-(need + 6) // (16 * PIECES)) * (16 * PIECES)
        self.cut = self.length // 2
        self.piece = self.length // PIECES
        self.step = max(
            rows for rows in range(16, 257, 16) if self.piece % rows == 0
        )
        self.mats = []
        offset = 0
        for height, extent in (
            (features, 3 * self.head_cols),
            (self.head_cols, features),
            (features, self.ffn_cols),
            (self.ffn_cols, features),
        ):
            assert extent % LANES == 0 and height % LANES == 0
            self.mats.append((offset, height, extent // LANES))
            offset += height * (extent // LANES)
        self.bias_start = offset
        self.bias_lines = self.lines - offset
        self.bias_rows = -(-self.bias_lines // 8) * 8
        self.flat_rows = -(-(self.starts[-1] + self.length) // 8) * 8


def weight_specs(lay):
    specs = [
        pl.BlockSpec((lay.features, 3 * lay.head_cols), lambda half: (0, half)),
        pl.BlockSpec((lay.head_cols, lay.features), lambda half: (half, 0)),
        pl.BlockSpec((lay.features, lay.ffn_cols), lambda half: (0, half)),
        pl.BlockSpec((lay.ffn_cols, lay.features), lambda half: (half, 0)),
        pl.BlockSpec((1, lay.bias_rows, LANES), lambda half: (half, 0, 0)),
    ]
    shapes = [
        (lay.features, MP * 3 * lay.head_cols),
        (MP * lay.head_cols, lay.features),
        (lay.features, MP * lay.ffn_cols),
        (MP * lay.ffn_cols, lay.features),
    ]
    return specs, shapes


def unpack_kernel(lay, lines_ref, qkv_ref, attn_ref, in_ref, out_ref, bias_ref, flat):
    for index in range(lay.dp_count):
        start = lay.starts[index]
        if index > 0:
            kept = flat[start : start + 1, :]
        flat[start : start + lay.length, :] = lines_ref[0, index].astype(jnp.float32)
        if index > 0:
            flat[start : start + 1, :] += kept
    for (offset, height, cols), ref in zip(lay.mats, (qkv_ref, attn_ref, in_ref, out_ref)):

        def body(step, carry, offset=offset, cols=cols, ref=ref):
            row = pl.multiple_of(step * LANES, LANES)
            for col in range(cols):
                block = flat[pl.ds(offset + row * cols + col, LANES, stride=cols), :]
                ref[pl.ds(row, LANES), col * LANES : (col + 1) * LANES] = block.astype(
                    jnp.bfloat16
                )
            return carry

        lax.fori_loop(0, height // LANES, body, 0)
    bias_ref[0] = flat[lay.bias_start : lay.bias_start + lay.bias_rows, :]


def unpack_weights(lay, gathered):
    specs, shapes = weight_specs(lay)
    return pl.pallas_call(
        partial(unpack_kernel, lay),
        grid=(MP,),
        in_specs=[
            pl.BlockSpec((1, lay.dp_count, lay.length, LANES), lambda half: (half, 0, 0, 0))
        ],
        out_specs=specs,
        out_shape=[jax.ShapeDtypeStruct(s, jnp.bfloat16) for s in shapes]
        + [jax.ShapeDtypeStruct((MP, lay.bias_rows, LANES), jnp.float32)],
        scratch_shapes=[pltpu.VMEM((lay.flat_rows, LANES), jnp.float32)],
        compiler_params=pltpu.CompilerParams(vmem_limit_bytes=VMEM_LIMIT),
        name="unpack_weights",
    )(gathered)


def pack_kernel(lay, qkv_ref, attn_ref, in_ref, out_ref, bias_ref, lines_ref, flat):
    for (offset, height, cols), ref in zip(lay.mats, (qkv_ref, attn_ref, in_ref, out_ref)):

        def body(step, carry, offset=offset, cols=cols, ref=ref):
            row = pl.multiple_of(step * LANES, LANES)
            for col in range(cols):
                block = ref[pl.ds(row, LANES), col * LANES : (col + 1) * LANES]
                flat[pl.ds(offset + row * cols + col, LANES, stride=cols), :] = block.astype(
                    jnp.float32
                )
            return carry

        lax.fori_loop(0, height // LANES, body, 0)
    tail = lay.flat_rows - lay.lines
    if tail:
        flat[lay.lines :, :] = jnp.zeros((tail, LANES), jnp.float32)
    flat[lay.bias_start : lay.lines, :] = bias_ref[0, : lay.bias_lines]
    for index in range(lay.dp_count):
        start = lay.starts[index]
        lines_ref[0, index] = flat[start : start + lay.length, :].astype(jnp.bfloat16)


def pack_gradients(lay, grads, bias_grad):
    specs, _ = weight_specs(lay)
    return pl.pallas_call(
        partial(pack_kernel, lay),
        grid=(MP,),
        in_specs=specs,
        out_specs=pl.BlockSpec(
            (1, lay.dp_count, lay.length, LANES), lambda half: (half, 0, 0, 0)
        ),
        out_shape=jax.ShapeDtypeStruct((MP, lay.dp_count, lay.length, LANES), jnp.bfloat16),
        scratch_shapes=[pltpu.VMEM((lay.flat_rows, LANES), jnp.float32)],
        compiler_params=pltpu.CompilerParams(vmem_limit_bytes=VMEM_LIMIT),
        name="pack_gradients",
    )(*grads, bias_grad)


class Place:
    def __init__(self):
        self.dp = lax.axis_index("dp")
        self.half = lax.axis_index("mp")
        self.z = self.dp // 4
        self.y = (self.dp // 2) % 2
        self.x = self.dp % 2
        self.has_up = self.z < 3
        self.has_down = self.z > 0
        self.up = (jnp.minimum(self.dp + 4, 12 + self.dp % 4), self.half)
        self.down = (jnp.maximum(self.dp - 4, self.dp % 4), self.half)
        self.xn = (self.shard(self.z, self.y, 1 - self.x), self.half)
        self.yn = (self.shard(self.z, 1 - self.y, self.x), self.half)
        self.sib = (self.dp, 1 - self.half)

    def shard(self, z, y, x):
        return z * 4 + y * 2 + x

    def barrier(self):
        bar = pltpu.get_barrier_semaphore()
        for dev in (self.xn, self.yn, self.sib):
            pl.semaphore_signal(bar, inc=1, device_id=dev, device_id_type=MESH)

        @pl.when(self.has_up)
        def _():
            pl.semaphore_signal(bar, inc=1, device_id=self.up, device_id_type=MESH)

        @pl.when(self.has_down)
        def _():
            pl.semaphore_signal(bar, inc=1, device_id=self.down, device_id_type=MESH)

        pl.semaphore_wait(
            bar, 3 + jnp.where(self.has_up, 1, 0) + jnp.where(self.has_down, 1, 0)
        )


def guarded(cond, work):
    if cond is None:
        work()
    else:
        pl.when(cond)(work)


def lane_ids(rows):
    return lax.broadcasted_iota(jnp.int32, (rows, LANES), 1)


def shift_into_lines(lay, own_ref, rolled, put):
    phase = lax.rem(lax.axis_index("dp") * lay.shard, LANES)
    rows = lay.length
    rolled[0:8, :] = jnp.zeros((8, LANES), jnp.float32)
    rolled[8 : 8 + rows, :] = pltpu.roll(own_ref[...], phase, 1)
    late = rolled[7 : 7 + rows, :]
    put(jnp.where(lane_ids(rows) < phase, late, rolled[8 : 8 + rows, :]))


def gather_kernel(
    lay, own_ref, buf, rolled, zs_sem, zr_sem, xs_sem, xr_sem, ys_sem, yr_sem, ss_sem, sr_sem
):
    at = Place()
    halves = ((0, lay.cut), (lay.cut, lay.length - lay.cut))

    def put(lines):
        buf[at.half, at.dp] = lines.astype(jnp.bfloat16)

    shift_into_lines(lay, own_ref, rolled, put)
    at.barrier()
    sends = []

    def remote(index, part, send_sem, recv_sem, dev):
        piece = buf.at[at.half, index, pl.ds(*halves[part])]
        return pltpu.make_async_remote_copy(
            src_ref=piece,
            dst_ref=piece,
            send_sem=send_sem,
            recv_sem=recv_sem,
            device_id=dev,
            device_id_type=MESH,
        )

    def send(index, part, send_sem, recv_sem, dev, cond=None):
        guarded(cond, lambda: remote(index, part, send_sem, recv_sem, dev).start())
        sends.append((cond, lambda: remote(index, part, send_sem, recv_sem, dev).wait_send()))

    def wait(index, part, send_sem, recv_sem, dev, cond=None):
        guarded(cond, lambda: remote(index, part, send_sem, recv_sem, dev).wait_recv())

    def share(index, part, cond=None):
        send(index, part, ss_sem.at[index, part], sr_sem.at[index, part], at.sib, cond)

    for part in range(2):
        send(at.dp, part, zs_sem.at[0, 0, part], zr_sem.at[0, 1, part], at.up, at.has_up)
        send(at.dp, part, zs_sem.at[1, 0, part], zr_sem.at[1, 1, part], at.down, at.has_down)
        send(at.dp, part, xs_sem.at[at.z, part], xr_sem.at[at.z, part], at.xn)
        send(at.dp, part, ys_sem.at[at.z, part], yr_sem.at[at.z, part], at.yn)
        share(at.dp, part)

    def chain(dist):
        for part in range(2):
            for down in range(2):
                src = at.z + dist if down else at.z - dist
                ok = (src <= 3) if down else (src >= 0)
                src = jnp.clip(src, 0, 3)
                index = at.shard(src, at.y, at.x)
                dev = at.down if down else at.up
                onward = at.has_down if down else at.has_up
                wait(
                    index, part, zs_sem.at[down, 0, part], zr_sem.at[down, dist, part], dev, ok
                )
                if dist < 3:
                    send(
                        index,
                        part,
                        zs_sem.at[down, dist, part],
                        zr_sem.at[down, dist + 1, part],
                        dev,
                        ok & onward,
                    )
                send(index, part, xs_sem.at[src, part], xr_sem.at[src, part], at.xn, ok)
                send(index, part, ys_sem.at[src, part], yr_sem.at[src, part], at.yn, ok)
                share(index, part, ok)

    def sources(dist):
        if dist == 0:
            return [(at.z, None)]
        return [
            (jnp.clip(at.z - dist, 0, 3), at.z - dist >= 0),
            (jnp.clip(at.z + dist, 0, 3), at.z + dist <= 3),
        ]

    def plane(dist):
        for src, ok in sources(dist):
            for part in range(2):
                from_x = at.shard(src, at.y, 1 - at.x)
                from_y = at.shard(src, 1 - at.y, at.x)
                wait(from_x, part, xs_sem.at[src, part], xr_sem.at[src, part], at.xn, ok)
                if part == 0:
                    send(from_x, 0, ys_sem.at[src, 2], yr_sem.at[src, 2], at.yn, ok)
                share(from_x, part, ok)
                wait(from_y, part, ys_sem.at[src, part], yr_sem.at[src, part], at.yn, ok)
                if part == 1:
                    send(from_y, 1, xs_sem.at[src, 2], xr_sem.at[src, 2], at.xn, ok)
                share(from_y, part, ok)

    def diagonal(dist):
        for src, ok in sources(dist):
            index = at.shard(src, 1 - at.y, 1 - at.x)
            wait(index, 0, ys_sem.at[src, 2], yr_sem.at[src, 2], at.yn, ok)
            wait(index, 1, xs_sem.at[src, 2], xr_sem.at[src, 2], at.xn, ok)
            for part in range(2):
                share(index, part, ok)

    chain(1)
    plane(0)
    chain(2)
    plane(1)
    diagonal(0)
    chain(3)
    plane(2)
    diagonal(1)
    plane(3)
    diagonal(2)
    diagonal(3)
    for index in range(16):
        for part in range(2):
            piece = buf.at[1 - at.half, index, pl.ds(*halves[part])]
            pltpu.make_async_remote_copy(
                src_ref=piece,
                dst_ref=piece,
                send_sem=ss_sem.at[index, part],
                recv_sem=sr_sem.at[index, part],
                device_id=at.sib,
                device_id_type=MESH,
            ).wait_recv()
    for cond, work in sends:
        guarded(cond, work)


def gather_lines(lay, own):
    if lay.dp_count != 16:
        flat = own.reshape(-1)
        phase = (lax.axis_index("dp") * lay.shard) % LANES
        own = jnp.roll(flat, phase).reshape(lay.length, LANES).astype(jnp.bfloat16)
        gathered = lax.all_gather(own, ("mp", "dp"), axis=0, tiled=True)
        return gathered.reshape(MP, lay.dp_count, lay.length, LANES)
    return pl.pallas_call(
        partial(gather_kernel, lay),
        out_shape=jax.ShapeDtypeStruct((MP, 16, lay.length, LANES), jnp.bfloat16),
        in_specs=[pl.BlockSpec(memory_space=pltpu.VMEM)],
        out_specs=pl.BlockSpec(memory_space=pltpu.VMEM),
        scratch_shapes=[
            pltpu.VMEM((lay.length + 8, LANES), jnp.float32),
            DMA((2, 4, 2)),
            DMA((2, 4, 2)),
            DMA((4, 3)),
            DMA((4, 3)),
            DMA((4, 3)),
            DMA((4, 3)),
            DMA((16, 2)),
            DMA((16, 2)),
        ],
        compiler_params=pltpu.CompilerParams(
            collective_id=0, has_side_effects=True, vmem_limit_bytes=VMEM_LIMIT
        ),
        name="gather_lines",
    )(own)


def exchange_kernel(
    pooled_ref,
    codes_ref,
    labels_ref,
    grad_ref,
    pooled,
    outgoing,
    incoming,
    returning,
    arrived,
    sib_sem,
    go_send,
    go_recv,
    back_send,
    back_recv,
):
    dp = lax.axis_index("dp")
    half = lax.axis_index("mp")
    sib = (dp, 1 - half)
    slots, capacity, features = outgoing.shape
    codes = slots * capacity
    core_sents = pooled_ref.shape[0]

    def peer(step):
        return (lax.rem(dp + step, slots), half)

    bar = pltpu.get_barrier_semaphore()
    pl.semaphore_signal(bar, inc=1, device_id=sib, device_id_type=MESH)
    for step in range(1, slots):
        pl.semaphore_signal(bar, inc=1, device_id=peer(step), device_id_type=MESH)
    pooled[half] = pooled_ref[...]
    pl.semaphore_wait(bar, slots)
    share = pltpu.make_async_remote_copy(
        src_ref=pooled_ref,
        dst_ref=pooled.at[half],
        send_sem=sib_sem.at[0],
        recv_sem=sib_sem.at[1],
        device_id=sib,
        device_id_type=MESH,
    )
    share.start()

    code_ids = lax.broadcasted_iota(jnp.int32, (codes, codes), 0)
    send_map = (code_ids == codes_ref[0:1, :]).astype(jnp.bfloat16)
    pairs = codes // 2
    even_map = (code_ids[:, :pairs] == codes_ref[1:2, :pairs]).astype(jnp.bfloat16)
    odd_map = (code_ids[:, :pairs] == codes_ref[2:3, :pairs]).astype(jnp.bfloat16)
    share.wait()
    everything = jnp.concatenate([pooled[0], pooled[1]], 0)
    out = jnp.dot(send_map, everything, preferred_element_type=jnp.float32)
    outgoing[...] = out.reshape(outgoing.shape).astype(jnp.bfloat16)

    def copy(src, dst, send_sem, recv_sem, step):
        return pltpu.make_async_remote_copy(
            src_ref=src,
            dst_ref=dst,
            send_sem=send_sem.at[step],
            recv_sem=recv_sem.at[step],
            device_id=peer(step),
            device_id_type=MESH,
        )

    def all_to_all(src, dst, send_sem, recv_sem):
        for step in range(1, slots):
            copy(src.at[lax.rem(dp + step, slots)], dst.at[dp], send_sem, recv_sem, step).start()
        dst[dp] = src[dp]
        for step in range(1, slots):
            sender = lax.rem(dp + slots - step, slots)
            copy(src.at[sender], dst.at[sender], send_sem, recv_sem, step).wait()

    all_to_all(outgoing, incoming, go_send, go_recv)
    items = incoming[...].astype(jnp.float32).reshape(codes, features).astype(jnp.bfloat16)
    left = lax.dot_general(even_map, items, FIRST, preferred_element_type=jnp.float32)
    right = lax.dot_general(odd_map, items, FIRST, preferred_element_type=jnp.float32)
    inner = jnp.sum(left * right, -1, keepdims=True)
    left_inv = lax.rsqrt(jnp.sum(left * left, -1, keepdims=True) + 1e-06)
    right_inv = lax.rsqrt(jnp.sum(right * right, -1, keepdims=True) + 1e-06)
    both = left_inv * right_inv
    cosine = inner * both
    square = (pairs, pairs)
    eye = lax.broadcasted_iota(jnp.int32, square, 0) == lax.broadcasted_iota(
        jnp.int32, square, 1
    )
    target = jnp.sum(
        jnp.where(eye, labels_ref[0:1, :pairs].astype(jnp.float32), 0.0), 1, keepdims=True
    )
    slope = (2.0 * LOSS_SCALE) * (cosine - target / 5.0)
    left_grad = slope * (both * right - (cosine * left_inv * left_inv) * left)
    right_grad = slope * (both * left - (cosine * right_inv * right_inv) * right)
    back = jnp.dot(
        even_map, left_grad.astype(jnp.bfloat16), preferred_element_type=jnp.float32
    ) + jnp.dot(odd_map, right_grad.astype(jnp.bfloat16), preferred_element_type=jnp.float32)
    returning[...] = back.reshape(returning.shape).astype(jnp.bfloat16)
    all_to_all(returning, arrived, back_send, back_recv)
    items = arrived[...].astype(jnp.float32).reshape(codes, features).astype(jnp.bfloat16)
    grads = lax.dot_general(send_map, items, FIRST, preferred_element_type=jnp.float32)
    grad_ref[...] = jnp.where(half == 0, grads[:core_sents], grads[core_sents:])


def exchange(pooled_core, sentence_dest, pair_source, labels, dp_count, capacity):
    core_sents, features = pooled_core.shape
    codes = dp_count * capacity
    send_code = sentence_dest[:, 0] * capacity + sentence_dest[:, 1]
    take_code = pair_source[:, 0] * capacity + pair_source[:, 1]
    if dp_count == 16 and codes == send_code.shape[0] == 2 * core_sents:
        pairs = take_code.reshape(-1, 2).T
        pairs = jnp.pad(pairs, ((0, 0), (0, codes - pairs.shape[1])))
        table = jnp.concatenate([send_code[None], pairs, jnp.zeros((5, codes), jnp.int32)], 0)
        wide = (dp_count, capacity, features)
        low = jnp.bfloat16
        vmem = pl.BlockSpec(memory_space=pltpu.VMEM)
        return pl.pallas_call(
            exchange_kernel,
            out_shape=jax.ShapeDtypeStruct((core_sents, features), jnp.float32),
            in_specs=[vmem] * 3,
            out_specs=vmem,
            scratch_shapes=[pltpu.VMEM((MP, core_sents, features), low)]
            + [pltpu.VMEM(wide, low)] * 4
            + [DMA((2,))]
            + [DMA((dp_count,))] * 4,
            compiler_params=pltpu.CompilerParams(
                collective_id=2, has_side_effects=True, vmem_limit_bytes=VMEM_LIMIT
            ),
            name="exchange_pairs",
        )(pooled_core, table, labels[None])
    mp_index = lax.axis_index("mp")
    pooled_flat = lax.all_gather(pooled_core, "mp", axis=0, tiled=True)
    code_ids = jnp.arange(codes, dtype=jnp.int32)
    send_map = (code_ids[:, None] == send_code[None, :]).astype(jnp.bfloat16)
    outgoing = jnp.dot(send_map, pooled_flat, preferred_element_type=jnp.float32).astype(
        jnp.bfloat16
    )
    outgoing = outgoing.reshape(dp_count, capacity, features)
    incoming = lax.all_to_all(outgoing, "dp", split_axis=0, concat_axis=0, tiled=True).reshape(
        codes, features
    )
    take_map = (take_code[:, None] == code_ids[None, :]).astype(jnp.bfloat16)
    pair_items = jnp.dot(take_map, incoming, preferred_element_type=jnp.float32)
    item_grad = jax.grad(pair_loss)(pair_items, labels).astype(jnp.bfloat16)
    returning = jnp.dot(take_map.T, item_grad, preferred_element_type=jnp.float32).astype(
        jnp.bfloat16
    )
    returning = returning.reshape(dp_count, capacity, features)
    arrived = lax.all_to_all(returning, "dp", split_axis=0, concat_axis=0, tiled=True).reshape(
        codes, features
    )
    core_map = lax.dynamic_slice_in_dim(send_map, mp_index * core_sents, core_sents, 1)
    return jnp.dot(core_map.T, arrived, preferred_element_type=jnp.float32)


SCORE_SCALE = HEAD_DIM ** (-0.5)
LAST = (((1,), (1,)), ((), ()))
FIRST = (((0,), (0,)), ((), ()))


def low_lanes(rows):
    return lax.broadcasted_iota(jnp.int32, (rows, LANES), 1) < HEAD_DIM


def one_head(tile, odd):
    mask = low_lanes(tile.shape[0])
    if odd:
        return jnp.where(mask, jnp.zeros_like(tile), tile)
    return jnp.where(mask, tile, jnp.zeros_like(tile))


def attend_kernel(tiles, qkv_ref, seg_col_ref, seg_row_ref, out_ref, log_ref):
    width = tiles * LANES
    bias = jnp.where(seg_col_ref[...] == seg_row_ref[0], 0.0, -1e30)
    logs = []
    for tile in range(tiles):
        cols = slice(tile * LANES, (tile + 1) * LANES)
        queries = qkv_ref[:, cols] * SCORE_SCALE
        keys = qkv_ref[:, width + tile * LANES : width + (tile + 1) * LANES]
        values = qkv_ref[:, 2 * width + tile * LANES : 2 * width + (tile + 1) * LANES]
        mixed = []
        for odd in range(2):
            scores = lax.dot_general(
                one_head(queries, odd), keys, LAST, preferred_element_type=jnp.float32
            )
            scores = scores + bias
            row_max = jnp.max(scores, -1, keepdims=True)
            exponent = jnp.exp(scores - row_max)
            row_total = jnp.sum(exponent, -1, keepdims=True)
            probs = exponent.astype(jnp.bfloat16)
            mixed.append(
                jnp.dot(probs, values, preferred_element_type=jnp.float32) * (1.0 / row_total)
            )
            logs.append(row_max + jnp.log(row_total))
        both = jnp.where(low_lanes(ROW), mixed[0], mixed[1])
        out_ref[:, cols] = both.astype(jnp.bfloat16)
    log_ref[0] = jnp.concatenate(logs + [logs[0]] * (8 - 2 * tiles), 1)


def attend(qkv, seg_col, seg_row, head_cols):
    rows = qkv.shape[0] // ROW
    return pl.pallas_call(
        partial(attend_kernel, head_cols // LANES),
        grid=(rows, MP),
        in_specs=[
            pl.BlockSpec((ROW, 3 * head_cols), lambda r, m: (r, m)),
            pl.BlockSpec((ROW, 1), lambda r, m: (r, 0)),
            pl.BlockSpec((1, 1, ROW), lambda r, m: (r, 0, 0)),
        ],
        out_specs=[
            pl.BlockSpec((ROW, head_cols), lambda r, m: (r, m)),
            pl.BlockSpec((1, ROW, 8), lambda r, m: (m, r, 0)),
        ],
        out_shape=[
            jax.ShapeDtypeStruct((rows * ROW, MP * head_cols), jnp.bfloat16),
            jax.ShapeDtypeStruct((MP, rows * ROW, 8), jnp.float32),
        ],
        compiler_params=pltpu.CompilerParams(vmem_limit_bytes=VMEM_LIMIT),
        name="attend",
    )(qkv, seg_col, seg_row)


def attend_back_row(
    tiles, qkv_ref, grad_ref, log_ref, seg_col_ref, seg_wide_ref, out_ref, key_acc, value_acc
):
    width = tiles * LANES
    block, window = LANES, 2 * LANES
    key_acc[...] = jnp.zeros_like(key_acc)
    value_acc[...] = jnp.zeros_like(value_acc)
    for step in range(ROW // block):
        start = min(max(step * block - block // 2, 0), ROW - window)
        rows = slice(step * block, (step + 1) * block)
        span = slice(start, start + window)
        bias = jnp.where(seg_col_ref[rows, :] == seg_wide_ref[step], 0.0, -1e30)
        for tile in range(tiles):
            cols = slice(tile * LANES, (tile + 1) * LANES)
            queries = qkv_ref[rows, cols] * SCORE_SCALE
            keys = qkv_ref[span, width + tile * LANES : width + (tile + 1) * LANES]
            values = qkv_ref[span, 2 * width + tile * LANES : 2 * width + (tile + 1) * LANES]
            mixed_grad = grad_ref[rows, cols]
            query_grad = key_grad = value_grad = 0.0
            for odd in range(2):
                head = 2 * tile + odd
                query_one = one_head(queries, odd)
                grad_one = one_head(mixed_grad, odd)
                scores = lax.dot_general(
                    query_one, keys, LAST, preferred_element_type=jnp.float32
                )
                probs = jnp.exp((scores + bias) - log_ref[rows, head : head + 1])
                prob_grad = lax.dot_general(
                    grad_one, values, LAST, preferred_element_type=jnp.float32
                )
                row_inner = jnp.sum(prob_grad * probs, -1, keepdims=True)
                score_grad = (probs * (prob_grad - row_inner)).astype(jnp.bfloat16)
                value_grad += lax.dot_general(
                    probs.astype(jnp.bfloat16),
                    grad_one,
                    FIRST,
                    preferred_element_type=jnp.float32,
                )
                query_grad += jnp.dot(
                    score_grad, one_head(keys, odd), preferred_element_type=jnp.float32
                )
                key_grad += lax.dot_general(
                    score_grad, query_one, FIRST, preferred_element_type=jnp.float32
                )
            out_ref[rows, cols] = (query_grad * SCORE_SCALE).astype(jnp.bfloat16)
            key_acc[span, cols] += key_grad
            value_acc[span, cols] += value_grad
    out_ref[:, width : 2 * width] = key_acc[...].astype(jnp.bfloat16)
    out_ref[:, 2 * width :] = value_acc[...].astype(jnp.bfloat16)


def attend_back_kernel(
    tiles, qkv_ref, grad_ref, log_ref, seg_col_ref, seg_wide_ref, out_ref, key_acc, value_acc
):
    attend_back_row(
        tiles,
        qkv_ref,
        grad_ref,
        log_ref.at[0],
        seg_col_ref,
        seg_wide_ref.at[0],
        out_ref,
        key_acc,
        value_acc,
    )


def window_segments(seg_row):
    window = 2 * LANES
    starts = [
        min(max(step * LANES - LANES // 2, 0), ROW - window) for step in range(ROW // LANES)
    ]
    return jnp.stack([seg_row[:, :, start : start + window] for start in starts], 1)


def attend_back(qkv, mixed_grad, logs, seg_col, seg_row, head_cols):
    rows = qkv.shape[0] // ROW
    window = 2 * LANES
    seg_wide = window_segments(seg_row)
    return pl.pallas_call(
        partial(attend_back_kernel, head_cols // LANES),
        grid=(rows, MP),
        in_specs=[
            pl.BlockSpec((ROW, 3 * head_cols), lambda r, m: (r, m)),
            pl.BlockSpec((ROW, head_cols), lambda r, m: (r, m)),
            pl.BlockSpec((1, ROW, 8), lambda r, m: (m, r, 0)),
            pl.BlockSpec((ROW, 1), lambda r, m: (r, 0)),
            pl.BlockSpec((1, ROW // LANES, 1, window), lambda r, m: (r, 0, 0, 0)),
        ],
        out_specs=pl.BlockSpec((ROW, 3 * head_cols), lambda r, m: (r, m)),
        out_shape=jax.ShapeDtypeStruct(qkv.shape, jnp.bfloat16),
        scratch_shapes=[pltpu.VMEM((ROW, head_cols), jnp.float32)] * 2,
        compiler_params=pltpu.CompilerParams(vmem_limit_bytes=VMEM_LIMIT),
        name="attend_back",
    )(qkv, mixed_grad, logs, seg_col, seg_wide)


STAT_ROWS = 8
EXTRA = 6
SPLIT = 6


def finish_kernel(
    lay,
    in_hbm,
    out_hbm,
    attn_hbm,
    qkv_hbm,
    mixed_hbm,
    tokens_hbm,
    weight_hbm,
    resid_hbm,
    logs_ref,
    seg_col_ref,
    seg_wide_ref,
    extra_ref,
    grad_ref,
    norm_ref,
    shared_ref,
    input_hbm,
    staged_in,
    staged_out,
    flat,
    part,
    from_sib,
    from_x,
    from_y,
    diag_x,
    diag_y,
    from_z,
    total,
    stats,
    extras,
    tail,
    qkv,
    mixed,
    tokens,
    qkv_grad,
    key_acc,
    value_acc,
    weight,
    resid,
    load_sem,
    row_sem,
    ss_sem,
    sr_sem,
    xs_sem,
    xr_sem,
    ys_sem,
    yr_sem,
    dx_sem,
    dy_sem,
    zs_sem,
    zr_sem,
    bs_sem,
    br_sem,
):
    at = Place()
    other_half = 1 - at.half
    width = 3 * lay.head_cols
    ffn_start = lay.mats[2][0]

    def load_in(half):
        cols = pl.ds(pl.multiple_of(half * lay.ffn_cols, LANES), lay.ffn_cols)
        return pltpu.make_async_copy(in_hbm.at[:, cols], staged_in, load_sem.at[0])

    def load_out(half):
        rows = pl.ds(pl.multiple_of(half * lay.ffn_cols, LANES), lay.ffn_cols)
        return pltpu.make_async_copy(out_hbm.at[rows, :], staged_out, load_sem.at[1])

    attn_space = staged_out.at[pl.ds(0, lay.head_cols)]
    head_space = staged_in.at[pl.ds(0, LANES)]

    def load_attn(half):
        rows = pl.ds(pl.multiple_of(half * lay.head_cols, LANES), lay.head_cols)
        return pltpu.make_async_copy(attn_hbm.at[rows, :], attn_space, load_sem.at[1])

    def load_head(half):
        cols = pl.ds(pl.multiple_of(half * lay.ffn_cols, LANES), lay.ffn_cols)
        return pltpu.make_async_copy(
            in_hbm.at[pl.ds(0, LANES), cols], head_space, load_sem.at[0]
        )

    def load_row(row):
        rows = pl.ds(row * ROW, ROW)
        return [
            pltpu.make_async_copy(qkv_hbm.at[rows, :], qkv, row_sem.at[0]),
            pltpu.make_async_copy(mixed_hbm.at[rows, :], mixed, row_sem.at[1]),
        ]

    load_tokens = pltpu.make_async_copy(tokens_hbm, tokens, row_sem.at[2])

    def load_back(chunk):
        cols = pl.ds(chunk * 2 * LANES, 2 * LANES)
        return [
            pltpu.make_async_copy(weight_hbm.at[cols, :], weight, row_sem.at[3]),
            pltpu.make_async_copy(resid_hbm.at[:, cols], resid, row_sem.at[4]),
        ]

    def store_back(chunk):
        cols = pl.ds(chunk * 2 * LANES, 2 * LANES)
        return pltpu.make_async_copy(resid, input_hbm.at[:, cols], row_sem.at[5])

    load_in(other_half).start()
    load_out(other_half).start()
    for copy in load_row(0):
        copy.start()
    load_tokens.start()

    bar = pltpu.get_barrier_semaphore()
    me = at.dp * MP + at.half
    count = 16 * MP

    def peer(step):
        other = lax.rem(me + step, count)
        return (other // MP, lax.rem(other, MP))

    def greet(step, carry):
        pl.semaphore_signal(bar, inc=1, device_id=peer(step), device_id_type=MESH)
        return carry

    lax.fori_loop(1, count, greet, 0)
    sends = []

    def remote(src, dst, send_sem, recv_sem, dev):
        return pltpu.make_async_remote_copy(
            src_ref=src,
            dst_ref=dst,
            send_sem=send_sem,
            recv_sem=recv_sem,
            device_id=dev,
            device_id_type=MESH,
        )

    def later(cond, copy):
        sends.append((cond, lambda: copy().wait_send()))

    def lay_out(ref, offset, height, cols, base):
        def body(step, carry):
            row = pl.multiple_of(step * LANES, LANES)
            for col in range(cols):
                block = ref[pl.ds(row, LANES), col * LANES : (col + 1) * LANES]
                flat[pl.ds(offset - base + row * cols + col, LANES, stride=cols), :] = (
                    block.astype(jnp.float32)
                )
            return carry

        lax.fori_loop(0, height // LANES, body, 0)

    tail_from = lay.need // 16 * 16
    spare = lay.need - tail_from

    def emit(half, index, base):
        start = lay.starts[index] - base
        if index >= SPLIT:
            part[half, index] = flat[start : start + lay.length, :].astype(jnp.bfloat16)
            return
        part[half, index, :tail_from] = flat[start : start + tail_from, :].astype(jnp.bfloat16)
        tail[0:spare, :] = flat[start + tail_from : start + lay.need, :]
        tail[spare : spare + EXTRA, :] = extras[half, EXTRA * index : EXTRA * (index + 1), :]
        part[half, index, tail_from : tail_from + 16] = tail[...].astype(jnp.bfloat16)
        part[half, index, tail_from + 16 :] = jnp.zeros(
            (lay.length - tail_from - 16, LANES), jnp.bfloat16
        )

    def to_sib(index):
        return remote(
            part.at[other_half, index],
            from_sib.at[index],
            ss_sem.at[index],
            sr_sem.at[index],
            at.sib,
        )

    def emit_all(half, indices, base, share):
        for index in indices:
            emit(half, index, base)
            if share:
                to_sib(index).start()
                later(None, lambda index=index: to_sib(index))

    early = list(range(12, 16)) + list(range(8, 12)) + list(range(SPLIT, 8))
    late = list(range(SPLIT))
    tail[...] = jnp.zeros_like(tail)
    rows = flat.shape[0] - (lay.bias_start - ffn_start)
    for half, share in ((other_half, True), (at.half, False)):
        load_in(half).wait()
        lay_out(staged_in, *lay.mats[2], ffn_start)
        if share:
            load_in(at.half).start()
        load_out(half).wait()
        lay_out(staged_out, *lay.mats[3], ffn_start)
        if share:
            load_out(at.half).start()
            pl.semaphore_wait(bar, count - 1)
        flat[lay.bias_start - ffn_start :, :] = jnp.zeros((rows, LANES), jnp.float32)
        emit_all(half, early, ffn_start, share)
    load_head(other_half).start()
    load_attn(other_half).start()

    my_part = part.at[at.half]

    def wait_sib(index):
        to_sib(index).wait_recv()

    def wide(ref, rows):
        return ref[rows, :].astype(jnp.float32)

    def add_span(dst, terms, begin, size):
        def body(step, carry):
            off = step * lay.step
            spans = [
                pl.ds(pl.multiple_of(first + off, 16), lay.step) for _, first in terms
            ]
            value = wide(terms[0][0], spans[0])
            for (ref, _), span in zip(terms[1:], spans[1:]):
                value = value + wide(ref, span)
            dst[pl.ds(pl.multiple_of(begin + off, 16), lay.step), :] = value.astype(dst.dtype)
            return carry

        lax.fori_loop(0, size // lay.step, body, 0)

    def active(phase, z, y):
        if z == 1:
            return y == (1 if phase == 1 else 0)
        return None

    def both(cond, other):
        return other if cond is None else cond & other

    def diag_out(z, index, axis):
        mine = my_part.at[index]
        if axis == 0:
            return remote(
                mine.at[pl.ds(0, lay.cut)], diag_y.at[z], dy_sem.at[z, 0], dy_sem.at[z, 1], at.yn
            )
        return remote(
            mine.at[pl.ds(lay.cut, lay.cut)],
            diag_x.at[z],
            dx_sem.at[z, 0],
            dx_sem.at[z, 1],
            at.xn,
        )

    def diagonal(phase, z):
        index = at.shard(z, 1 - at.y, 1 - at.x)
        cond = active(phase, z, 1 - at.y)

        def work():
            wait_sib(index)
            mine = my_part.at[index]
            add_span(mine, [(mine, 0), (from_sib.at[index], 0)], 0, lay.length)
            diag_out(z, index, 0).start()
            diag_out(z, index, 1).start()

        guarded(cond, work)
        later(cond, lambda: diag_out(z, index, 0))
        later(cond, lambda: diag_out(z, index, 1))

    def plane_out(z, index, piece, to_y):
        rows = pl.ds(piece * lay.piece, lay.piece)
        if to_y:
            return remote(
                my_part.at[index, rows],
                from_y.at[z, rows],
                ys_sem.at[z, piece],
                yr_sem.at[z, piece],
                at.yn,
            )
        return remote(
            my_part.at[index, rows],
            from_x.at[z, rows],
            xs_sem.at[z, piece],
            xr_sem.at[z, piece],
            at.xn,
        )

    def plane(phase, z):
        for to_y in range(2):
            y = 1 - at.y if to_y else at.y
            x = at.x if to_y else 1 - at.x
            index = at.shard(z, y, x)
            cond = active(phase, z, y)

            def work(index=index, to_y=to_y):
                mine, sib = my_part.at[index], from_sib.at[index]
                wait_sib(index)
                diag_out(z, index, 1 if to_y else 0).wait_recv()
                for piece in range(PIECES):
                    begin = piece * lay.piece
                    terms = [(mine, begin), (sib, begin)]
                    if to_y and begin >= lay.cut:
                        terms.append((diag_x.at[z], begin - lay.cut))
                    if not to_y and begin < lay.cut:
                        terms.append((diag_y.at[z], begin))
                    add_span(mine, terms, begin, lay.piece)
                    plane_out(z, index, piece, to_y).start()

            guarded(cond, work)
            for piece in range(PIECES):
                later(
                    cond,
                    lambda index=index, piece=piece, to_y=to_y: plane_out(
                        z, index, piece, to_y
                    ),
                )

    def chain_out(z, index, piece, dev, slot):
        rows = pl.ds(piece * lay.piece, lay.piece)
        return remote(
            my_part.at[index, rows],
            from_z.at[slot, rows],
            zs_sem.at[z, piece],
            zr_sem.at[slot, piece],
            dev,
        )

    def chain_in(slot, piece):
        return chain_out(0, at.dp, piece, at.sib, slot)

    def gather_terms(z, index, piece):
        plane_out(z, index, piece, 0).wait_recv()
        plane_out(z, index, piece, 1).wait_recv()
        begin = piece * lay.piece
        return [
            (my_part.at[index], begin),
            (from_sib.at[index], begin),
            (from_x.at[z], begin),
            (from_y.at[z], begin),
        ]

    def chain(phase, z, hop):
        index = at.shard(z, at.y, at.x)
        for down in range(2):
            spot = 3 - hop if down else hop
            if (spot <= z) if down else (spot >= z):
                continue
            dev = at.down if down else at.up
            slot = 4 if down and spot - 1 == z else z
            cond = both(active(phase, z, at.y), at.z == spot)

            def work(dev=dev, slot=slot):
                wait_sib(index)
                for piece in range(PIECES):
                    terms = gather_terms(z, index, piece)
                    begin = piece * lay.piece
                    if hop > 0:
                        chain_in(z, piece).wait_recv()
                        terms.append((from_z.at[z], begin))
                    add_span(my_part.at[index], terms, begin, lay.piece)
                    chain_out(z, index, piece, dev, slot).start()

            guarded(cond, work)
            for piece in range(PIECES):
                later(
                    cond,
                    lambda piece=piece, dev=dev, slot=slot: chain_out(
                        z, index, piece, dev, slot
                    ),
                )

    tiles = lay.head_cols // LANES

    def attention(row, half):
        cols = pl.ds(half * width, width)
        attend_back_row(
            tiles,
            qkv.at[:, cols],
            mixed.at[:, pl.ds(half * lay.head_cols, lay.head_cols)],
            logs_ref.at[half, pl.ds(row * ROW, ROW)],
            seg_col_ref.at[pl.ds(row * ROW, ROW)],
            seg_wide_ref.at[row],
            qkv_grad.at[pl.ds(row * ROW, ROW), cols],
            key_acc,
            value_acc,
        )

    core_rows = qkv_grad.shape[0]

    def weights(half, share):
        ones = jnp.ones((16, core_rows), jnp.bfloat16)
        for section in range(3):
            cols = pl.ds(
                pl.multiple_of(half * width + section * lay.head_cols, LANES), lay.head_cols
            )
            grads = qkv_grad[:, cols]
            result = jnp.dot(tokens[...], grads, preferred_element_type=jnp.float32)
            for tile in range(tiles):
                flat[pl.ds(section * tiles + tile, lay.features, stride=3 * tiles), :] = (
                    result[:, tile * LANES : (tile + 1) * LANES]
                )
            if section != 1:
                sums = jnp.dot(ones, grads, preferred_element_type=jnp.float32)
                first = 0 if section == 0 else tiles
                for tile in range(tiles):
                    extras[half, first + tile : first + tile + 1, :] = sums[
                        0:1, tile * LANES : (tile + 1) * LANES
                    ]
        load_attn(half).wait()
        lay_out(attn_space, *lay.mats[1], 0)
        load_head(half).wait()
        lay_out(head_space, lay.mats[2][0], LANES, lay.mats[2][2], 0)
        if share:
            load_attn(at.half).start()
            load_head(at.half).start()
        emit_all(half, late, 0, share)

    def back(chunk):
        for copy in load_back(chunk):
            copy.wait()
        for row in range(core_rows // ROW):
            rows = pl.ds(row * ROW, ROW)
            resid[rows, :] += lax.dot_general(
                qkv_grad[rows, :], weight[...], LAST, preferred_element_type=jnp.float32
            )
        store_back(chunk).start()

    extras[...] = extra_ref[...]
    for z in (3, 2, 1):
        diagonal(1, z)
    for copy in load_row(0):
        copy.wait()
    attention(0, 0)
    plane(1, 3)
    attention(0, 1)
    for copy in load_row(1):
        copy.start()
    plane(1, 2)
    for copy in load_row(1):
        copy.wait()
    attention(1, 0)
    plane(1, 1)
    chain(1, 3, 0)
    attention(1, 1)
    load_tokens.wait()
    chain(1, 3, 1)
    chain(1, 2, 0)
    weights(other_half, True)
    chain(1, 3, 2)
    chain(1, 2, 1)
    chain(1, 1, 0)
    weights(at.half, False)
    chain(1, 1, 1)
    for copy in load_back(0):
        copy.start()
    diagonal(2, 0)
    diagonal(2, 1)
    back(0)
    plane(2, 0)
    plane(2, 1)
    store_back(0).wait()
    for copy in load_back(1):
        copy.start()
    chain(2, 0, 0)
    back(1)
    chain(2, 0, 1)
    chain(2, 1, 0)
    store_back(1).wait()
    for copy in load_back(2):
        copy.start()
    chain(2, 0, 2)
    chain(2, 1, 1)
    back(2)

    index = at.dp
    wait_sib(index)
    for piece in range(PIECES):
        begin = piece * lay.piece
        add_span(total, gather_terms(at.z, index, piece), begin, lay.piece)
    for down in range(2):
        slot = 4 if down else at.z

        @pl.when((at.z < 3) if down else (at.z > 0))
        def _(slot=slot):
            for piece in range(PIECES):
                chain_in(slot, piece).wait_recv()
                begin = piece * lay.piece
                add_span(total, [(total, begin), (from_z.at[slot], begin)], begin, lay.piece)

    scale = 1.0 / LOSS_SCALE
    phase = lax.rem(lax.axis_index("dp") * lay.shard, LANES)
    keep = lay.length - 8
    lanes = lane_ids(keep)
    spots = lax.broadcasted_iota(jnp.int32, (keep, LANES), 0) * LANES + lanes - phase
    lines = jnp.where((spots >= 0) & (spots < lay.shard), total[:keep, :] * scale, 0.0)
    extra = total[lay.need : lay.need + EXTRA, :] * scale
    stats[me] = jnp.zeros((STAT_ROWS, LANES), jnp.float32)
    stats[me, 0:1] = jnp.sum(lines * lines, 0, keepdims=True)
    stats[me, 1 : 1 + EXTRA] = jnp.where(at.dp < SPLIT, extra, 0.0)

    def tell(step):
        return remote(stats.at[me], stats.at[me], bs_sem.at[step], br_sem.at[step], peer(step))

    def hear(step):
        other = lax.rem(me + count - step, count)
        return remote(
            stats.at[other], stats.at[other], bs_sem.at[step], br_sem.at[step], peer(step)
        )

    def start_tell(step, carry):
        tell(step).start()
        return carry

    def finish(step, carry):
        hear(step).wait_recv()
        tell(step).wait_send()
        return carry

    lax.fori_loop(1, count, start_tell, 0)
    store_back(2).wait()
    for cond, work in sends:
        guarded(cond, work)
    lax.fori_loop(1, count, finish, 0)
    everyone = stats[...]
    squares = jnp.sum(everyone[:, 0])
    for row in range(EXTRA):
        squares = squares + jnp.sum(everyone[:, 1 + row] * everyone[:, 1 + row])
    norm_ref[...] = jnp.full((1, LANES), squares, jnp.float32)

    def extra_line(half, place):
        return stats.at[(place // EXTRA) * MP + half, pl.ds(1 + place % EXTRA, 1)]

    across = lay.features // LANES
    lines_half = 6 * across // MP
    for line in range(6 * across):
        half, place = line // lines_half, line % lines_half
        row, col = line // across, line % across
        shared_ref[row : row + 1, col * LANES : (col + 1) * LANES] = extra_line(
            half, lay.bias_lines + place
        )[...]

    @pl.when(at.dp == 15)
    def _():
        first = lay.bias_start - lay.starts[15]
        for place in range(lay.bias_lines):
            total[first + place : first + place + 1, :] = (
                extra_line(at.half, place)[...] * LOSS_SCALE
            )

    back_shift = lax.rem(LANES - phase, LANES)
    total[...] = pltpu.roll(total[...] * scale, back_shift, 1)
    grad_ref[:keep, :] = jnp.where(
        lanes < LANES - phase, total[:keep, :], total[1 : keep + 1, :]
    )
    grad_ref[keep:, :] = jnp.zeros((8, LANES), jnp.float32)


def finish_step(
    lay,
    ffn_grads,
    w_attn_grad,
    qkv,
    mixed_grad,
    tokens_turned,
    w_qkv,
    resid_grad,
    logs,
    seg_col,
    seg_row,
    in_sums,
    shared_step,
):
    across = lay.features // LANES
    lines_half = 6 * across // MP
    assert lay.starts[SPLIT] >= lay.mats[2][0] > lay.starts[SPLIT - 1]
    assert lay.starts[SPLIT - 1] + lay.length <= lay.mats[2][0] + LANES * lay.mats[2][2]
    assert lay.bias_lines + lines_half == SPLIT * EXTRA
    assert lay.need % 16 + EXTRA <= 16 and lay.length * LANES - lay.shard >= 8 * LANES
    heads = 2 * lay.head_cols // LANES
    extra = jnp.concatenate(
        [
            jnp.zeros((MP, heads, LANES), jnp.float32),
            in_sums.reshape(MP, -1, LANES),
            shared_step.reshape(MP, lines_half, LANES),
            jnp.zeros((MP, 40 - SPLIT * EXTRA, LANES), jnp.float32),
        ],
        1,
    )
    flat_rows = -(-(lay.starts[15] + lay.length - lay.mats[2][0]) // 8) * 8
    core_rows = qkv.shape[0]
    size = (lay.length, LANES)
    low, full = jnp.bfloat16, jnp.float32
    vmem = pl.BlockSpec(memory_space=pltpu.VMEM)
    anywhere = pl.BlockSpec(memory_space=pl.ANY)
    scratch = pltpu.VMEM
    lines, squares, shared_grad, input_core = pl.pallas_call(
        partial(finish_kernel, lay),
        out_shape=[
            jax.ShapeDtypeStruct(size, full),
            jax.ShapeDtypeStruct((1, LANES), full),
            jax.ShapeDtypeStruct(shared_step.shape, full),
            jax.ShapeDtypeStruct(resid_grad.shape, full),
        ],
        in_specs=[anywhere] * 8 + [vmem] * 4,
        out_specs=[vmem] * 3 + [anywhere],
        scratch_shapes=[
            scratch((lay.features, lay.ffn_cols), low),
            scratch((lay.ffn_cols, lay.features), low),
            scratch((flat_rows, LANES), full),
            scratch((MP, 16) + size, low),
            scratch((16,) + size, low),
            scratch((4,) + size, low),
            scratch((4,) + size, low),
            scratch((4, lay.cut, LANES), low),
            scratch((4, lay.cut, LANES), low),
            scratch((5,) + size, low),
            scratch(size, full),
            scratch((16 * MP, STAT_ROWS, LANES), full),
            scratch((MP, 40, LANES), full),
            scratch((16, LANES), full),
            scratch((ROW, qkv.shape[1]), low),
            scratch((ROW, lay.features), low),
            scratch((lay.features, core_rows), low),
            scratch(qkv.shape, low),
            scratch((ROW, lay.head_cols), full),
            scratch((ROW, lay.head_cols), full),
            scratch((2 * LANES, qkv.shape[1]), low),
            scratch((core_rows, 2 * LANES), full),
            DMA((2,)),
            DMA((6,)),
            DMA((16,)),
            DMA((16,)),
            DMA((4, PIECES)),
            DMA((4, PIECES)),
            DMA((4, PIECES)),
            DMA((4, PIECES)),
            DMA((4, 2)),
            DMA((4, 2)),
            DMA((4, PIECES)),
            DMA((5, PIECES)),
            DMA((16 * MP,)),
            DMA((16 * MP,)),
        ],
        compiler_params=pltpu.CompilerParams(
            collective_id=1, has_side_effects=True, vmem_limit_bytes=VMEM_MOST
        ),
        name="finish_step",
    )(
        *ffn_grads,
        w_attn_grad,
        qkv,
        mixed_grad,
        tokens_turned,
        w_qkv,
        resid_grad,
        logs,
        seg_col,
        window_segments(seg_row),
        extra,
    )
    return input_core, lines.reshape(1, -1), squares[0, 0], shared_grad


def scatter_gradients(lay, grads, bias_grad, shared_step):
    phase = (lax.axis_index("dp") * lay.shard) % LANES
    packed = pack_gradients(lay, grads, bias_grad)
    flat = packed.reshape(MP * lay.dp_count * lay.length, LANES)
    lines = lax.psum_scatter(flat, ("mp", "dp"), scatter_dimension=0, tiled=True)
    lines = lines.astype(jnp.float32).reshape(-1) / LOSS_SCALE
    lines = jnp.roll(lines, -phase)
    lines = jnp.where(jnp.arange(lines.size) < lay.shard, lines, 0.0)
    shared_grad = lax.psum(shared_step, ("dp", "mp")) / LOSS_SCALE
    squares = lax.psum(jnp.sum(lines * lines), ("dp", "mp"))
    squares = squares + jnp.sum(shared_grad * shared_grad)
    return lines.reshape(1, -1), squares, shared_grad


def back_norm(values_in, scale_vec, grad):
    center = jnp.mean(values_in, -1, keepdims=True)
    centered = values_in - center
    inverse = lax.rsqrt(jnp.mean(centered * centered, -1, keepdims=True) + NORM_EPS)
    unit = centered * inverse
    scaled = grad * scale_vec
    out = inverse * (
        scaled
        - jnp.mean(scaled, -1, keepdims=True)
        - unit * jnp.mean(scaled * unit, -1, keepdims=True)
    )
    return out, jnp.sum(grad * unit, 0), jnp.sum(grad, 0)


def per_device(
    tokens,
    segments,
    sentence_dest,
    pair_source,
    labels,
    params,
    first,
    second,
    shared,
    shared_first,
    shared_second,
):
    features = tokens.shape[1]
    dp_count = lax.axis_size("dp")
    dp_index = lax.axis_index("dp")
    mp_index = lax.axis_index("mp")
    shard = params.shape[1]
    lay = Layout(features, shard, dp_count)
    head_cols = lay.head_cols
    sent_slots = ROWS_DEV * SEG
    slot_capacity = max(2, sent_slots // dp_count)
    params_total = MP * shard * dp_count + 6 * features
    core_rows = ROWS_CORE * ROW

    own = jnp.pad(params, ((0, 0), (0, lay.length * LANES - shard))).reshape(lay.length, LANES)
    w_qkv, w_attn, w_in, w_out, biases = unpack_weights(lay, gather_lines(lay, own))
    head_lines = head_cols // LANES
    b_query = biases[:, :head_lines].reshape(MP, head_cols)
    b_value = biases[:, head_lines : 2 * head_lines].reshape(MP, head_cols)
    b_in = biases[:, 2 * head_lines : lay.bias_lines].reshape(MP * lay.ffn_cols)
    b_qkv = jnp.concatenate([b_query, jnp.zeros_like(b_query), b_value], 1).reshape(-1)

    tokens_core = lax.dynamic_slice_in_dim(tokens, mp_index * core_rows, core_rows, 0)
    segments_core = lax.dynamic_slice_in_dim(segments, mp_index * core_rows, core_rows, 0)
    seg_col = segments_core.reshape(core_rows, 1)
    seg_row = segments_core.reshape(ROWS_CORE, 1, ROW)

    qkv = (jnp.dot(tokens_core, w_qkv, preferred_element_type=jnp.float32) + b_qkv).astype(
        jnp.bfloat16
    )
    mixed, logs = attend(qkv, seg_col, seg_row, head_cols)
    attn_out = jnp.dot(mixed, w_attn, preferred_element_type=jnp.float32) + shared[4]
    resid_one = tokens_core.astype(jnp.float32) + attn_out
    hidden = normalize(resid_one, shared[0], shared[1])
    hidden_low = hidden.astype(jnp.bfloat16)
    up_proj = jnp.dot(hidden_low, w_in, preferred_element_type=jnp.float32) + b_in
    cdf = 0.5 * (1.0 + lax.erf(up_proj * (0.5**0.5)))
    activated = (up_proj * cdf).astype(jnp.bfloat16)
    slope = (
        cdf + up_proj * jnp.exp(-0.5 * up_proj * up_proj) * ((2.0 * math.pi) ** -0.5)
    ).astype(jnp.bfloat16)
    ffn_out = jnp.dot(activated, w_out, preferred_element_type=jnp.float32) + shared[5]
    resid_two = hidden + ffn_out
    encoded_core = normalize(resid_two, shared[2], shared[3])
    encoded = lax.all_gather(encoded_core.astype(jnp.bfloat16), "mp", axis=0, tiled=True)

    slot_ids = jnp.arange(SEG, dtype=jnp.int32)
    onehot = (seg_row == slot_ids[None, :, None]).astype(jnp.float32)
    weight = onehot / jnp.sum(onehot, 2, keepdims=True)
    pooled_core = jnp.einsum(
        "kvf,kfo->kvo",
        weight,
        encoded_core.reshape(ROWS_CORE, ROW, features),
        precision=TOP_PRECISION,
    ).astype(jnp.bfloat16)
    pooled_grad = exchange(
        pooled_core.reshape(ROWS_CORE * SEG, features),
        sentence_dest,
        pair_source,
        labels,
        dp_count,
        slot_capacity,
    )

    encoded_grad = jnp.einsum(
        "jix,jip->jxp",
        weight,
        pooled_grad.reshape(ROWS_CORE, SEG, features),
        precision=TOP_PRECISION,
    ).reshape(core_rows, features)
    resid_two_grad, scale_two, shift_two = back_norm(resid_two, shared[2], encoded_grad)
    ffn_grad = resid_two_grad.astype(jnp.bfloat16)
    act_grad = lax.dot_general(ffn_grad, w_out, LAST, preferred_element_type=jnp.float32)
    up_grad = (act_grad * slope.astype(jnp.float32)).astype(jnp.bfloat16)
    w_out_grad = lax.dot_general(activated, ffn_grad, FIRST, preferred_element_type=jnp.float32)
    w_in_grad = lax.dot_general(hidden_low, up_grad, FIRST, preferred_element_type=jnp.float32)
    hidden_term = lax.dot_general(up_grad, w_in, LAST, preferred_element_type=jnp.float32)
    hidden_grad = resid_two_grad + hidden_term
    resid_one_grad, scale_one, shift_one = back_norm(resid_one, shared[0], hidden_grad)
    attn_grad = resid_one_grad.astype(jnp.bfloat16)
    w_attn_grad = lax.dot_general(mixed, attn_grad, FIRST, preferred_element_type=jnp.float32)
    mixed_grad = lax.dot_general(
        attn_grad, w_attn, LAST, preferred_element_type=jnp.float32
    ).astype(jnp.bfloat16)
    in_sums = jnp.sum(up_grad.astype(jnp.float32), 0)
    shared_step = jnp.stack(
        [
            scale_one,
            shift_one,
            scale_two,
            shift_two,
            jnp.sum(attn_grad.astype(jnp.float32), 0),
            jnp.sum(ffn_grad.astype(jnp.float32), 0),
        ]
    )
    ffn_grads = [w_in_grad.astype(jnp.bfloat16), w_out_grad.astype(jnp.bfloat16)]
    w_attn_grad = w_attn_grad.astype(jnp.bfloat16)
    if dp_count == 16:
        input_core, grad_lines, total_squares, shared_grad = finish_step(
            lay,
            ffn_grads,
            w_attn_grad,
            qkv,
            mixed_grad,
            tokens_core.T,
            w_qkv,
            resid_one_grad,
            logs,
            seg_col,
            seg_row,
            in_sums,
            shared_step,
        )
    else:
        qkv_grad = attend_back(qkv, mixed_grad, logs, seg_col, seg_row, head_cols)
        w_qkv_grad = lax.dot_general(
            tokens_core, qkv_grad, FIRST, preferred_element_type=jnp.float32
        ).astype(jnp.bfloat16)
        input_term = lax.dot_general(qkv_grad, w_qkv, LAST, preferred_element_type=jnp.float32)
        input_core = resid_one_grad + input_term
        qkv_sums = jnp.sum(qkv_grad.astype(jnp.float32), 0).reshape(MP, 3, head_lines, LANES)
        bias_grad = jnp.concatenate(
            [qkv_sums[:, 0], qkv_sums[:, 2], in_sums.reshape(MP, -1, LANES)], 1
        )
        bias_grad = jnp.pad(bias_grad, ((0, 0), (0, lay.bias_rows - lay.bias_lines), (0, 0)))
        grad_lines, total_squares, shared_grad = scatter_gradients(
            lay, [w_qkv_grad, w_attn_grad] + ffn_grads, bias_grad, shared_step
        )
    input_grad = lax.all_gather(input_core, "mp", axis=0, tiled=True)
    flat_grad = grad_lines[:, :shard]
    norm_value = jnp.sqrt(total_squares)
    factor = jnp.minimum(1.0, CLIP_NORM / norm_value)
    step_count = STEP_COUNT
    params_new, first_new, second_new = adamw(
        params, first, second, flat_grad, factor, step_count, LEARN_RATE
    )
    shared_new, shared_first_new, shared_second_new = adamw(
        shared, shared_first, shared_second, shared_grad, factor, step_count, SHARED_RATE
    )
    grad_unit = math.sqrt(params_total) / CLIP_NORM
    params_grad = flat_grad * factor * grad_unit
    shared_grad_out = shared_grad * factor * grad_unit
    return (
        encoded,
        input_grad,
        norm_value.reshape(1),
        params_new,
        first_new,
        second_new,
        params_new.astype(jnp.bfloat16),
        shared_new,
        shared_first_new,
        shared_second_new,
        params_grad,
        shared_grad_out,
    )


def solution(mesh):
    in_specs = (
        P("dp", None),
        P("dp"),
        P("dp", None),
        P("dp", None),
        P("dp"),
        P("mp", "dp"),
        P("mp", "dp"),
        P("mp", "dp"),
        P(),
        P(),
        P(),
    )
    out_specs = (
        P("dp", None),
        P("dp", None),
        P(),
        P("mp", "dp"),
        P("mp", "dp"),
        P("mp", "dp"),
        P("mp", "dp"),
        P(),
        P(),
        P(),
        P("mp", "dp"),
        P(),
    )
    return jax.shard_map(
        per_device, mesh=mesh, in_specs=in_specs, out_specs=out_specs, check_vma=False
    )
```

```python
from functools import partial
import math

import jax
import jax.numpy as jnp
from jax import lax
from jax.experimental import pallas as pl
from jax.experimental.pallas import tpu as pltpu
from jax.sharding import PartitionSpec as P

HEAD_DIM = 64
FF = 3072
ROW = 512
SEG = 32
RPM = 2
MB = 2
MP = 2
LANES = 128
ROWS_DEV = MB * RPM
ROWS_CORE = ROWS_DEV // MP


LOSS_SCALE = 1024.0
CLIP_NORM = 0.5
LEARN_RATE = 0.1
SHARED_RATE = 0.5
BETA_ONE = 0.9
BETA_TWO = 0.999
ADAM_EPS = 1e-08
DECAY = 0.01
NORM_EPS = 1e-12
STEP_COUNT = 10.0
TOP_PRECISION = lax.Precision.HIGHEST
MESH = pl.DeviceIdType.MESH
DMA = pltpu.SemaphoreType.DMA
VMEM_LIMIT = 60 << 20
VMEM_MOST = 62 << 20
PIECES = 4


def normalize(values_in, scale_vec, shift_vec):
    center = jnp.mean(values_in, -1, keepdims=True)
    centered = values_in - center
    spread = jnp.mean(centered * centered, -1, keepdims=True)
    return centered * lax.rsqrt(spread + NORM_EPS) * scale_vec + shift_vec


def pair_loss(pair_items, labels):
    first_vec = pair_items[..., 0::2, :]
    second_vec = pair_items[..., 1::2, :]
    inner_prod = jnp.sum(first_vec * second_vec, -1)
    cosine = (
        inner_prod
        * lax.rsqrt(jnp.sum(first_vec * first_vec, -1) + 1e-06)
        * lax.rsqrt(jnp.sum(second_vec * second_vec, -1) + 1e-06)
    )
    error_term = cosine - labels.astype(jnp.float32) / 5.0
    return LOSS_SCALE * jnp.sum(error_term * error_term)


def adamw(weight, moment_one, moment_two, gradient, factor, step_count, rate):
    clipped = gradient * factor
    first_new = BETA_ONE * moment_one + (1.0 - BETA_ONE) * clipped
    second_new = BETA_TWO * moment_two + (1.0 - BETA_TWO) * clipped * clipped
    first_hat = first_new / (1.0 - BETA_ONE**step_count)
    second_hat = second_new / (1.0 - BETA_TWO**step_count)
    weight_new = weight - rate * (first_hat / (jnp.sqrt(second_hat) + ADAM_EPS) + DECAY * weight)
    return (weight_new, first_new, second_new)


class Layout:
    def __init__(self, features, shard, dp_count):
        self.features = features
        self.shard = shard
        self.dp_count = dp_count
        self.head_cols = features // MP
        self.ffn_cols = FF // MP
        self.total = shard * dp_count
        self.lines = self.total // LANES
        assert self.lines * LANES == self.total
        self.starts = [index * shard // LANES for index in range(dp_count)]
        need = max(
            ((index + 1) * shard - 1) // LANES - index * shard // LANES + 1
            for index in range(dp_count)
        )
        self.need = need
        self.length = -(-(need + 3) // (16 * PIECES)) * (16 * PIECES)
        self.cut = self.length // 2
        self.piece = self.length // PIECES
        self.step = max(
            rows for rows in range(16, 257, 16) if self.piece % rows == 0
        )
        self.mats = []
        offset = 0
        for height, extent in (
            (features, 3 * self.head_cols),
            (self.head_cols, features),
            (features, self.ffn_cols),
            (self.ffn_cols, features),
        ):
            assert extent % LANES == 0 and height % LANES == 0
            self.mats.append((offset, height, extent // LANES))
            offset += height * (extent // LANES)
        self.bias_start = offset
        self.bias_lines = self.lines - offset
        self.bias_rows = -(-self.bias_lines // 8) * 8
        self.flat_rows = -(-(self.starts[-1] + self.length) // 8) * 8


def weight_specs(lay):
    specs = [
        pl.BlockSpec((lay.features, 3 * lay.head_cols), lambda half: (0, half)),
        pl.BlockSpec((lay.head_cols, lay.features), lambda half: (half, 0)),
        pl.BlockSpec((lay.features, lay.ffn_cols), lambda half: (0, half)),
        pl.BlockSpec((lay.ffn_cols, lay.features), lambda half: (half, 0)),
        pl.BlockSpec((1, lay.bias_rows, LANES), lambda half: (half, 0, 0)),
    ]
    shapes = [
        (lay.features, MP * 3 * lay.head_cols),
        (MP * lay.head_cols, lay.features),
        (lay.features, MP * lay.ffn_cols),
        (MP * lay.ffn_cols, lay.features),
    ]
    return specs, shapes


def unpack_kernel(lay, lines_ref, qkv_ref, attn_ref, in_ref, out_ref, bias_ref, flat):
    for index in range(lay.dp_count):
        start = lay.starts[index]
        if index > 0:
            kept = flat[start : start + 1, :]
        flat[start : start + lay.length, :] = lines_ref[0, index].astype(jnp.float32)
        if index > 0:
            flat[start : start + 1, :] += kept
    for (offset, height, cols), ref in zip(lay.mats, (qkv_ref, attn_ref, in_ref, out_ref)):

        def body(step, carry, offset=offset, cols=cols, ref=ref):
            row = pl.multiple_of(step * LANES, LANES)
            for col in range(cols):
                block = flat[pl.ds(offset + row * cols + col, LANES, stride=cols), :]
                ref[pl.ds(row, LANES), col * LANES : (col + 1) * LANES] = block.astype(
                    jnp.bfloat16
                )
            return carry

        lax.fori_loop(0, height // LANES, body, 0)
    bias_ref[0] = flat[lay.bias_start : lay.bias_start + lay.bias_rows, :]


def unpack_weights(lay, gathered):
    specs, shapes = weight_specs(lay)
    return pl.pallas_call(
        partial(unpack_kernel, lay),
        grid=(MP,),
        in_specs=[
            pl.BlockSpec((1, lay.dp_count, lay.length, LANES), lambda half: (half, 0, 0, 0))
        ],
        out_specs=specs,
        out_shape=[jax.ShapeDtypeStruct(s, jnp.bfloat16) for s in shapes]
        + [jax.ShapeDtypeStruct((MP, lay.bias_rows, LANES), jnp.float32)],
        scratch_shapes=[pltpu.VMEM((lay.flat_rows, LANES), jnp.float32)],
        compiler_params=pltpu.CompilerParams(vmem_limit_bytes=VMEM_LIMIT),
        name="unpack_weights",
    )(gathered)


def pack_kernel(lay, qkv_ref, attn_ref, in_ref, out_ref, bias_ref, lines_ref, flat):
    for (offset, height, cols), ref in zip(lay.mats, (qkv_ref, attn_ref, in_ref, out_ref)):

        def body(step, carry, offset=offset, cols=cols, ref=ref):
            row = pl.multiple_of(step * LANES, LANES)
            for col in range(cols):
                block = ref[pl.ds(row, LANES), col * LANES : (col + 1) * LANES]
                flat[pl.ds(offset + row * cols + col, LANES, stride=cols), :] = block.astype(
                    jnp.float32
                )
            return carry

        lax.fori_loop(0, height // LANES, body, 0)
    tail = lay.flat_rows - lay.lines
    if tail:
        flat[lay.lines :, :] = jnp.zeros((tail, LANES), jnp.float32)
    flat[lay.bias_start : lay.lines, :] = bias_ref[0, : lay.bias_lines]
    for index in range(lay.dp_count):
        start = lay.starts[index]
        lines_ref[0, index] = flat[start : start + lay.length, :].astype(jnp.bfloat16)


def pack_gradients(lay, grads, bias_grad):
    specs, _ = weight_specs(lay)
    return pl.pallas_call(
        partial(pack_kernel, lay),
        grid=(MP,),
        in_specs=specs,
        out_specs=pl.BlockSpec(
            (1, lay.dp_count, lay.length, LANES), lambda half: (half, 0, 0, 0)
        ),
        out_shape=jax.ShapeDtypeStruct((MP, lay.dp_count, lay.length, LANES), jnp.bfloat16),
        scratch_shapes=[pltpu.VMEM((lay.flat_rows, LANES), jnp.float32)],
        compiler_params=pltpu.CompilerParams(vmem_limit_bytes=VMEM_LIMIT),
        name="pack_gradients",
    )(*grads, bias_grad)


class Place:
    def __init__(self):
        self.dp = lax.axis_index("dp")
        self.half = lax.axis_index("mp")
        self.z = self.dp // 4
        self.y = (self.dp // 2) % 2
        self.x = self.dp % 2
        self.has_up = self.z < 3
        self.has_down = self.z > 0
        self.up = (jnp.minimum(self.dp + 4, 12 + self.dp % 4), self.half)
        self.down = (jnp.maximum(self.dp - 4, self.dp % 4), self.half)
        self.xn = (self.shard(self.z, self.y, 1 - self.x), self.half)
        self.yn = (self.shard(self.z, 1 - self.y, self.x), self.half)
        self.sib = (self.dp, 1 - self.half)

    def shard(self, z, y, x):
        return z * 4 + y * 2 + x

    def barrier(self):
        bar = pltpu.get_barrier_semaphore()
        for dev in (self.xn, self.yn, self.sib):
            pl.semaphore_signal(bar, inc=1, device_id=dev, device_id_type=MESH)

        @pl.when(self.has_up)
        def _():
            pl.semaphore_signal(bar, inc=1, device_id=self.up, device_id_type=MESH)

        @pl.when(self.has_down)
        def _():
            pl.semaphore_signal(bar, inc=1, device_id=self.down, device_id_type=MESH)

        pl.semaphore_wait(
            bar, 3 + jnp.where(self.has_up, 1, 0) + jnp.where(self.has_down, 1, 0)
        )


def guarded(cond, work):
    if cond is None:
        work()
    else:
        pl.when(cond)(work)


def lane_ids(rows):
    return lax.broadcasted_iota(jnp.int32, (rows, LANES), 1)


def shift_into_lines(lay, own_ref, rolled, put):
    phase = lax.rem(lax.axis_index("dp") * lay.shard, LANES)
    rows = lay.length
    rolled[0:8, :] = jnp.zeros((8, LANES), jnp.float32)
    rolled[8 : 8 + rows, :] = pltpu.roll(own_ref[...], phase, 1)
    late = rolled[7 : 7 + rows, :]
    put(jnp.where(lane_ids(rows) < phase, late, rolled[8 : 8 + rows, :]))


def gather_lines(lay, own):
    flat = own.reshape(-1)
    phase = (lax.axis_index("dp") * lay.shard) % LANES
    own = jnp.roll(flat, phase).reshape(lay.length, LANES).astype(jnp.bfloat16)
    gathered = lax.all_gather(own, ("mp", "dp"), axis=0, tiled=True)
    return gathered.reshape(MP, lay.dp_count, lay.length, LANES)


def exchange_kernel(
    pooled_ref,
    codes_ref,
    labels_ref,
    core_ref,
    grad_ref,
    encoded_hbm,
    pooled,
    outgoing,
    incoming,
    returning,
    arrived,
    sib_sem,
    go_send,
    go_recv,
    back_send,
    back_recv,
    enc_sem,
):
    dp = lax.axis_index("dp")
    half = lax.axis_index("mp")
    sib = (dp, 1 - half)
    slots, capacity, features = outgoing.shape
    codes = slots * capacity
    core_sents = pooled_ref.shape[0]

    def peer(step):
        return (lax.rem(dp + step, slots), half)

    bar = pltpu.get_barrier_semaphore()
    pl.semaphore_signal(bar, inc=1, device_id=sib, device_id_type=MESH)
    for step in range(1, slots):
        pl.semaphore_signal(bar, inc=1, device_id=peer(step), device_id_type=MESH)
    pooled[half] = pooled_ref[...]
    pl.semaphore_wait(bar, slots)
    share = pltpu.make_async_remote_copy(
        src_ref=pooled_ref,
        dst_ref=pooled.at[half],
        send_sem=sib_sem.at[0],
        recv_sem=sib_sem.at[1],
        device_id=sib,
        device_id_type=MESH,
    )
    share.start()
    core_rows = core_ref.shape[0]
    place = encoded_hbm.at[pl.ds(pl.multiple_of(half * core_rows, 16), core_rows)]
    keep = pltpu.make_async_copy(core_ref, place, enc_sem.at[2])
    give = pltpu.make_async_remote_copy(
        src_ref=core_ref,
        dst_ref=place,
        send_sem=enc_sem.at[0],
        recv_sem=enc_sem.at[1],
        device_id=sib,
        device_id_type=MESH,
    )
    keep.start()
    give.start()

    code_ids = lax.broadcasted_iota(jnp.int32, (codes, codes), 0)
    send_map = (code_ids == codes_ref[0:1, :]).astype(jnp.bfloat16)
    pairs = codes // 2
    even_map = (code_ids[:, :pairs] == codes_ref[1:2, :pairs]).astype(jnp.bfloat16)
    odd_map = (code_ids[:, :pairs] == codes_ref[2:3, :pairs]).astype(jnp.bfloat16)
    share.wait()
    everything = jnp.concatenate([pooled[0], pooled[1]], 0)
    out = jnp.dot(send_map, everything, preferred_element_type=jnp.float32)
    outgoing[...] = out.reshape(outgoing.shape).astype(jnp.bfloat16)

    def copy(src, dst, send_sem, recv_sem, step):
        return pltpu.make_async_remote_copy(
            src_ref=src,
            dst_ref=dst,
            send_sem=send_sem.at[step],
            recv_sem=recv_sem.at[step],
            device_id=peer(step),
            device_id_type=MESH,
        )

    def all_to_all(src, dst, send_sem, recv_sem):
        for step in range(1, slots):
            copy(src.at[lax.rem(dp + step, slots)], dst.at[dp], send_sem, recv_sem, step).start()
        dst[dp] = src[dp]
        for step in range(1, slots):
            sender = lax.rem(dp + slots - step, slots)
            copy(src.at[sender], dst.at[sender], send_sem, recv_sem, step).wait()

    all_to_all(outgoing, incoming, go_send, go_recv)
    items = incoming[...].astype(jnp.float32).reshape(codes, features).astype(jnp.bfloat16)
    left = lax.dot_general(even_map, items, FIRST, preferred_element_type=jnp.float32)
    right = lax.dot_general(odd_map, items, FIRST, preferred_element_type=jnp.float32)
    inner = jnp.sum(left * right, -1, keepdims=True)
    left_inv = lax.rsqrt(jnp.sum(left * left, -1, keepdims=True) + 1e-06)
    right_inv = lax.rsqrt(jnp.sum(right * right, -1, keepdims=True) + 1e-06)
    both = left_inv * right_inv
    cosine = inner * both
    square = (pairs, pairs)
    eye = lax.broadcasted_iota(jnp.int32, square, 0) == lax.broadcasted_iota(
        jnp.int32, square, 1
    )
    target = jnp.sum(
        jnp.where(eye, labels_ref[0:1, :pairs].astype(jnp.float32), 0.0), 1, keepdims=True
    )
    slope = (2.0 * LOSS_SCALE) * (cosine - target / 5.0)
    left_grad = slope * (both * right - (cosine * left_inv * left_inv) * left)
    right_grad = slope * (both * left - (cosine * right_inv * right_inv) * right)
    back = jnp.dot(
        even_map, left_grad.astype(jnp.bfloat16), preferred_element_type=jnp.float32
    ) + jnp.dot(odd_map, right_grad.astype(jnp.bfloat16), preferred_element_type=jnp.float32)
    returning[...] = back.reshape(returning.shape).astype(jnp.bfloat16)
    all_to_all(returning, arrived, back_send, back_recv)
    items = arrived[...].astype(jnp.float32).reshape(codes, features).astype(jnp.bfloat16)
    grads = lax.dot_general(send_map, items, FIRST, preferred_element_type=jnp.float32)
    grad_ref[...] = jnp.where(half == 0, grads[:core_sents], grads[core_sents:])
    keep.wait()
    give.wait()


def exchange(
    pooled_core, encoded_core, sentence_dest, pair_source, labels, dp_count, capacity
):
    core_sents, features = pooled_core.shape
    codes = dp_count * capacity
    send_code = sentence_dest[:, 0] * capacity + sentence_dest[:, 1]
    take_code = pair_source[:, 0] * capacity + pair_source[:, 1]
    if dp_count == 16 and codes == send_code.shape[0] == 2 * core_sents:
        pairs = take_code.reshape(-1, 2).T
        pairs = jnp.pad(pairs, ((0, 0), (0, codes - pairs.shape[1])))
        table = jnp.concatenate([send_code[None], pairs, jnp.zeros((5, codes), jnp.int32)], 0)
        wide = (dp_count, capacity, features)
        low = jnp.bfloat16
        anywhere = pl.BlockSpec(memory_space=pl.ANY)
        vmem = pl.BlockSpec(memory_space=pltpu.VMEM)
        return pl.pallas_call(
            exchange_kernel,
            out_shape=[
                jax.ShapeDtypeStruct((core_sents, features), jnp.float32),
                jax.ShapeDtypeStruct((MP * encoded_core.shape[0], features), low),
            ],
            in_specs=[vmem] * 4,
            out_specs=[vmem, anywhere],
            scratch_shapes=[pltpu.VMEM((MP, core_sents, features), low)]
            + [pltpu.VMEM(wide, low)] * 4
            + [DMA((2,))]
            + [DMA((dp_count,))] * 4
            + [DMA((3,))],
            compiler_params=pltpu.CompilerParams(
                collective_id=2, has_side_effects=True, vmem_limit_bytes=VMEM_LIMIT
            ),
            name="exchange_pairs",
        )(pooled_core, table, labels[None], encoded_core)
    encoded = lax.all_gather(encoded_core, "mp", axis=0, tiled=True)
    mp_index = lax.axis_index("mp")
    pooled_flat = lax.all_gather(pooled_core, "mp", axis=0, tiled=True)
    code_ids = jnp.arange(codes, dtype=jnp.int32)
    send_map = (code_ids[:, None] == send_code[None, :]).astype(jnp.bfloat16)
    outgoing = jnp.dot(send_map, pooled_flat, preferred_element_type=jnp.float32).astype(
        jnp.bfloat16
    )
    outgoing = outgoing.reshape(dp_count, capacity, features)
    incoming = lax.all_to_all(outgoing, "dp", split_axis=0, concat_axis=0, tiled=True).reshape(
        codes, features
    )
    take_map = (take_code[:, None] == code_ids[None, :]).astype(jnp.bfloat16)
    pair_items = jnp.dot(take_map, incoming, preferred_element_type=jnp.float32)
    item_grad = jax.grad(pair_loss)(pair_items, labels).astype(jnp.bfloat16)
    returning = jnp.dot(take_map.T, item_grad, preferred_element_type=jnp.float32).astype(
        jnp.bfloat16
    )
    returning = returning.reshape(dp_count, capacity, features)
    arrived = lax.all_to_all(returning, "dp", split_axis=0, concat_axis=0, tiled=True).reshape(
        codes, features
    )
    core_map = lax.dynamic_slice_in_dim(send_map, mp_index * core_sents, core_sents, 1)
    return jnp.dot(core_map.T, arrived, preferred_element_type=jnp.float32), encoded


SCORE_SCALE = HEAD_DIM ** (-0.5)
LAST = (((1,), (1,)), ((), ()))
FIRST = (((0,), (0,)), ((), ()))


def low_lanes(rows):
    return lax.broadcasted_iota(jnp.int32, (rows, LANES), 1) < HEAD_DIM


def one_head(tile, odd):
    mask = low_lanes(tile.shape[0])
    if odd:
        return jnp.where(mask, jnp.zeros_like(tile), tile)
    return jnp.where(mask, tile, jnp.zeros_like(tile))


def attend_row(tiles, qkv_ref, seg_col_ref, seg_row_ref, out_ref, log_ref):
    width = tiles * LANES
    bias = jnp.where(seg_col_ref[...] == seg_row_ref[...], 0.0, -1e30)
    logs = []
    for tile in range(tiles):
        cols = slice(tile * LANES, (tile + 1) * LANES)
        queries = qkv_ref[:, cols] * SCORE_SCALE
        keys = qkv_ref[:, width + tile * LANES : width + (tile + 1) * LANES]
        values = qkv_ref[:, 2 * width + tile * LANES : 2 * width + (tile + 1) * LANES]
        mixed = []
        for odd in range(2):
            scores = lax.dot_general(
                one_head(queries, odd), keys, LAST, preferred_element_type=jnp.float32
            )
            scores = scores + bias
            row_max = jnp.max(scores, -1, keepdims=True)
            exponent = jnp.exp(scores - row_max)
            row_total = jnp.sum(exponent, -1, keepdims=True)
            probs = exponent.astype(jnp.bfloat16)
            mixed.append(
                jnp.dot(probs, values, preferred_element_type=jnp.float32) * (1.0 / row_total)
            )
            logs.append(row_max + jnp.log(row_total))
        both = jnp.where(low_lanes(ROW), mixed[0], mixed[1])
        out_ref[:, cols] = both.astype(jnp.bfloat16)
    log_ref[...] = jnp.concatenate(logs + [logs[0]] * (8 - 2 * tiles), 1)


def attend_kernel(tiles, qkv_ref, seg_col_ref, seg_row_ref, out_ref, log_ref):
    attend_row(tiles, qkv_ref, seg_col_ref, seg_row_ref.at[0], out_ref, log_ref.at[0])


def attend(qkv, seg_col, seg_row, head_cols):
    rows = qkv.shape[0] // ROW
    return pl.pallas_call(
        partial(attend_kernel, head_cols // LANES),
        grid=(rows, MP),
        in_specs=[
            pl.BlockSpec((ROW, 3 * head_cols), lambda r, m: (r, m)),
            pl.BlockSpec((ROW, 1), lambda r, m: (r, 0)),
            pl.BlockSpec((1, 1, ROW), lambda r, m: (r, 0, 0)),
        ],
        out_specs=[
            pl.BlockSpec((ROW, head_cols), lambda r, m: (r, m)),
            pl.BlockSpec((1, ROW, 8), lambda r, m: (m, r, 0)),
        ],
        out_shape=[
            jax.ShapeDtypeStruct((rows * ROW, MP * head_cols), jnp.bfloat16),
            jax.ShapeDtypeStruct((MP, rows * ROW, 8), jnp.float32),
        ],
        compiler_params=pltpu.CompilerParams(vmem_limit_bytes=VMEM_LIMIT),
        name="attend",
    )(qkv, seg_col, seg_row)


def attend_back_row(
    tiles, qkv_ref, grad_ref, log_ref, seg_col_ref, seg_wide_ref, out_ref, key_acc, value_acc
):
    width = tiles * LANES
    block, window = LANES, 2 * LANES
    key_acc[...] = jnp.zeros_like(key_acc)
    value_acc[...] = jnp.zeros_like(value_acc)
    for step in range(ROW // block):
        start = min(max(step * block - block // 2, 0), ROW - window)
        rows = slice(step * block, (step + 1) * block)
        span = slice(start, start + window)
        bias = jnp.where(seg_col_ref[rows, :] == seg_wide_ref[step], 0.0, -1e30)
        for tile in range(tiles):
            cols = slice(tile * LANES, (tile + 1) * LANES)
            queries = qkv_ref[rows, cols] * SCORE_SCALE
            keys = qkv_ref[span, width + tile * LANES : width + (tile + 1) * LANES]
            values = qkv_ref[span, 2 * width + tile * LANES : 2 * width + (tile + 1) * LANES]
            mixed_grad = grad_ref[rows, cols]
            query_grad = key_grad = value_grad = 0.0
            for odd in range(2):
                head = 2 * tile + odd
                query_one = one_head(queries, odd)
                grad_one = one_head(mixed_grad, odd)
                scores = lax.dot_general(
                    query_one, keys, LAST, preferred_element_type=jnp.float32
                )
                probs = jnp.exp((scores + bias) - log_ref[rows, head : head + 1])
                prob_grad = lax.dot_general(
                    grad_one, values, LAST, preferred_element_type=jnp.float32
                )
                row_inner = jnp.sum(prob_grad * probs, -1, keepdims=True)
                score_grad = (probs * (prob_grad - row_inner)).astype(jnp.bfloat16)
                value_grad += lax.dot_general(
                    probs.astype(jnp.bfloat16),
                    grad_one,
                    FIRST,
                    preferred_element_type=jnp.float32,
                )
                query_grad += jnp.dot(
                    score_grad, one_head(keys, odd), preferred_element_type=jnp.float32
                )
                key_grad += lax.dot_general(
                    score_grad, query_one, FIRST, preferred_element_type=jnp.float32
                )
            out_ref[rows, cols] = (query_grad * SCORE_SCALE).astype(jnp.bfloat16)
            key_acc[span, cols] += key_grad
            value_acc[span, cols] += value_grad
    out_ref[:, width : 2 * width] = key_acc[...].astype(jnp.bfloat16)
    out_ref[:, 2 * width :] = value_acc[...].astype(jnp.bfloat16)


def attend_back_kernel(
    tiles, qkv_ref, grad_ref, log_ref, seg_col_ref, seg_wide_ref, out_ref, key_acc, value_acc
):
    attend_back_row(
        tiles,
        qkv_ref,
        grad_ref,
        log_ref.at[0],
        seg_col_ref,
        seg_wide_ref.at[0],
        out_ref,
        key_acc,
        value_acc,
    )


def window_segments(seg_row):
    window = 2 * LANES
    starts = [
        min(max(step * LANES - LANES // 2, 0), ROW - window) for step in range(ROW // LANES)
    ]
    return jnp.stack([seg_row[:, :, start : start + window] for start in starts], 1)


def attend_back(qkv, mixed_grad, logs, seg_col, seg_row, head_cols):
    rows = qkv.shape[0] // ROW
    window = 2 * LANES
    seg_wide = window_segments(seg_row)
    return pl.pallas_call(
        partial(attend_back_kernel, head_cols // LANES),
        grid=(rows, MP),
        in_specs=[
            pl.BlockSpec((ROW, 3 * head_cols), lambda r, m: (r, m)),
            pl.BlockSpec((ROW, head_cols), lambda r, m: (r, m)),
            pl.BlockSpec((1, ROW, 8), lambda r, m: (m, r, 0)),
            pl.BlockSpec((ROW, 1), lambda r, m: (r, 0)),
            pl.BlockSpec((1, ROW // LANES, 1, window), lambda r, m: (r, 0, 0, 0)),
        ],
        out_specs=pl.BlockSpec((ROW, 3 * head_cols), lambda r, m: (r, m)),
        out_shape=jax.ShapeDtypeStruct(qkv.shape, jnp.bfloat16),
        scratch_shapes=[pltpu.VMEM((ROW, head_cols), jnp.float32)] * 2,
        compiler_params=pltpu.CompilerParams(vmem_limit_bytes=VMEM_LIMIT),
        name="attend_back",
    )(qkv, mixed_grad, logs, seg_col, seg_wide)


PARTS = 4
BIAS_ROWS = 32


def start_kernel(
    lay,
    own_ref,
    tokens_hbm,
    seg_col_ref,
    seg_row_ref,
    qkv_weight_hbm,
    attn_weight_hbm,
    in_weight_hbm,
    out_weight_hbm,
    bias_ref,
    qkv_hbm,
    mixed_hbm,
    log_ref,
    buf,
    rolled,
    flat,
    biases,
    tokens,
    qkv_weight,
    attn_weight,
    in_weight,
    out_weight,
    qkv,
    mixed,
    load_sem,
    store_sem,
    zs_sem,
    zr_sem,
    xs_sem,
    xr_sem,
    ys_sem,
    yr_sem,
    ss_sem,
    sr_sem,
    bs_sem,
    br_sem,
):
    at = Place()
    other_half = 1 - at.half
    width = 3 * lay.head_cols
    me = at.dp * MP + at.half
    count = 16 * MP
    last = 15
    bias_from = lay.bias_start - lay.starts[last]
    core_rows = tokens.shape[0]

    load_tokens = pltpu.make_async_copy(
        tokens_hbm.at[pl.ds(pl.multiple_of(at.half * core_rows, 16), core_rows)], tokens, load_sem
    )
    load_tokens.start()

    def peer(step):
        other = lax.rem(me + step, count)
        return (other // MP, lax.rem(other, MP))

    bar = pltpu.get_barrier_semaphore()

    def greet(step, carry):
        pl.semaphore_signal(bar, inc=1, device_id=peer(step), device_id_type=MESH)
        return carry

    lax.fori_loop(1, count, greet, 0)

    def put(lines):
        buf[at.half, at.dp] = lines.astype(jnp.bfloat16)

    shift_into_lines(lay, own_ref, rolled, put)
    pl.semaphore_wait(bar, count - 1)
    sends = []

    def remote(src, dst, send_sem, recv_sem, dev):
        return pltpu.make_async_remote_copy(
            src_ref=src,
            dst_ref=dst,
            send_sem=send_sem,
            recv_sem=recv_sem,
            device_id=dev,
            device_id_type=MESH,
        )

    def bias_out(step):
        return remote(
            buf.at[at.half, last, pl.ds(bias_from, BIAS_ROWS)],
            biases.at[at.half],
            bs_sem.at[step],
            br_sem.at[at.half],
            peer(step),
        )

    @pl.when(at.dp == last)
    def _():
        def go(step, carry):
            bias_out(step).start()
            return carry

        lax.fori_loop(1, count, go, 0)
        biases[at.half] = buf[at.half, last, bias_from : bias_from + BIAS_ROWS, :]

    def wait_biases():
        for half in range(MP):

            @pl.when((at.dp != last) | (at.half != half))
            def _(half=half):
                remote(
                    buf.at[half, last, pl.ds(bias_from, BIAS_ROWS)],
                    biases.at[half],
                    bs_sem.at[0],
                    br_sem.at[half],
                    at.sib,
                ).wait_recv()

    def wait_bias_sends():
        @pl.when(at.dp == last)
        def _():
            def done(step, carry):
                bias_out(step).wait_send()
                return carry

            lax.fori_loop(1, count, done, 0)

    def move(index, part, send_sem, recv_sem, dev, half=None):
        rows = lay.length // PARTS
        piece = buf.at[at.half if half is None else half, index, pl.ds(part * rows, rows)]
        return remote(piece, piece, send_sem, recv_sem, dev)

    def send(index, part, send_sem, recv_sem, dev, cond=None):
        guarded(cond, lambda: move(index, part, send_sem, recv_sem, dev).start())
        sends.append((cond, lambda: move(index, part, send_sem, recv_sem, dev).wait_send()))

    def share(index, part, cond=None):
        send(index, part, ss_sem.at[index, part], sr_sem.at[index, part], at.sib, cond)

    def up(group, part, cond):
        index = at.shard(group, at.y, at.x)
        send(index, part, zs_sem.at[0, group, part], zr_sem.at[group, part], at.up, cond)

    def down(group, part, cond):
        index = at.shard(group, at.y, at.x)
        send(index, part, zs_sem.at[1, group, part], zr_sem.at[group, part], at.down, cond)

    def spread(group, part):
        index = at.shard(group, at.y, at.x)
        send(index, part, xs_sem.at[group, part], xr_sem.at[group, part], at.xn)
        send(index, part, ys_sem.at[group, part], yr_sem.at[group, part], at.yn)
        share(index, part)

    turns = (
        at.z,
        jnp.where(at.z == 0, 1, 0),
        jnp.where(at.z <= 1, 2, 1),
        jnp.where(at.z == 3, 2, 3),
    )

    def wait_along(group, part):
        index = at.shard(group, at.y, at.x)
        move(
            index, part, zs_sem.at[0, group, part], zr_sem.at[group, part], at.sib
        ).wait_recv()

    def along(turn):
        group = turns[turn]
        for part in range(PARTS):
            if turn < 3:
                wait_along(group, part)
                up(group, part, (group < at.z) & at.has_up)
                down(group, part, (group > at.z) & at.has_down)
            else:
                guarded((at.z == 0) | (at.z == 3), lambda part=part: wait_along(group, part))
            spread(group, part)

    def relay(z):
        for part in range(PARTS):
            guarded(at.z == z, lambda part=part: wait_along(3, part))
            down(3, part, at.z == z)

    def plane(turn):
        group = turns[turn]
        for part in range(PARTS):
            from_x = at.shard(group, at.y, 1 - at.x)
            from_y = at.shard(group, 1 - at.y, at.x)
            move(
                from_x, part, xs_sem.at[group, part], xr_sem.at[group, part], at.xn
            ).wait_recv()
            if part < PARTS // 2:
                slot = PARTS + part
                send(from_x, part, ys_sem.at[group, slot], yr_sem.at[group, slot], at.yn)
            share(from_x, part)
            move(
                from_y, part, ys_sem.at[group, part], yr_sem.at[group, part], at.yn
            ).wait_recv()
            if part >= PARTS // 2:
                slot = PARTS // 2 + part
                send(from_y, part, xs_sem.at[group, slot], xr_sem.at[group, slot], at.xn)
            share(from_y, part)

    def diagonal(turn):
        group = turns[turn]
        index = at.shard(group, 1 - at.y, 1 - at.x)
        for part in range(PARTS):
            if part < PARTS // 2:
                slot = PARTS + part
                move(
                    index, part, ys_sem.at[group, slot], yr_sem.at[group, slot], at.yn
                ).wait_recv()
            else:
                slot = PARTS // 2 + part
                move(
                    index, part, xs_sem.at[group, slot], xr_sem.at[group, slot], at.xn
                ).wait_recv()
            share(index, part)

    def wait_shared(groups):
        for index in range(4 * groups[0], 4 * groups[-1] + 4):
            for part in range(PARTS):
                move(
                    index,
                    part,
                    ss_sem.at[index, part],
                    sr_sem.at[index, part],
                    at.sib,
                    other_half,
                ).wait_recv()

    stores = []

    def store(src, dst):
        copy = pltpu.make_async_copy(src, dst, store_sem.at[len(stores)])
        copy.start()
        stores.append(copy)

    def to_lines(half, shards):
        base = lay.starts[shards[0]]
        for index in shards:
            start = lay.starts[index] - base
            if index > shards[0]:
                kept = flat[start : start + 1, :]
            flat[start : start + lay.length, :] = buf[half, index].astype(jnp.float32)
            if index > shards[0]:
                flat[start : start + 1, :] += kept
        return base

    def to_matrix(base, which, ref, row_at, col_at, first_row, rows):
        offset, _, cols = lay.mats[which]

        def body(step, carry):
            row = pl.multiple_of(first_row + step * LANES, LANES)
            dst = pl.ds(pl.multiple_of(row_at + row, LANES), LANES)
            for col in range(cols):
                block = flat[pl.ds(offset - base + row * cols + col, LANES, stride=cols), :]
                lanes = pl.ds(pl.multiple_of(col_at + col * LANES, LANES), LANES)
                ref[dst, lanes] = block.astype(jnp.bfloat16)
            return carry

        lax.fori_loop(0, rows // LANES, body, 0)

    features = lay.features
    halves = (at.half, other_half)

    def stage_one(half):
        base = to_lines(half, range(0, 4))
        to_matrix(base, 0, qkv_weight, 0, half * width, 0, features)

    cut_rows = (lay.starts[8] - lay.mats[2][0]) // lay.mats[2][2] // LANES * LANES

    def stage_two(half):
        base = to_lines(half, range(3, 8))
        to_matrix(base, 1, attn_weight, half * lay.head_cols, 0, 0, lay.head_cols)
        to_matrix(base, 2, in_weight, 0, half * lay.ffn_cols, 0, cut_rows)

    def stage_three(half):
        base = to_lines(half, range(7, 16))
        to_matrix(base, 2, in_weight, 0, half * lay.ffn_cols, cut_rows, features - cut_rows)
        later_rows = pl.ds(cut_rows, features - cut_rows)
        cols = pl.ds(pl.multiple_of(half * lay.ffn_cols, LANES), lay.ffn_cols)
        store(in_weight.at[later_rows, cols], in_weight_hbm.at[later_rows, cols])
        to_matrix(base, 3, out_weight, half * lay.ffn_cols, 0, 0, lay.ffn_cols)
        rows = pl.ds(pl.multiple_of(half * lay.ffn_cols, LANES), lay.ffn_cols)
        store(out_weight.at[rows], out_weight_hbm.at[rows])

    tiles = lay.head_cols // LANES

    def project(row, half):
        rows = pl.ds(row * ROW, ROW)
        cols = pl.ds(half * width, width)
        lines = biases[half].astype(jnp.float32)
        bias = jnp.concatenate(
            [lines[tile : tile + 1] for tile in range(tiles)]
            + [jnp.zeros((1, lay.head_cols), jnp.float32)]
            + [lines[tiles + tile : tiles + tile + 1] for tile in range(tiles)],
            1,
        )
        value = jnp.dot(tokens[rows, :], qkv_weight[:, cols], preferred_element_type=jnp.float32)
        qkv[rows, cols] = (value + bias).astype(jnp.bfloat16)

    def attention(row, half):
        rows = pl.ds(row * ROW, ROW)
        attend_row(
            tiles,
            qkv.at[rows, pl.ds(half * width, width)],
            seg_col_ref.at[rows],
            seg_row_ref.at[row],
            mixed.at[rows, pl.ds(half * lay.head_cols, lay.head_cols)],
            log_ref.at[half, rows],
        )

    for part in range(PARTS):
        spread(at.z, part)
        down(at.z, part, at.has_down)
        up(at.z, part, at.z == 0)
    along(1)
    for part in range(PARTS):
        up(at.z, part, at.z == 1)
    relay(2)
    plane(0)
    along(2)
    for part in range(PARTS):
        up(at.z, part, at.z == 2)
    diagonal(0)
    plane(1)
    relay(1)
    diagonal(1)
    load_tokens.wait()
    stage_one(halves[0])
    wait_shared((0,))
    stage_one(halves[1])
    store(qkv_weight, qkv_weight_hbm)
    wait_biases()
    along(3)
    project(0, 0)
    project(0, 1)
    plane(2)
    project(1, 0)
    project(1, 1)
    store(qkv, qkv_hbm)
    diagonal(2)
    attention(0, 0)
    wait_shared((1,))
    for half in halves:
        stage_two(half)
    store(attn_weight, attn_weight_hbm)
    store(in_weight.at[pl.ds(0, cut_rows)], in_weight_hbm.at[pl.ds(0, cut_rows)])
    attention(0, 1)
    plane(3)
    attention(1, 0)
    diagonal(3)
    attention(1, 1)
    store(mixed, mixed_hbm)
    stage_three(halves[0])
    wait_shared((2, 3))
    stage_three(halves[1])
    for half in range(MP):
        bias_ref[half] = biases[half].astype(jnp.float32)
    wait_bias_sends()
    for cond, work in sends:
        guarded(cond, work)
    for copy in stores:
        copy.wait()


def start_step(lay, own, tokens, seg_col, seg_row):
    core_rows = seg_col.shape[0]
    features, width = lay.features, 3 * lay.head_cols
    assert lay.starts[4] >= lay.mats[1][0] and lay.starts[3] <= lay.mats[1][0]
    assert lay.starts[8] >= lay.mats[2][0] and lay.bias_lines <= BIAS_ROWS
    assert (lay.bias_start - lay.starts[15]) % 16 == 0
    assert lay.bias_start - lay.starts[15] + BIAS_ROWS <= lay.length
    low, full = jnp.bfloat16, jnp.float32
    flat_rows = max(
        lay.starts[high] - lay.starts[first] + lay.length
        for first, high in ((0, 3), (3, 7), (7, 15))
    )
    flat_rows = -(-flat_rows // 8) * 8
    vmem = pl.BlockSpec(memory_space=pltpu.VMEM)
    anywhere = pl.BlockSpec(memory_space=pl.ANY)
    shape = jax.ShapeDtypeStruct
    weights = [
        (features, MP * width),
        (features, features),
        (features, MP * lay.ffn_cols),
        (MP * lay.ffn_cols, features),
    ]
    acts = [(core_rows, MP * width), (core_rows, features)]
    scratch = pltpu.VMEM
    return pl.pallas_call(
        partial(start_kernel, lay),
        out_shape=[shape(size, low) for size in weights]
        + [shape((MP, BIAS_ROWS, LANES), full)]
        + [shape(size, low) for size in acts]
        + [shape((MP, core_rows, 8), full)],
        in_specs=[vmem, anywhere, vmem, vmem],
        out_specs=[anywhere] * 4 + [vmem] + [anywhere] * 2 + [vmem],
        scratch_shapes=[
            scratch((MP, 16, lay.length, LANES), low),
            scratch((lay.length + 8, LANES), full),
            scratch((flat_rows, LANES), full),
            scratch((MP, BIAS_ROWS, LANES), low),
            scratch((core_rows, features), low),
        ]
        + [scratch(size, low) for size in weights + acts]
        + [
            DMA,
            DMA((12,)),
            DMA((2, 4, PARTS)),
            DMA((4, PARTS)),
            DMA((4, 2 * PARTS)),
            DMA((4, 2 * PARTS)),
            DMA((4, 2 * PARTS)),
            DMA((4, 2 * PARTS)),
            DMA((16, PARTS)),
            DMA((16, PARTS)),
            DMA((16 * MP,)),
            DMA((MP,)),
        ],
        compiler_params=pltpu.CompilerParams(
            collective_id=0, has_side_effects=True, vmem_limit_bytes=VMEM_MOST
        ),
        name="start_step",
    )(own, tokens, seg_col, seg_row)


STAT_ROWS = 4
SPLIT = 4
LATE_LINES = 6


def extra_lines(index):
    if index < SPLIT:
        return (2 * index, 2) if 2 * index < LATE_LINES else (0, 0)
    first = LATE_LINES + 3 * (index - SPLIT)
    return (first, 3) if first < 36 else (0, 0)


def extra_place(place):
    if place < LATE_LINES:
        return place // 2, 1 + place % 2
    return SPLIT + (place - LATE_LINES) // 3, 1 + (place - LATE_LINES) % 3


def finish_kernel(
    lay,
    in_hbm,
    out_hbm,
    attn_hbm,
    qkv_hbm,
    mixed_hbm,
    tokens_hbm,
    weight_hbm,
    resid_hbm,
    logs_ref,
    seg_col_ref,
    seg_wide_ref,
    extra_ref,
    grad_ref,
    norm_ref,
    shared_ref,
    input_hbm,
    staged_in,
    staged_out,
    staged_attn,
    flat,
    part,
    from_sib,
    from_x,
    from_y,
    diag_x,
    diag_y,
    from_z,
    total,
    stats,
    extras,
    tail,
    qkv,
    mixed,
    tokens,
    qkv_grad,
    key_acc,
    value_acc,
    weight,
    resid,
    load_sem,
    row_sem,
    ss_sem,
    sr_sem,
    xs_sem,
    xr_sem,
    ys_sem,
    yr_sem,
    dx_sem,
    dy_sem,
    zs_sem,
    zr_sem,
    bs_sem,
    br_sem,
    is_sem,
    ir_sem,
):
    at = Place()
    other_half = 1 - at.half
    width = 3 * lay.head_cols
    first_line = lay.mats[1][0]

    def load_in(half):
        cols = pl.ds(pl.multiple_of(half * lay.ffn_cols, LANES), lay.ffn_cols)
        return pltpu.make_async_copy(in_hbm.at[:, cols], staged_in, load_sem.at[0])

    def load_out(half):
        rows = pl.ds(pl.multiple_of(half * lay.ffn_cols, LANES), lay.ffn_cols)
        return pltpu.make_async_copy(out_hbm.at[rows, :], staged_out, load_sem.at[1])

    def load_attn(half):
        rows = pl.ds(pl.multiple_of(half * lay.head_cols, LANES), lay.head_cols)
        return pltpu.make_async_copy(attn_hbm.at[rows, :], staged_attn, load_sem.at[2])

    head_space = staged_attn.at[pl.ds(0, LANES)]

    def load_head(half):
        rows = pl.ds(pl.multiple_of(half * lay.head_cols, LANES), LANES)
        return pltpu.make_async_copy(attn_hbm.at[rows, :], head_space, load_sem.at[2])

    def load_row(row):
        rows = pl.ds(row * ROW, ROW)
        return [
            pltpu.make_async_copy(qkv_hbm.at[rows, :], qkv, row_sem.at[0]),
            pltpu.make_async_copy(mixed_hbm.at[rows, :], mixed, row_sem.at[1]),
        ]

    load_tokens = pltpu.make_async_copy(tokens_hbm, tokens, row_sem.at[2])

    def load_back(chunk):
        cols = pl.ds(chunk * 2 * LANES, 2 * LANES)
        return [
            pltpu.make_async_copy(weight_hbm.at[cols, :], weight, row_sem.at[3]),
            pltpu.make_async_copy(resid_hbm.at[:, cols], resid, row_sem.at[4]),
        ]

    def back_place(chunk, half):
        rows = pl.ds(pl.multiple_of(half * resid.shape[0], 16), resid.shape[0])
        return input_hbm.at[rows, pl.ds(chunk * 2 * LANES, 2 * LANES)]

    def store_back(chunk):
        return pltpu.make_async_copy(resid, back_place(chunk, at.half), row_sem.at[5])

    def share_back(chunk):
        return remote(
            resid, back_place(chunk, at.half), is_sem.at[chunk], ir_sem.at[chunk], at.sib
        )

    load_in(other_half).start()
    load_out(other_half).start()
    load_attn(other_half).start()
    for copy in load_row(0):
        copy.start()
    load_tokens.start()

    bar = pltpu.get_barrier_semaphore()
    me = at.dp * MP + at.half
    count = 16 * MP

    def peer(step):
        other = lax.rem(me + step, count)
        return (other // MP, lax.rem(other, MP))

    def greet(step, carry):
        pl.semaphore_signal(bar, inc=1, device_id=peer(step), device_id_type=MESH)
        return carry

    lax.fori_loop(1, count, greet, 0)
    sends = []

    def remote(src, dst, send_sem, recv_sem, dev):
        return pltpu.make_async_remote_copy(
            src_ref=src,
            dst_ref=dst,
            send_sem=send_sem,
            recv_sem=recv_sem,
            device_id=dev,
            device_id_type=MESH,
        )

    def later(cond, copy):
        sends.append((cond, lambda: copy().wait_send()))

    def lay_out(ref, offset, height, cols, base):
        def body(step, carry):
            row = pl.multiple_of(step * LANES, LANES)
            for col in range(cols):
                block = ref[pl.ds(row, LANES), col * LANES : (col + 1) * LANES]
                flat[pl.ds(offset - base + row * cols + col, LANES, stride=cols), :] = (
                    block.astype(jnp.float32)
                )
            return carry

        lax.fori_loop(0, height // LANES, body, 0)

    tail_from = lay.need // 16 * 16
    spare = lay.need - tail_from

    def emit(half, index, base):
        start = lay.starts[index] - base
        first, number = extra_lines(index)
        if number == 0:
            part[half, index] = flat[start : start + lay.length, :].astype(jnp.bfloat16)
            return
        part[half, index, :tail_from] = flat[start : start + tail_from, :].astype(jnp.bfloat16)
        tail[0:spare, :] = flat[start + tail_from : start + lay.need, :]
        tail[spare : spare + number, :] = extras[half, first : first + number, :]
        part[half, index, tail_from : tail_from + 16] = tail[...].astype(jnp.bfloat16)
        part[half, index, tail_from + 16 :] = jnp.zeros(
            (lay.length - tail_from - 16, LANES), jnp.bfloat16
        )

    def to_sib(index):
        return remote(
            part.at[other_half, index],
            from_sib.at[index],
            ss_sem.at[index],
            sr_sem.at[index],
            at.sib,
        )

    def emit_all(half, indices, base, share):
        for index in indices:
            emit(half, index, base)
            if share:
                to_sib(index).start()
                later(None, lambda index=index: to_sib(index))

    extras[...] = extra_ref[...]
    early = list(range(12, 16)) + list(range(8, 12)) + list(range(SPLIT, 8))
    late = list(range(SPLIT))
    tail[...] = jnp.zeros_like(tail)
    rows = flat.shape[0] - (lay.bias_start - first_line)
    for half, share in ((other_half, True), (at.half, False)):
        load_in(half).wait()
        lay_out(staged_in, *lay.mats[2], first_line)
        if share:
            load_in(at.half).start()
        load_out(half).wait()
        lay_out(staged_out, *lay.mats[3], first_line)
        if share:
            load_out(at.half).start()
            pl.semaphore_wait(bar, count - 1)
        load_attn(half).wait()
        lay_out(staged_attn, *lay.mats[1], first_line)
        if share:
            load_attn(at.half).start()
        flat[lay.bias_start - first_line :, :] = jnp.zeros((rows, LANES), jnp.float32)
        emit_all(half, early, first_line, share)
    load_head(other_half).start()

    my_part = part.at[at.half]

    def wait_sib(index):
        to_sib(index).wait_recv()

    def wide(ref, rows):
        return ref[rows, :].astype(jnp.float32)

    def add_span(dst, terms, begin, size):
        def body(step, carry):
            off = step * lay.step
            spans = [
                pl.ds(pl.multiple_of(first + off, 16), lay.step) for _, first in terms
            ]
            value = wide(terms[0][0], spans[0])
            for (ref, _), span in zip(terms[1:], spans[1:]):
                value = value + wide(ref, span)
            dst[pl.ds(pl.multiple_of(begin + off, 16), lay.step), :] = value.astype(dst.dtype)
            return carry

        lax.fori_loop(0, size // lay.step, body, 0)

    def diag_out(z, index, axis):
        mine = my_part.at[index]
        if axis == 0:
            return remote(
                mine.at[pl.ds(0, lay.cut)], diag_y.at[z], dy_sem.at[z, 0], dy_sem.at[z, 1], at.yn
            )
        return remote(
            mine.at[pl.ds(lay.cut, lay.cut)],
            diag_x.at[z],
            dx_sem.at[z, 0],
            dx_sem.at[z, 1],
            at.xn,
        )

    def diagonal(z):
        index = at.shard(z, 1 - at.y, 1 - at.x)
        wait_sib(index)
        mine = my_part.at[index]
        add_span(mine, [(mine, 0), (from_sib.at[index], 0)], 0, lay.length)
        for axis in range(2):
            diag_out(z, index, axis).start()
            later(None, lambda axis=axis: diag_out(z, index, axis))

    def plane_out(z, index, piece, to_y):
        rows = pl.ds(piece * lay.piece, lay.piece)
        if to_y:
            return remote(
                my_part.at[index, rows],
                from_y.at[z, rows],
                ys_sem.at[z, piece],
                yr_sem.at[z, piece],
                at.yn,
            )
        return remote(
            my_part.at[index, rows],
            from_x.at[z, rows],
            xs_sem.at[z, piece],
            xr_sem.at[z, piece],
            at.xn,
        )

    def plane(z):
        for to_y in range(2):
            y = 1 - at.y if to_y else at.y
            x = at.x if to_y else 1 - at.x
            index = at.shard(z, y, x)
            mine, sib = my_part.at[index], from_sib.at[index]
            wait_sib(index)
            diag_out(z, index, 1 if to_y else 0).wait_recv()
            for piece in range(PIECES):
                begin = piece * lay.piece
                terms = [(mine, begin), (sib, begin)]
                if to_y and begin >= lay.cut:
                    terms.append((diag_x.at[z], begin - lay.cut))
                if not to_y and begin < lay.cut:
                    terms.append((diag_y.at[z], begin))
                add_span(mine, terms, begin, lay.piece)
                plane_out(z, index, piece, to_y).start()
                later(
                    None,
                    lambda index=index, piece=piece, to_y=to_y: plane_out(
                        z, index, piece, to_y
                    ),
                )

    def chain_out(z, index, piece, dev, slot):
        rows = pl.ds(piece * lay.piece, lay.piece)
        return remote(
            my_part.at[index, rows],
            from_z.at[slot, rows],
            zs_sem.at[z, piece],
            zr_sem.at[slot, piece],
            dev,
        )

    def chain_in(slot, piece):
        return chain_out(0, at.dp, piece, at.sib, slot)

    def gather_terms(z, index, piece):
        plane_out(z, index, piece, 0).wait_recv()
        plane_out(z, index, piece, 1).wait_recv()
        begin = piece * lay.piece
        return [
            (my_part.at[index], begin),
            (from_sib.at[index], begin),
            (from_x.at[z], begin),
            (from_y.at[z], begin),
        ]

    def chain(z, hop):
        index = at.shard(z, at.y, at.x)
        for down in range(2):
            spot = 3 - hop if down else hop
            if (spot <= z) if down else (spot >= z):
                continue
            dev = at.down if down else at.up
            slot = 4 if down and spot - 1 == z else z
            cond = at.z == spot

            def work(dev=dev, slot=slot):
                wait_sib(index)
                for piece in range(PIECES):
                    terms = gather_terms(z, index, piece)
                    begin = piece * lay.piece
                    if hop > 0:
                        chain_in(z, piece).wait_recv()
                        terms.append((from_z.at[z], begin))
                    add_span(my_part.at[index], terms, begin, lay.piece)
                    chain_out(z, index, piece, dev, slot).start()

            guarded(cond, work)
            for piece in range(PIECES):
                later(
                    cond,
                    lambda piece=piece, dev=dev, slot=slot: chain_out(
                        z, index, piece, dev, slot
                    ),
                )

    tiles = lay.head_cols // LANES

    def attention(row, half):
        cols = pl.ds(half * width, width)
        attend_back_row(
            tiles,
            qkv.at[:, cols],
            mixed.at[:, pl.ds(half * lay.head_cols, lay.head_cols)],
            logs_ref.at[half, pl.ds(row * ROW, ROW)],
            seg_col_ref.at[pl.ds(row * ROW, ROW)],
            seg_wide_ref.at[row],
            qkv_grad.at[pl.ds(row * ROW, ROW), cols],
            key_acc,
            value_acc,
        )

    core_rows = qkv_grad.shape[0]

    def weights(half, share):
        ones = jnp.ones((16, core_rows), jnp.bfloat16)
        for section in range(3):
            cols = pl.ds(
                pl.multiple_of(half * width + section * lay.head_cols, LANES), lay.head_cols
            )
            grads = qkv_grad[:, cols]
            result = jnp.dot(tokens[...], grads, preferred_element_type=jnp.float32)
            for tile in range(tiles):
                flat[pl.ds(section * tiles + tile, lay.features, stride=3 * tiles), :] = (
                    result[:, tile * LANES : (tile + 1) * LANES]
                )
            if section != 1:
                sums = jnp.dot(ones, grads, preferred_element_type=jnp.float32)
                first = 0 if section == 0 else tiles
                for tile in range(tiles):
                    extras[half, first + tile : first + tile + 1, :] = sums[
                        0:1, tile * LANES : (tile + 1) * LANES
                    ]
        load_head(half).wait()
        lay_out(head_space, lay.mats[1][0], LANES, lay.mats[1][2], 0)
        if share:
            load_head(at.half).start()
        emit_all(half, late, 0, share)

    def back(chunk):
        for copy in load_back(chunk):
            copy.wait()
        for row in range(core_rows // ROW):
            rows = pl.ds(row * ROW, ROW)
            resid[rows, :] += lax.dot_general(
                qkv_grad[rows, :], weight[...], LAST, preferred_element_type=jnp.float32
            )
        store_back(chunk).start()
        share_back(chunk).start()

    diagonal(3)
    diagonal(2)
    diagonal(1)
    for copy in load_row(0):
        copy.wait()
    attention(0, 0)
    plane(3)
    attention(0, 1)
    for copy in load_row(1):
        copy.start()
    plane(2)
    for copy in load_row(1):
        copy.wait()
    attention(1, 0)
    plane(1)
    chain(3, 0)
    attention(1, 1)
    load_tokens.wait()
    chain(3, 1)
    chain(2, 0)
    weights(other_half, True)
    for copy in load_back(0):
        copy.start()
    weights(at.half, False)
    diagonal(0)
    chain(3, 2)
    chain(1, 0)
    chain(2, 1)
    back(0)
    plane(0)
    store_back(0).wait()
    share_back(0).wait_send()
    for copy in load_back(1):
        copy.start()
    chain(1, 1)
    back(1)
    chain(0, 0)
    store_back(1).wait()
    share_back(1).wait_send()
    for copy in load_back(2):
        copy.start()
    chain(0, 1)
    back(2)
    chain(0, 2)

    index = at.dp
    wait_sib(index)
    for piece in range(PIECES):
        begin = piece * lay.piece
        add_span(total, gather_terms(at.z, index, piece), begin, lay.piece)
    for down in range(2):
        slot = 4 if down else at.z

        @pl.when((at.z < 3) if down else (at.z > 0))
        def _(slot=slot):
            for piece in range(PIECES):
                chain_in(slot, piece).wait_recv()
                begin = piece * lay.piece
                add_span(total, [(total, begin), (from_z.at[slot], begin)], begin, lay.piece)

    scale = 1.0 / LOSS_SCALE
    phase = lax.rem(lax.axis_index("dp") * lay.shard, LANES)
    keep = lay.length - 8
    lanes = lane_ids(keep)
    spots = lax.broadcasted_iota(jnp.int32, (keep, LANES), 0) * LANES + lanes - phase
    lines = jnp.where((spots >= 0) & (spots < lay.shard), total[:keep, :] * scale, 0.0)
    extra = total[lay.need : lay.need + 3, :] * scale
    number = jnp.where(at.dp < SPLIT, 2, 3)
    for index in range(16):
        if extra_lines(index)[1] == 0:
            number = jnp.where(at.dp == index, 0, number)
    extra_rows = lax.broadcasted_iota(jnp.int32, (3, LANES), 0)
    stats[me, 0:1] = jnp.sum(lines * lines, 0, keepdims=True)
    stats[me, 1:4] = jnp.where(extra_rows < number, extra, 0.0)

    def tell(step):
        return remote(stats.at[me], stats.at[me], bs_sem.at[step], br_sem.at[step], peer(step))

    def hear(step):
        other = lax.rem(me + count - step, count)
        return remote(
            stats.at[other], stats.at[other], bs_sem.at[step], br_sem.at[step], peer(step)
        )

    def start_tell(step, carry):
        tell(step).start()
        return carry

    def finish(step, carry):
        hear(step).wait_recv()
        tell(step).wait_send()
        return carry

    lax.fori_loop(1, count, start_tell, 0)
    store_back(2).wait()
    share_back(2).wait_send()
    for chunk in range(3):
        share_back(chunk).wait_recv()
    for cond, work in sends:
        guarded(cond, work)
    lax.fori_loop(1, count, finish, 0)
    everyone = stats[...]
    squares = jnp.sum(everyone[:, 0])
    for row in range(3):
        squares = squares + jnp.sum(everyone[:, 1 + row] * everyone[:, 1 + row])
    norm_ref[...] = jnp.full((1, LANES), squares, jnp.float32)

    def extra_line(half, place):
        shard, row = extra_place(place)
        return stats.at[shard * MP + half, pl.ds(row, 1)]

    across = lay.features // LANES
    lines_half = 6 * across // MP
    for line in range(6 * across):
        half, place = line // lines_half, line % lines_half
        row, col = line // across, line % across
        shared_ref[row : row + 1, col * LANES : (col + 1) * LANES] = extra_line(
            half, lay.bias_lines + place
        )[...]

    @pl.when(at.dp == 15)
    def _():
        first = lay.bias_start - lay.starts[15]
        for place in range(lay.bias_lines):
            total[first + place : first + place + 1, :] = (
                extra_line(at.half, place)[...] * LOSS_SCALE
            )

    back_shift = lax.rem(LANES - phase, LANES)
    total[...] = pltpu.roll(total[...] * scale, back_shift, 1)
    grad_ref[:keep, :] = jnp.where(
        lanes < LANES - phase, total[:keep, :], total[1 : keep + 1, :]
    )
    grad_ref[keep:, :] = jnp.zeros((8, LANES), jnp.float32)


def finish_step(
    lay,
    ffn_grads,
    w_attn_grad,
    qkv,
    mixed_grad,
    tokens_turned,
    w_qkv,
    resid_grad,
    logs,
    seg_col,
    seg_row,
    in_sums,
    shared_step,
):
    across = lay.features // LANES
    lines_half = 6 * across // MP
    assert lay.starts[SPLIT] >= lay.mats[1][0] > lay.starts[SPLIT - 1]
    assert lay.starts[SPLIT - 1] + lay.length <= lay.mats[1][0] + LANES * lay.mats[1][2]
    assert lay.bias_lines + lines_half == 36 and 2 * lay.head_cols // LANES == LATE_LINES
    assert lay.need % 16 + 3 <= 16 and lay.length * LANES - lay.shard >= 8 * LANES
    heads = 2 * lay.head_cols // LANES
    extra = jnp.concatenate(
        [
            jnp.zeros((MP, heads, LANES), jnp.float32),
            in_sums.reshape(MP, -1, LANES),
            shared_step.reshape(MP, lines_half, LANES),
            jnp.zeros((MP, 4, LANES), jnp.float32),
        ],
        1,
    )
    flat_rows = -(-(lay.starts[15] + lay.length - lay.mats[1][0]) // 8) * 8
    core_rows = qkv.shape[0]
    size = (lay.length, LANES)
    low, full = jnp.bfloat16, jnp.float32
    vmem = pl.BlockSpec(memory_space=pltpu.VMEM)
    anywhere = pl.BlockSpec(memory_space=pl.ANY)
    scratch = pltpu.VMEM
    lines, squares, shared_grad, input_grad = pl.pallas_call(
        partial(finish_kernel, lay),
        out_shape=[
            jax.ShapeDtypeStruct(size, full),
            jax.ShapeDtypeStruct((1, LANES), full),
            jax.ShapeDtypeStruct(shared_step.shape, full),
            jax.ShapeDtypeStruct((MP * core_rows, lay.features), full),
        ],
        in_specs=[anywhere] * 8 + [vmem] * 4,
        out_specs=[vmem] * 3 + [anywhere],
        scratch_shapes=[
            scratch((lay.features, lay.ffn_cols), low),
            scratch((lay.ffn_cols, lay.features), low),
            scratch((lay.head_cols, lay.features), low),
            scratch((flat_rows, LANES), full),
            scratch((MP, 16) + size, low),
            scratch((16,) + size, low),
            scratch((4,) + size, low),
            scratch((4,) + size, low),
            scratch((4, lay.cut, LANES), low),
            scratch((4, lay.cut, LANES), low),
            scratch((5,) + size, low),
            scratch(size, full),
            scratch((16 * MP, STAT_ROWS, LANES), full),
            scratch((MP, 40, LANES), full),
            scratch((16, LANES), full),
            scratch((ROW, qkv.shape[1]), low),
            scratch((ROW, lay.features), low),
            scratch((lay.features, core_rows), low),
            scratch(qkv.shape, low),
            scratch((ROW, lay.head_cols), full),
            scratch((ROW, lay.head_cols), full),
            scratch((2 * LANES, qkv.shape[1]), low),
            scratch((core_rows, 2 * LANES), full),
            DMA((3,)),
            DMA((6,)),
            DMA((16,)),
            DMA((16,)),
            DMA((4, PIECES)),
            DMA((4, PIECES)),
            DMA((4, PIECES)),
            DMA((4, PIECES)),
            DMA((4, 2)),
            DMA((4, 2)),
            DMA((4, PIECES)),
            DMA((5, PIECES)),
            DMA((16 * MP,)),
            DMA((16 * MP,)),
            DMA((3,)),
            DMA((3,)),
        ],
        compiler_params=pltpu.CompilerParams(
            collective_id=1, has_side_effects=True, vmem_limit_bytes=VMEM_MOST
        ),
        name="finish_step",
    )(
        *ffn_grads,
        w_attn_grad,
        qkv,
        mixed_grad,
        tokens_turned,
        w_qkv,
        resid_grad,
        logs,
        seg_col,
        window_segments(seg_row),
        extra,
    )
    return input_grad, lines.reshape(1, -1), squares[0, 0], shared_grad


def scatter_gradients(lay, grads, bias_grad, shared_step):
    phase = (lax.axis_index("dp") * lay.shard) % LANES
    packed = pack_gradients(lay, grads, bias_grad)
    flat = packed.reshape(MP * lay.dp_count * lay.length, LANES)
    lines = lax.psum_scatter(flat, ("mp", "dp"), scatter_dimension=0, tiled=True)
    lines = lines.astype(jnp.float32).reshape(-1) / LOSS_SCALE
    lines = jnp.roll(lines, -phase)
    lines = jnp.where(jnp.arange(lines.size) < lay.shard, lines, 0.0)
    shared_grad = lax.psum(shared_step, ("dp", "mp")) / LOSS_SCALE
    squares = lax.psum(jnp.sum(lines * lines), ("dp", "mp"))
    squares = squares + jnp.sum(shared_grad * shared_grad)
    return lines.reshape(1, -1), squares, shared_grad


def back_norm(values_in, scale_vec, grad):
    center = jnp.mean(values_in, -1, keepdims=True)
    centered = values_in - center
    inverse = lax.rsqrt(jnp.mean(centered * centered, -1, keepdims=True) + NORM_EPS)
    unit = centered * inverse
    scaled = grad * scale_vec
    out = inverse * (
        scaled
        - jnp.mean(scaled, -1, keepdims=True)
        - unit * jnp.mean(scaled * unit, -1, keepdims=True)
    )
    return out, jnp.sum(grad * unit, 0), jnp.sum(grad, 0)


def per_device(
    tokens,
    segments,
    sentence_dest,
    pair_source,
    labels,
    params,
    first,
    second,
    shared,
    shared_first,
    shared_second,
):
    features = tokens.shape[1]
    dp_count = lax.axis_size("dp")
    dp_index = lax.axis_index("dp")
    mp_index = lax.axis_index("mp")
    shard = params.shape[1]
    lay = Layout(features, shard, dp_count)
    head_cols = lay.head_cols
    sent_slots = ROWS_DEV * SEG
    slot_capacity = max(2, sent_slots // dp_count)
    params_total = MP * shard * dp_count + 6 * features
    core_rows = ROWS_CORE * ROW

    own = jnp.pad(params, ((0, 0), (0, lay.length * LANES - shard))).reshape(lay.length, LANES)
    tokens_core = lax.dynamic_slice_in_dim(tokens, mp_index * core_rows, core_rows, 0)
    segments_core = lax.dynamic_slice_in_dim(segments, mp_index * core_rows, core_rows, 0)
    seg_col = segments_core.reshape(core_rows, 1)
    seg_row = segments_core.reshape(ROWS_CORE, 1, ROW)
    head_lines = head_cols // LANES

    if dp_count == 16:
        w_qkv, w_attn, w_in, w_out, biases, qkv, mixed, logs = start_step(
            lay, own, tokens, seg_col, seg_row
        )
    else:
        w_qkv, w_attn, w_in, w_out, biases = unpack_weights(lay, gather_lines(lay, own))
        b_query = biases[:, :head_lines].reshape(MP, head_cols)
        b_value = biases[:, head_lines : 2 * head_lines].reshape(MP, head_cols)
        b_qkv = jnp.concatenate([b_query, jnp.zeros_like(b_query), b_value], 1).reshape(-1)
        qkv = jnp.dot(tokens_core, w_qkv, preferred_element_type=jnp.float32)
        qkv = (qkv + b_qkv).astype(jnp.bfloat16)
        mixed, logs = attend(qkv, seg_col, seg_row, head_cols)
    b_in = biases[:, 2 * head_lines : lay.bias_lines].reshape(MP * lay.ffn_cols)
    attn_out = jnp.dot(mixed, w_attn, preferred_element_type=jnp.float32) + shared[4]
    resid_one = tokens_core.astype(jnp.float32) + attn_out
    hidden = normalize(resid_one, shared[0], shared[1])
    hidden_low = hidden.astype(jnp.bfloat16)
    up_proj = jnp.dot(hidden_low, w_in, preferred_element_type=jnp.float32) + b_in
    cdf = 0.5 * (1.0 + lax.erf(up_proj * (0.5**0.5)))
    activated = (up_proj * cdf).astype(jnp.bfloat16)
    slope = (
        cdf + up_proj * jnp.exp(-0.5 * up_proj * up_proj) * ((2.0 * math.pi) ** -0.5)
    ).astype(jnp.bfloat16)
    ffn_out = jnp.dot(activated, w_out, preferred_element_type=jnp.float32) + shared[5]
    resid_two = hidden + ffn_out
    encoded_core = normalize(resid_two, shared[2], shared[3])

    slot_ids = jnp.arange(SEG, dtype=jnp.int32)
    onehot = (seg_row == slot_ids[None, :, None]).astype(jnp.float32)
    weight = onehot / jnp.sum(onehot, 2, keepdims=True)
    pooled_core = jnp.einsum(
        "kvf,kfo->kvo",
        weight,
        encoded_core.reshape(ROWS_CORE, ROW, features),
        precision=TOP_PRECISION,
    ).astype(jnp.bfloat16)
    pooled_grad, encoded = exchange(
        pooled_core.reshape(ROWS_CORE * SEG, features),
        encoded_core.astype(jnp.bfloat16),
        sentence_dest,
        pair_source,
        labels,
        dp_count,
        slot_capacity,
    )

    encoded_grad = jnp.einsum(
        "jix,jip->jxp",
        weight,
        pooled_grad.reshape(ROWS_CORE, SEG, features),
        precision=TOP_PRECISION,
    ).reshape(core_rows, features)
    resid_two_grad, scale_two, shift_two = back_norm(resid_two, shared[2], encoded_grad)
    ffn_grad = resid_two_grad.astype(jnp.bfloat16)
    act_grad = lax.dot_general(ffn_grad, w_out, LAST, preferred_element_type=jnp.float32)
    up_grad = (act_grad * slope.astype(jnp.float32)).astype(jnp.bfloat16)
    w_out_grad = lax.dot_general(activated, ffn_grad, FIRST, preferred_element_type=jnp.float32)
    w_in_grad = lax.dot_general(hidden_low, up_grad, FIRST, preferred_element_type=jnp.float32)
    hidden_term = lax.dot_general(up_grad, w_in, LAST, preferred_element_type=jnp.float32)
    hidden_grad = resid_two_grad + hidden_term
    resid_one_grad, scale_one, shift_one = back_norm(resid_one, shared[0], hidden_grad)
    attn_grad = resid_one_grad.astype(jnp.bfloat16)
    w_attn_grad = lax.dot_general(mixed, attn_grad, FIRST, preferred_element_type=jnp.float32)
    mixed_grad = lax.dot_general(
        attn_grad, w_attn, LAST, preferred_element_type=jnp.float32
    ).astype(jnp.bfloat16)
    in_sums = jnp.sum(up_grad.astype(jnp.float32), 0)
    shared_step = jnp.stack(
        [
            scale_one,
            shift_one,
            scale_two,
            shift_two,
            jnp.sum(attn_grad.astype(jnp.float32), 0),
            jnp.sum(ffn_grad.astype(jnp.float32), 0),
        ]
    )
    ffn_grads = [w_in_grad.astype(jnp.bfloat16), w_out_grad.astype(jnp.bfloat16)]
    w_attn_grad = w_attn_grad.astype(jnp.bfloat16)
    if dp_count == 16:
        input_grad, grad_lines, total_squares, shared_grad = finish_step(
            lay,
            ffn_grads,
            w_attn_grad,
            qkv,
            mixed_grad,
            tokens_core.T,
            w_qkv,
            resid_one_grad,
            logs,
            seg_col,
            seg_row,
            in_sums,
            shared_step,
        )
    else:
        qkv_grad = attend_back(qkv, mixed_grad, logs, seg_col, seg_row, head_cols)
        w_qkv_grad = lax.dot_general(
            tokens_core, qkv_grad, FIRST, preferred_element_type=jnp.float32
        ).astype(jnp.bfloat16)
        input_term = lax.dot_general(qkv_grad, w_qkv, LAST, preferred_element_type=jnp.float32)
        input_core = resid_one_grad + input_term
        qkv_sums = jnp.sum(qkv_grad.astype(jnp.float32), 0).reshape(MP, 3, head_lines, LANES)
        bias_grad = jnp.concatenate(
            [qkv_sums[:, 0], qkv_sums[:, 2], in_sums.reshape(MP, -1, LANES)], 1
        )
        bias_grad = jnp.pad(bias_grad, ((0, 0), (0, lay.bias_rows - lay.bias_lines), (0, 0)))
        grad_lines, total_squares, shared_grad = scatter_gradients(
            lay, [w_qkv_grad, w_attn_grad] + ffn_grads, bias_grad, shared_step
        )
        input_grad = lax.all_gather(input_core, "mp", axis=0, tiled=True)
    flat_grad = grad_lines[:, :shard]
    norm_value = jnp.sqrt(total_squares)
    factor = jnp.minimum(1.0, CLIP_NORM / norm_value)
    step_count = STEP_COUNT
    params_new, first_new, second_new = adamw(
        params, first, second, flat_grad, factor, step_count, LEARN_RATE
    )
    shared_new, shared_first_new, shared_second_new = adamw(
        shared, shared_first, shared_second, shared_grad, factor, step_count, SHARED_RATE
    )
    grad_unit = math.sqrt(params_total) / CLIP_NORM
    params_grad = flat_grad * factor * grad_unit
    shared_grad_out = shared_grad * factor * grad_unit
    return (
        encoded,
        input_grad,
        norm_value.reshape(1),
        params_new,
        first_new,
        second_new,
        params_new.astype(jnp.bfloat16),
        shared_new,
        shared_first_new,
        shared_second_new,
        params_grad,
        shared_grad_out,
    )


def solution(mesh):
    in_specs = (
        P("dp", None),
        P("dp"),
        P("dp", None),
        P("dp", None),
        P("dp"),
        P("mp", "dp"),
        P("mp", "dp"),
        P("mp", "dp"),
        P(),
        P(),
        P(),
    )
    out_specs = (
        P("dp", None),
        P("dp", None),
        P(),
        P("mp", "dp"),
        P("mp", "dp"),
        P("mp", "dp"),
        P("mp", "dp"),
        P(),
        P(),
        P(),
        P("mp", "dp"),
        P(),
    )
    return jax.shard_map(
        per_device, mesh=mesh, in_specs=in_specs, out_specs=out_specs, check_vma=False
    )
```

```python
from functools import partial
import math

import jax
import jax.numpy as jnp
from jax import lax
from jax.experimental import pallas as pl
from jax.experimental.pallas import tpu as pltpu
from jax.sharding import PartitionSpec as P

HEAD_DIM = 64
FF = 3072
ROW = 512
SEG = 32
RPM = 2
MB = 2
MP = 2
LANES = 128
ROWS_DEV = MB * RPM
ROWS_CORE = ROWS_DEV // MP


LOSS_SCALE = 1024.0
CLIP_NORM = 0.5
LEARN_RATE = 0.1
SHARED_RATE = 0.5
BETA_ONE = 0.9
BETA_TWO = 0.999
ADAM_EPS = 1e-08
DECAY = 0.01
NORM_EPS = 1e-12
STEP_COUNT = 10.0
TOP_PRECISION = lax.Precision.HIGHEST
MESH = pl.DeviceIdType.MESH
DMA = pltpu.SemaphoreType.DMA
VMEM_LIMIT = 60 << 20
VMEM_MOST = 62 << 20
PIECES = 4


def normalize(values_in, scale_vec, shift_vec):
    center = jnp.mean(values_in, -1, keepdims=True)
    centered = values_in - center
    spread = jnp.mean(centered * centered, -1, keepdims=True)
    return centered * lax.rsqrt(spread + NORM_EPS) * scale_vec + shift_vec


def pair_loss(pair_items, labels):
    first_vec = pair_items[..., 0::2, :]
    second_vec = pair_items[..., 1::2, :]
    inner_prod = jnp.sum(first_vec * second_vec, -1)
    cosine = (
        inner_prod
        * lax.rsqrt(jnp.sum(first_vec * first_vec, -1) + 1e-06)
        * lax.rsqrt(jnp.sum(second_vec * second_vec, -1) + 1e-06)
    )
    error_term = cosine - labels.astype(jnp.float32) / 5.0
    return LOSS_SCALE * jnp.sum(error_term * error_term)


def adamw(weight, moment_one, moment_two, gradient, factor, step_count, rate):
    clipped = gradient * factor
    first_new = BETA_ONE * moment_one + (1.0 - BETA_ONE) * clipped
    second_new = BETA_TWO * moment_two + (1.0 - BETA_TWO) * clipped * clipped
    first_hat = first_new / (1.0 - BETA_ONE**step_count)
    second_hat = second_new / (1.0 - BETA_TWO**step_count)
    weight_new = weight - rate * (first_hat / (jnp.sqrt(second_hat) + ADAM_EPS) + DECAY * weight)
    return (weight_new, first_new, second_new)


class Layout:
    def __init__(self, features, shard, dp_count):
        self.features = features
        self.shard = shard
        self.dp_count = dp_count
        self.head_cols = features // MP
        self.ffn_cols = FF // MP
        self.total = shard * dp_count
        self.lines = self.total // LANES
        assert self.lines * LANES == self.total
        self.starts = [index * shard // LANES for index in range(dp_count)]
        need = max(
            ((index + 1) * shard - 1) // LANES - index * shard // LANES + 1
            for index in range(dp_count)
        )
        self.need = need
        self.length = -(-(need + 3) // (16 * PIECES)) * (16 * PIECES)
        self.cut = self.length // 2
        self.piece = self.length // PIECES
        self.step = max(
            rows for rows in range(16, 257, 16) if self.piece % rows == 0
        )
        self.mats = []
        offset = 0
        for height, extent in (
            (features, 3 * self.head_cols),
            (self.head_cols, features),
            (features, self.ffn_cols),
            (self.ffn_cols, features),
        ):
            assert extent % LANES == 0 and height % LANES == 0
            self.mats.append((offset, height, extent // LANES))
            offset += height * (extent // LANES)
        self.bias_start = offset
        self.bias_lines = self.lines - offset
        self.bias_rows = -(-self.bias_lines // 8) * 8
        self.flat_rows = -(-(self.starts[-1] + self.length) // 8) * 8


def weight_specs(lay):
    specs = [
        pl.BlockSpec((lay.features, 3 * lay.head_cols), lambda half: (0, half)),
        pl.BlockSpec((lay.head_cols, lay.features), lambda half: (half, 0)),
        pl.BlockSpec((lay.features, lay.ffn_cols), lambda half: (0, half)),
        pl.BlockSpec((lay.ffn_cols, lay.features), lambda half: (half, 0)),
        pl.BlockSpec((1, lay.bias_rows, LANES), lambda half: (half, 0, 0)),
    ]
    shapes = [
        (lay.features, MP * 3 * lay.head_cols),
        (MP * lay.head_cols, lay.features),
        (lay.features, MP * lay.ffn_cols),
        (MP * lay.ffn_cols, lay.features),
    ]
    return specs, shapes


def unpack_kernel(lay, lines_ref, qkv_ref, attn_ref, in_ref, out_ref, bias_ref, flat):
    for index in range(lay.dp_count):
        start = lay.starts[index]
        if index > 0:
            kept = flat[start : start + 1, :]
        flat[start : start + lay.length, :] = lines_ref[0, index].astype(jnp.float32)
        if index > 0:
            flat[start : start + 1, :] += kept
    for (offset, height, cols), ref in zip(lay.mats, (qkv_ref, attn_ref, in_ref, out_ref)):

        def body(step, carry, offset=offset, cols=cols, ref=ref):
            row = pl.multiple_of(step * LANES, LANES)
            for col in range(cols):
                block = flat[pl.ds(offset + row * cols + col, LANES, stride=cols), :]
                ref[pl.ds(row, LANES), col * LANES : (col + 1) * LANES] = block.astype(
                    jnp.bfloat16
                )
            return carry

        lax.fori_loop(0, height // LANES, body, 0)
    bias_ref[0] = flat[lay.bias_start : lay.bias_start + lay.bias_rows, :]


def unpack_weights(lay, gathered):
    specs, shapes = weight_specs(lay)
    return pl.pallas_call(
        partial(unpack_kernel, lay),
        grid=(MP,),
        in_specs=[
            pl.BlockSpec((1, lay.dp_count, lay.length, LANES), lambda half: (half, 0, 0, 0))
        ],
        out_specs=specs,
        out_shape=[jax.ShapeDtypeStruct(s, jnp.bfloat16) for s in shapes]
        + [jax.ShapeDtypeStruct((MP, lay.bias_rows, LANES), jnp.float32)],
        scratch_shapes=[pltpu.VMEM((lay.flat_rows, LANES), jnp.float32)],
        compiler_params=pltpu.CompilerParams(vmem_limit_bytes=VMEM_LIMIT),
        name="unpack_weights",
    )(gathered)


def pack_kernel(lay, qkv_ref, attn_ref, in_ref, out_ref, bias_ref, lines_ref, flat):
    for (offset, height, cols), ref in zip(lay.mats, (qkv_ref, attn_ref, in_ref, out_ref)):

        def body(step, carry, offset=offset, cols=cols, ref=ref):
            row = pl.multiple_of(step * LANES, LANES)
            for col in range(cols):
                block = ref[pl.ds(row, LANES), col * LANES : (col + 1) * LANES]
                flat[pl.ds(offset + row * cols + col, LANES, stride=cols), :] = block.astype(
                    jnp.float32
                )
            return carry

        lax.fori_loop(0, height // LANES, body, 0)
    tail = lay.flat_rows - lay.lines
    if tail:
        flat[lay.lines :, :] = jnp.zeros((tail, LANES), jnp.float32)
    flat[lay.bias_start : lay.lines, :] = bias_ref[0, : lay.bias_lines]
    for index in range(lay.dp_count):
        start = lay.starts[index]
        lines_ref[0, index] = flat[start : start + lay.length, :].astype(jnp.bfloat16)


def pack_gradients(lay, grads, bias_grad):
    specs, _ = weight_specs(lay)
    return pl.pallas_call(
        partial(pack_kernel, lay),
        grid=(MP,),
        in_specs=specs,
        out_specs=pl.BlockSpec(
            (1, lay.dp_count, lay.length, LANES), lambda half: (half, 0, 0, 0)
        ),
        out_shape=jax.ShapeDtypeStruct((MP, lay.dp_count, lay.length, LANES), jnp.bfloat16),
        scratch_shapes=[pltpu.VMEM((lay.flat_rows, LANES), jnp.float32)],
        compiler_params=pltpu.CompilerParams(vmem_limit_bytes=VMEM_LIMIT),
        name="pack_gradients",
    )(*grads, bias_grad)


class Place:
    def __init__(self):
        self.dp = lax.axis_index("dp")
        self.half = lax.axis_index("mp")
        self.z = self.dp // 4
        self.y = (self.dp // 2) % 2
        self.x = self.dp % 2
        self.has_up = self.z < 3
        self.has_down = self.z > 0
        self.up = (jnp.minimum(self.dp + 4, 12 + self.dp % 4), self.half)
        self.down = (jnp.maximum(self.dp - 4, self.dp % 4), self.half)
        self.xn = (self.shard(self.z, self.y, 1 - self.x), self.half)
        self.yn = (self.shard(self.z, 1 - self.y, self.x), self.half)
        self.sib = (self.dp, 1 - self.half)

    def shard(self, z, y, x):
        return z * 4 + y * 2 + x

    def barrier(self):
        bar = pltpu.get_barrier_semaphore()
        for dev in (self.xn, self.yn, self.sib):
            pl.semaphore_signal(bar, inc=1, device_id=dev, device_id_type=MESH)

        @pl.when(self.has_up)
        def _():
            pl.semaphore_signal(bar, inc=1, device_id=self.up, device_id_type=MESH)

        @pl.when(self.has_down)
        def _():
            pl.semaphore_signal(bar, inc=1, device_id=self.down, device_id_type=MESH)

        pl.semaphore_wait(
            bar, 3 + jnp.where(self.has_up, 1, 0) + jnp.where(self.has_down, 1, 0)
        )


def guarded(cond, work):
    if cond is None:
        work()
    else:
        pl.when(cond)(work)


def lane_ids(rows):
    return lax.broadcasted_iota(jnp.int32, (rows, LANES), 1)


def shift_into_lines(lay, own_ref, rolled, put):
    phase = lax.rem(lax.axis_index("dp") * lay.shard, LANES)
    rows = lay.length
    rolled[0:8, :] = jnp.zeros((8, LANES), jnp.float32)
    rolled[8 : 8 + rows, :] = pltpu.roll(own_ref[...], phase, 1)
    late = rolled[7 : 7 + rows, :]
    put(jnp.where(lane_ids(rows) < phase, late, rolled[8 : 8 + rows, :]))


def gather_lines(lay, own):
    flat = own.reshape(-1)
    phase = (lax.axis_index("dp") * lay.shard) % LANES
    own = jnp.roll(flat, phase).reshape(lay.length, LANES).astype(jnp.bfloat16)
    gathered = lax.all_gather(own, ("mp", "dp"), axis=0, tiled=True)
    return gathered.reshape(MP, lay.dp_count, lay.length, LANES)


def exchange_kernel(
    pooled_ref,
    codes_ref,
    labels_ref,
    core_ref,
    grad_ref,
    encoded_hbm,
    pooled,
    outgoing,
    incoming,
    returning,
    arrived,
    sib_sem,
    go_send,
    go_recv,
    back_send,
    back_recv,
    enc_sem,
):
    dp = lax.axis_index("dp")
    half = lax.axis_index("mp")
    sib = (dp, 1 - half)
    slots, capacity, features = outgoing.shape
    codes = slots * capacity
    core_sents = pooled_ref.shape[0]

    def peer(step):
        return (lax.rem(dp + step, slots), half)

    bar = pltpu.get_barrier_semaphore()
    pl.semaphore_signal(bar, inc=1, device_id=sib, device_id_type=MESH)
    for step in range(1, slots):
        pl.semaphore_signal(bar, inc=1, device_id=peer(step), device_id_type=MESH)
    pooled[half] = pooled_ref[...]
    pl.semaphore_wait(bar, slots)
    share = pltpu.make_async_remote_copy(
        src_ref=pooled_ref,
        dst_ref=pooled.at[half],
        send_sem=sib_sem.at[0],
        recv_sem=sib_sem.at[1],
        device_id=sib,
        device_id_type=MESH,
    )
    share.start()
    core_rows = core_ref.shape[0]
    place = encoded_hbm.at[pl.ds(pl.multiple_of(half * core_rows, 16), core_rows)]
    keep = pltpu.make_async_copy(core_ref, place, enc_sem.at[2])
    give = pltpu.make_async_remote_copy(
        src_ref=core_ref,
        dst_ref=place,
        send_sem=enc_sem.at[0],
        recv_sem=enc_sem.at[1],
        device_id=sib,
        device_id_type=MESH,
    )
    keep.start()
    give.start()

    code_ids = lax.broadcasted_iota(jnp.int32, (codes, codes), 0)
    send_map = (code_ids == codes_ref[0:1, :]).astype(jnp.bfloat16)
    pairs = codes // 2
    even_map = (code_ids[:, :pairs] == codes_ref[1:2, :pairs]).astype(jnp.bfloat16)
    odd_map = (code_ids[:, :pairs] == codes_ref[2:3, :pairs]).astype(jnp.bfloat16)
    share.wait()
    everything = jnp.concatenate([pooled[0], pooled[1]], 0)
    out = jnp.dot(send_map, everything, preferred_element_type=jnp.float32)
    outgoing[...] = out.reshape(outgoing.shape).astype(jnp.bfloat16)

    def copy(src, dst, send_sem, recv_sem, step):
        return pltpu.make_async_remote_copy(
            src_ref=src,
            dst_ref=dst,
            send_sem=send_sem.at[step],
            recv_sem=recv_sem.at[step],
            device_id=peer(step),
            device_id_type=MESH,
        )

    def all_to_all(src, dst, send_sem, recv_sem):
        for step in range(1, slots):
            copy(src.at[lax.rem(dp + step, slots)], dst.at[dp], send_sem, recv_sem, step).start()
        dst[dp] = src[dp]
        for step in range(1, slots):
            sender = lax.rem(dp + slots - step, slots)
            copy(src.at[sender], dst.at[sender], send_sem, recv_sem, step).wait()

    all_to_all(outgoing, incoming, go_send, go_recv)
    items = incoming[...].astype(jnp.float32).reshape(codes, features).astype(jnp.bfloat16)
    left = lax.dot_general(even_map, items, FIRST, preferred_element_type=jnp.float32)
    right = lax.dot_general(odd_map, items, FIRST, preferred_element_type=jnp.float32)
    inner = jnp.sum(left * right, -1, keepdims=True)
    left_inv = lax.rsqrt(jnp.sum(left * left, -1, keepdims=True) + 1e-06)
    right_inv = lax.rsqrt(jnp.sum(right * right, -1, keepdims=True) + 1e-06)
    both = left_inv * right_inv
    cosine = inner * both
    square = (pairs, pairs)
    eye = lax.broadcasted_iota(jnp.int32, square, 0) == lax.broadcasted_iota(
        jnp.int32, square, 1
    )
    target = jnp.sum(
        jnp.where(eye, labels_ref[0:1, :pairs].astype(jnp.float32), 0.0), 1, keepdims=True
    )
    slope = (2.0 * LOSS_SCALE) * (cosine - target / 5.0)
    left_grad = slope * (both * right - (cosine * left_inv * left_inv) * left)
    right_grad = slope * (both * left - (cosine * right_inv * right_inv) * right)
    back = jnp.dot(
        even_map, left_grad.astype(jnp.bfloat16), preferred_element_type=jnp.float32
    ) + jnp.dot(odd_map, right_grad.astype(jnp.bfloat16), preferred_element_type=jnp.float32)
    returning[...] = back.reshape(returning.shape).astype(jnp.bfloat16)
    all_to_all(returning, arrived, back_send, back_recv)
    items = arrived[...].astype(jnp.float32).reshape(codes, features).astype(jnp.bfloat16)
    grads = lax.dot_general(send_map, items, FIRST, preferred_element_type=jnp.float32)
    grad_ref[...] = jnp.where(half == 0, grads[:core_sents], grads[core_sents:])
    keep.wait()
    give.wait()


def exchange(
    pooled_core, encoded_core, sentence_dest, pair_source, labels, dp_count, capacity
):
    core_sents, features = pooled_core.shape
    codes = dp_count * capacity
    send_code = sentence_dest[:, 0] * capacity + sentence_dest[:, 1]
    take_code = pair_source[:, 0] * capacity + pair_source[:, 1]
    if dp_count == 16 and codes == send_code.shape[0] == 2 * core_sents:
        pairs = take_code.reshape(-1, 2).T
        pairs = jnp.pad(pairs, ((0, 0), (0, codes - pairs.shape[1])))
        table = jnp.concatenate([send_code[None], pairs, jnp.zeros((5, codes), jnp.int32)], 0)
        wide = (dp_count, capacity, features)
        low = jnp.bfloat16
        anywhere = pl.BlockSpec(memory_space=pl.ANY)
        vmem = pl.BlockSpec(memory_space=pltpu.VMEM)
        return pl.pallas_call(
            exchange_kernel,
            out_shape=[
                jax.ShapeDtypeStruct((core_sents, features), jnp.float32),
                jax.ShapeDtypeStruct((MP * encoded_core.shape[0], features), low),
            ],
            in_specs=[vmem] * 4,
            out_specs=[vmem, anywhere],
            scratch_shapes=[pltpu.VMEM((MP, core_sents, features), low)]
            + [pltpu.VMEM(wide, low)] * 4
            + [DMA((2,))]
            + [DMA((dp_count,))] * 4
            + [DMA((3,))],
            compiler_params=pltpu.CompilerParams(
                collective_id=2, has_side_effects=True, vmem_limit_bytes=VMEM_LIMIT
            ),
            name="exchange_pairs",
        )(pooled_core, table, labels[None], encoded_core)
    encoded = lax.all_gather(encoded_core, "mp", axis=0, tiled=True)
    mp_index = lax.axis_index("mp")
    pooled_flat = lax.all_gather(pooled_core, "mp", axis=0, tiled=True)
    code_ids = jnp.arange(codes, dtype=jnp.int32)
    send_map = (code_ids[:, None] == send_code[None, :]).astype(jnp.bfloat16)
    outgoing = jnp.dot(send_map, pooled_flat, preferred_element_type=jnp.float32).astype(
        jnp.bfloat16
    )
    outgoing = outgoing.reshape(dp_count, capacity, features)
    incoming = lax.all_to_all(outgoing, "dp", split_axis=0, concat_axis=0, tiled=True).reshape(
        codes, features
    )
    take_map = (take_code[:, None] == code_ids[None, :]).astype(jnp.bfloat16)
    pair_items = jnp.dot(take_map, incoming, preferred_element_type=jnp.float32)
    item_grad = jax.grad(pair_loss)(pair_items, labels).astype(jnp.bfloat16)
    returning = jnp.dot(take_map.T, item_grad, preferred_element_type=jnp.float32).astype(
        jnp.bfloat16
    )
    returning = returning.reshape(dp_count, capacity, features)
    arrived = lax.all_to_all(returning, "dp", split_axis=0, concat_axis=0, tiled=True).reshape(
        codes, features
    )
    core_map = lax.dynamic_slice_in_dim(send_map, mp_index * core_sents, core_sents, 1)
    return jnp.dot(core_map.T, arrived, preferred_element_type=jnp.float32), encoded


SCORE_SCALE = HEAD_DIM ** (-0.5)
LAST = (((1,), (1,)), ((), ()))
FIRST = (((0,), (0,)), ((), ()))


def low_lanes(rows):
    return lax.broadcasted_iota(jnp.int32, (rows, LANES), 1) < HEAD_DIM


def one_head(tile, odd):
    mask = low_lanes(tile.shape[0])
    if odd:
        return jnp.where(mask, jnp.zeros_like(tile), tile)
    return jnp.where(mask, tile, jnp.zeros_like(tile))


def attend_row(tiles, qkv_ref, seg_col_ref, seg_row_ref, out_ref, log_ref):
    width = tiles * LANES
    bias = jnp.where(seg_col_ref[...] == seg_row_ref[...], 0.0, -1e30)
    logs = []
    for tile in range(tiles):
        cols = slice(tile * LANES, (tile + 1) * LANES)
        queries = qkv_ref[:, cols] * SCORE_SCALE
        keys = qkv_ref[:, width + tile * LANES : width + (tile + 1) * LANES]
        values = qkv_ref[:, 2 * width + tile * LANES : 2 * width + (tile + 1) * LANES]
        mixed = []
        for odd in range(2):
            scores = lax.dot_general(
                one_head(queries, odd), keys, LAST, preferred_element_type=jnp.float32
            )
            scores = scores + bias
            row_max = jnp.max(scores, -1, keepdims=True)
            exponent = jnp.exp(scores - row_max)
            row_total = jnp.sum(exponent, -1, keepdims=True)
            probs = exponent.astype(jnp.bfloat16)
            mixed.append(
                jnp.dot(probs, values, preferred_element_type=jnp.float32) * (1.0 / row_total)
            )
            logs.append(row_max + jnp.log(row_total))
        both = jnp.where(low_lanes(ROW), mixed[0], mixed[1])
        out_ref[:, cols] = both.astype(jnp.bfloat16)
    log_ref[...] = jnp.concatenate(logs + [logs[0]] * (8 - 2 * tiles), 1)


def attend_kernel(tiles, qkv_ref, seg_col_ref, seg_row_ref, out_ref, log_ref):
    attend_row(tiles, qkv_ref, seg_col_ref, seg_row_ref.at[0], out_ref, log_ref.at[0])


def attend(qkv, seg_col, seg_row, head_cols):
    rows = qkv.shape[0] // ROW
    return pl.pallas_call(
        partial(attend_kernel, head_cols // LANES),
        grid=(rows, MP),
        in_specs=[
            pl.BlockSpec((ROW, 3 * head_cols), lambda r, m: (r, m)),
            pl.BlockSpec((ROW, 1), lambda r, m: (r, 0)),
            pl.BlockSpec((1, 1, ROW), lambda r, m: (r, 0, 0)),
        ],
        out_specs=[
            pl.BlockSpec((ROW, head_cols), lambda r, m: (r, m)),
            pl.BlockSpec((1, ROW, 8), lambda r, m: (m, r, 0)),
        ],
        out_shape=[
            jax.ShapeDtypeStruct((rows * ROW, MP * head_cols), jnp.bfloat16),
            jax.ShapeDtypeStruct((MP, rows * ROW, 8), jnp.float32),
        ],
        compiler_params=pltpu.CompilerParams(vmem_limit_bytes=VMEM_LIMIT),
        name="attend",
    )(qkv, seg_col, seg_row)


def attend_back_row(
    tiles, qkv_ref, grad_ref, log_ref, seg_col_ref, seg_wide_ref, out_ref, key_acc, value_acc
):
    width = tiles * LANES
    block, window = LANES, 2 * LANES
    key_acc[...] = jnp.zeros_like(key_acc)
    value_acc[...] = jnp.zeros_like(value_acc)
    for step in range(ROW // block):
        start = min(max(step * block - block // 2, 0), ROW - window)
        rows = slice(step * block, (step + 1) * block)
        span = slice(start, start + window)
        bias = jnp.where(seg_col_ref[rows, :] == seg_wide_ref[step], 0.0, -1e30)
        for tile in range(tiles):
            cols = slice(tile * LANES, (tile + 1) * LANES)
            queries = qkv_ref[rows, cols] * SCORE_SCALE
            keys = qkv_ref[span, width + tile * LANES : width + (tile + 1) * LANES]
            values = qkv_ref[span, 2 * width + tile * LANES : 2 * width + (tile + 1) * LANES]
            mixed_grad = grad_ref[rows, cols]
            query_grad = key_grad = value_grad = 0.0
            for odd in range(2):
                head = 2 * tile + odd
                query_one = one_head(queries, odd)
                grad_one = one_head(mixed_grad, odd)
                scores = lax.dot_general(
                    query_one, keys, LAST, preferred_element_type=jnp.float32
                )
                probs = jnp.exp((scores + bias) - log_ref[rows, head : head + 1])
                prob_grad = lax.dot_general(
                    grad_one, values, LAST, preferred_element_type=jnp.float32
                )
                row_inner = jnp.sum(prob_grad * probs, -1, keepdims=True)
                score_grad = (probs * (prob_grad - row_inner)).astype(jnp.bfloat16)
                value_grad += lax.dot_general(
                    probs.astype(jnp.bfloat16),
                    grad_one,
                    FIRST,
                    preferred_element_type=jnp.float32,
                )
                query_grad += jnp.dot(
                    score_grad, one_head(keys, odd), preferred_element_type=jnp.float32
                )
                key_grad += lax.dot_general(
                    score_grad, query_one, FIRST, preferred_element_type=jnp.float32
                )
            out_ref[rows, cols] = (query_grad * SCORE_SCALE).astype(jnp.bfloat16)
            key_acc[span, cols] += key_grad
            value_acc[span, cols] += value_grad
    out_ref[:, width : 2 * width] = key_acc[...].astype(jnp.bfloat16)
    out_ref[:, 2 * width :] = value_acc[...].astype(jnp.bfloat16)


def attend_back_kernel(
    tiles, qkv_ref, grad_ref, log_ref, seg_col_ref, seg_wide_ref, out_ref, key_acc, value_acc
):
    attend_back_row(
        tiles,
        qkv_ref,
        grad_ref,
        log_ref.at[0],
        seg_col_ref,
        seg_wide_ref.at[0],
        out_ref,
        key_acc,
        value_acc,
    )


def window_segments(seg_row):
    window = 2 * LANES
    starts = [
        min(max(step * LANES - LANES // 2, 0), ROW - window) for step in range(ROW // LANES)
    ]
    return jnp.stack([seg_row[:, :, start : start + window] for start in starts], 1)


def attend_back(qkv, mixed_grad, logs, seg_col, seg_row, head_cols):
    rows = qkv.shape[0] // ROW
    window = 2 * LANES
    seg_wide = window_segments(seg_row)
    return pl.pallas_call(
        partial(attend_back_kernel, head_cols // LANES),
        grid=(rows, MP),
        in_specs=[
            pl.BlockSpec((ROW, 3 * head_cols), lambda r, m: (r, m)),
            pl.BlockSpec((ROW, head_cols), lambda r, m: (r, m)),
            pl.BlockSpec((1, ROW, 8), lambda r, m: (m, r, 0)),
            pl.BlockSpec((ROW, 1), lambda r, m: (r, 0)),
            pl.BlockSpec((1, ROW // LANES, 1, window), lambda r, m: (r, 0, 0, 0)),
        ],
        out_specs=pl.BlockSpec((ROW, 3 * head_cols), lambda r, m: (r, m)),
        out_shape=jax.ShapeDtypeStruct(qkv.shape, jnp.bfloat16),
        scratch_shapes=[pltpu.VMEM((ROW, head_cols), jnp.float32)] * 2,
        compiler_params=pltpu.CompilerParams(vmem_limit_bytes=VMEM_LIMIT),
        name="attend_back",
    )(qkv, mixed_grad, logs, seg_col, seg_wide)


PARTS = 4
BIAS_ROWS = 32


def start_kernel(
    lay,
    own_ref,
    tokens_hbm,
    seg_col_ref,
    seg_row_ref,
    qkv_weight_hbm,
    attn_weight_hbm,
    in_weight_hbm,
    out_weight_hbm,
    bias_ref,
    qkv_hbm,
    mixed_hbm,
    log_ref,
    buf,
    rolled,
    flat,
    biases,
    tokens,
    qkv_weight,
    attn_weight,
    in_weight,
    out_weight,
    qkv,
    mixed,
    load_sem,
    store_sem,
    zs_sem,
    zr_sem,
    xs_sem,
    xr_sem,
    ys_sem,
    yr_sem,
    ss_sem,
    sr_sem,
    bs_sem,
    br_sem,
):
    at = Place()
    other_half = 1 - at.half
    width = 3 * lay.head_cols
    me = at.dp * MP + at.half
    count = 16 * MP
    last = 15
    bias_from = lay.bias_start - lay.starts[last]
    core_rows = tokens.shape[0]

    load_tokens = pltpu.make_async_copy(
        tokens_hbm.at[pl.ds(pl.multiple_of(at.half * core_rows, 16), core_rows)], tokens, load_sem
    )
    load_tokens.start()

    def peer(step):
        other = lax.rem(me + step, count)
        return (other // MP, lax.rem(other, MP))

    bar = pltpu.get_barrier_semaphore()

    def greet(step, carry):
        pl.semaphore_signal(bar, inc=1, device_id=peer(step), device_id_type=MESH)
        return carry

    lax.fori_loop(1, count, greet, 0)

    def put(lines):
        buf[at.half, at.dp] = lines.astype(jnp.bfloat16)

    shift_into_lines(lay, own_ref, rolled, put)
    pl.semaphore_wait(bar, count - 1)
    sends = []

    def remote(src, dst, send_sem, recv_sem, dev):
        return pltpu.make_async_remote_copy(
            src_ref=src,
            dst_ref=dst,
            send_sem=send_sem,
            recv_sem=recv_sem,
            device_id=dev,
            device_id_type=MESH,
        )

    def bias_out(step):
        return remote(
            buf.at[at.half, last, pl.ds(bias_from, BIAS_ROWS)],
            biases.at[at.half],
            bs_sem.at[step],
            br_sem.at[at.half],
            peer(step),
        )

    @pl.when(at.dp == last)
    def _():
        def go(step, carry):
            bias_out(step).start()
            return carry

        lax.fori_loop(1, count, go, 0)
        biases[at.half] = buf[at.half, last, bias_from : bias_from + BIAS_ROWS, :]

    def wait_biases():
        for half in range(MP):

            @pl.when((at.dp != last) | (at.half != half))
            def _(half=half):
                remote(
                    buf.at[half, last, pl.ds(bias_from, BIAS_ROWS)],
                    biases.at[half],
                    bs_sem.at[0],
                    br_sem.at[half],
                    at.sib,
                ).wait_recv()

    def wait_bias_sends():
        @pl.when(at.dp == last)
        def _():
            def done(step, carry):
                bias_out(step).wait_send()
                return carry

            lax.fori_loop(1, count, done, 0)

    def move(index, part, send_sem, recv_sem, dev, half=None):
        rows = lay.length // PARTS
        piece = buf.at[at.half if half is None else half, index, pl.ds(part * rows, rows)]
        return remote(piece, piece, send_sem, recv_sem, dev)

    def send(index, part, send_sem, recv_sem, dev, cond=None):
        guarded(cond, lambda: move(index, part, send_sem, recv_sem, dev).start())
        sends.append((cond, lambda: move(index, part, send_sem, recv_sem, dev).wait_send()))

    def share(index, part, cond=None):
        send(index, part, ss_sem.at[index, part], sr_sem.at[index, part], at.sib, cond)

    def up(group, part, cond):
        index = at.shard(group, at.y, at.x)
        send(index, part, zs_sem.at[0, group, part], zr_sem.at[group, part], at.up, cond)

    def down(group, part, cond):
        index = at.shard(group, at.y, at.x)
        send(index, part, zs_sem.at[1, group, part], zr_sem.at[group, part], at.down, cond)

    def spread(group, part):
        index = at.shard(group, at.y, at.x)
        send(index, part, xs_sem.at[group, part], xr_sem.at[group, part], at.xn)
        send(index, part, ys_sem.at[group, part], yr_sem.at[group, part], at.yn)
        share(index, part)

    turns = (
        at.z,
        jnp.where(at.z == 0, 1, 0),
        jnp.where(at.z <= 1, 2, 1),
        jnp.where(at.z == 3, 2, 3),
    )

    def wait_along(group, part):
        index = at.shard(group, at.y, at.x)
        move(
            index, part, zs_sem.at[0, group, part], zr_sem.at[group, part], at.sib
        ).wait_recv()

    def along(turn):
        group = turns[turn]
        for part in range(PARTS):
            if turn < 3:
                wait_along(group, part)
                up(group, part, (group < at.z) & at.has_up)
                down(group, part, (group > at.z) & at.has_down)
            else:
                guarded((at.z == 0) | (at.z == 3), lambda part=part: wait_along(group, part))
            spread(group, part)

    def relay(z):
        for part in range(PARTS):
            guarded(at.z == z, lambda part=part: wait_along(3, part))
            down(3, part, at.z == z)

    def plane(turn):
        group = turns[turn]
        for part in range(PARTS):
            from_x = at.shard(group, at.y, 1 - at.x)
            from_y = at.shard(group, 1 - at.y, at.x)
            move(
                from_x, part, xs_sem.at[group, part], xr_sem.at[group, part], at.xn
            ).wait_recv()
            if part < PARTS // 2:
                slot = PARTS + part
                send(from_x, part, ys_sem.at[group, slot], yr_sem.at[group, slot], at.yn)
            share(from_x, part)
            move(
                from_y, part, ys_sem.at[group, part], yr_sem.at[group, part], at.yn
            ).wait_recv()
            if part >= PARTS // 2:
                slot = PARTS // 2 + part
                send(from_y, part, xs_sem.at[group, slot], xr_sem.at[group, slot], at.xn)
            share(from_y, part)

    def diagonal(turn):
        group = turns[turn]
        index = at.shard(group, 1 - at.y, 1 - at.x)
        for part in range(PARTS):
            if part < PARTS // 2:
                slot = PARTS + part
                move(
                    index, part, ys_sem.at[group, slot], yr_sem.at[group, slot], at.yn
                ).wait_recv()
            else:
                slot = PARTS // 2 + part
                move(
                    index, part, xs_sem.at[group, slot], xr_sem.at[group, slot], at.xn
                ).wait_recv()
            share(index, part)

    def wait_shared(groups):
        for index in range(4 * groups[0], 4 * groups[-1] + 4):
            for part in range(PARTS):
                move(
                    index,
                    part,
                    ss_sem.at[index, part],
                    sr_sem.at[index, part],
                    at.sib,
                    other_half,
                ).wait_recv()

    stores = []

    def store(src, dst):
        copy = pltpu.make_async_copy(src, dst, store_sem.at[len(stores)])
        copy.start()
        stores.append(copy)

    def to_lines(half, shards):
        base = lay.starts[shards[0]]
        for index in shards:
            start = lay.starts[index] - base
            if index > shards[0]:
                kept = flat[start : start + 1, :]
            flat[start : start + lay.length, :] = buf[half, index].astype(jnp.float32)
            if index > shards[0]:
                flat[start : start + 1, :] += kept
        return base

    def to_matrix(base, which, ref, row_at, col_at, first_row, rows):
        offset, _, cols = lay.mats[which]

        def body(step, carry):
            row = pl.multiple_of(first_row + step * LANES, LANES)
            dst = pl.ds(pl.multiple_of(row_at + row, LANES), LANES)
            for col in range(cols):
                block = flat[pl.ds(offset - base + row * cols + col, LANES, stride=cols), :]
                lanes = pl.ds(pl.multiple_of(col_at + col * LANES, LANES), LANES)
                ref[dst, lanes] = block.astype(jnp.bfloat16)
            return carry

        lax.fori_loop(0, rows // LANES, body, 0)

    features = lay.features
    halves = (at.half, other_half)

    def stage_one(half):
        base = to_lines(half, range(0, 4))
        to_matrix(base, 0, qkv_weight, 0, half * width, 0, features)

    cut_rows = (lay.starts[8] - lay.mats[2][0]) // lay.mats[2][2] // LANES * LANES

    def stage_two(half):
        base = to_lines(half, range(3, 8))
        to_matrix(base, 1, attn_weight, half * lay.head_cols, 0, 0, lay.head_cols)
        to_matrix(base, 2, in_weight, 0, half * lay.ffn_cols, 0, cut_rows)

    def stage_three(half):
        base = to_lines(half, range(7, 16))
        to_matrix(base, 2, in_weight, 0, half * lay.ffn_cols, cut_rows, features - cut_rows)
        later_rows = pl.ds(cut_rows, features - cut_rows)
        cols = pl.ds(pl.multiple_of(half * lay.ffn_cols, LANES), lay.ffn_cols)
        store(in_weight.at[later_rows, cols], in_weight_hbm.at[later_rows, cols])
        to_matrix(base, 3, out_weight, half * lay.ffn_cols, 0, 0, lay.ffn_cols)
        rows = pl.ds(pl.multiple_of(half * lay.ffn_cols, LANES), lay.ffn_cols)
        store(out_weight.at[rows], out_weight_hbm.at[rows])

    tiles = lay.head_cols // LANES

    def project(row, half):
        rows = pl.ds(row * ROW, ROW)
        cols = pl.ds(half * width, width)
        lines = biases[half].astype(jnp.float32)
        bias = jnp.concatenate(
            [lines[tile : tile + 1] for tile in range(tiles)]
            + [jnp.zeros((1, lay.head_cols), jnp.float32)]
            + [lines[tiles + tile : tiles + tile + 1] for tile in range(tiles)],
            1,
        )
        value = jnp.dot(tokens[rows, :], qkv_weight[:, cols], preferred_element_type=jnp.float32)
        qkv[rows, cols] = (value + bias).astype(jnp.bfloat16)

    def attention(row, half):
        rows = pl.ds(row * ROW, ROW)
        attend_row(
            tiles,
            qkv.at[rows, pl.ds(half * width, width)],
            seg_col_ref.at[rows],
            seg_row_ref.at[row],
            mixed.at[rows, pl.ds(half * lay.head_cols, lay.head_cols)],
            log_ref.at[half, rows],
        )

    for part in range(PARTS):
        spread(at.z, part)
        down(at.z, part, at.has_down)
        up(at.z, part, at.z == 0)
    along(1)
    for part in range(PARTS):
        up(at.z, part, at.z == 1)
    relay(2)
    plane(0)
    along(2)
    for part in range(PARTS):
        up(at.z, part, at.z == 2)
    diagonal(0)
    plane(1)
    relay(1)
    diagonal(1)
    load_tokens.wait()
    stage_one(halves[0])
    wait_shared((0,))
    stage_one(halves[1])
    store(qkv_weight, qkv_weight_hbm)
    wait_biases()
    along(3)
    project(0, 0)
    project(0, 1)
    plane(2)
    project(1, 0)
    project(1, 1)
    store(qkv, qkv_hbm)
    diagonal(2)
    attention(0, 0)
    wait_shared((1,))
    for half in halves:
        stage_two(half)
    store(attn_weight, attn_weight_hbm)
    store(in_weight.at[pl.ds(0, cut_rows)], in_weight_hbm.at[pl.ds(0, cut_rows)])
    attention(0, 1)
    plane(3)
    attention(1, 0)
    diagonal(3)
    attention(1, 1)
    store(mixed, mixed_hbm)
    stage_three(halves[0])
    wait_shared((2, 3))
    stage_three(halves[1])
    for half in range(MP):
        bias_ref[half] = biases[half].astype(jnp.float32)
    wait_bias_sends()
    for cond, work in sends:
        guarded(cond, work)
    for copy in stores:
        copy.wait()


def start_step(lay, own, tokens, seg_col, seg_row):
    core_rows = seg_col.shape[0]
    features, width = lay.features, 3 * lay.head_cols
    assert lay.starts[4] >= lay.mats[1][0] and lay.starts[3] <= lay.mats[1][0]
    assert lay.starts[8] >= lay.mats[2][0] and lay.bias_lines <= BIAS_ROWS
    assert (lay.bias_start - lay.starts[15]) % 16 == 0
    assert lay.bias_start - lay.starts[15] + BIAS_ROWS <= lay.length
    low, full = jnp.bfloat16, jnp.float32
    flat_rows = max(
        lay.starts[high] - lay.starts[first] + lay.length
        for first, high in ((0, 3), (3, 7), (7, 15))
    )
    flat_rows = -(-flat_rows // 8) * 8
    vmem = pl.BlockSpec(memory_space=pltpu.VMEM)
    anywhere = pl.BlockSpec(memory_space=pl.ANY)
    shape = jax.ShapeDtypeStruct
    weights = [
        (features, MP * width),
        (features, features),
        (features, MP * lay.ffn_cols),
        (MP * lay.ffn_cols, features),
    ]
    acts = [(core_rows, MP * width), (core_rows, features)]
    scratch = pltpu.VMEM
    return pl.pallas_call(
        partial(start_kernel, lay),
        out_shape=[shape(size, low) for size in weights]
        + [shape((MP, BIAS_ROWS, LANES), full)]
        + [shape(size, low) for size in acts]
        + [shape((MP, core_rows, 8), full)],
        in_specs=[vmem, anywhere, vmem, vmem],
        out_specs=[anywhere] * 4 + [vmem] + [anywhere] * 2 + [vmem],
        scratch_shapes=[
            scratch((MP, 16, lay.length, LANES), low),
            scratch((lay.length + 8, LANES), full),
            scratch((flat_rows, LANES), full),
            scratch((MP, BIAS_ROWS, LANES), low),
            scratch((core_rows, features), low),
        ]
        + [scratch(size, low) for size in weights + acts]
        + [
            DMA,
            DMA((12,)),
            DMA((2, 4, PARTS)),
            DMA((4, PARTS)),
            DMA((4, 2 * PARTS)),
            DMA((4, 2 * PARTS)),
            DMA((4, 2 * PARTS)),
            DMA((4, 2 * PARTS)),
            DMA((16, PARTS)),
            DMA((16, PARTS)),
            DMA((16 * MP,)),
            DMA((MP,)),
        ],
        compiler_params=pltpu.CompilerParams(
            collective_id=0, has_side_effects=True, vmem_limit_bytes=VMEM_MOST
        ),
        name="start_step",
    )(own, tokens, seg_col, seg_row)


STAT_ROWS = 4
SPLIT = 4
LATE_LINES = 6


def extra_lines(index):
    if index < SPLIT:
        return (2 * index, 2) if 2 * index < LATE_LINES else (0, 0)
    first = LATE_LINES + 3 * (index - SPLIT)
    return (first, 3) if first < 36 else (0, 0)


def extra_place(place):
    if place < LATE_LINES:
        return place // 2, 1 + place % 2
    return SPLIT + (place - LATE_LINES) // 3, 1 + (place - LATE_LINES) % 3


def finish_kernel(
    lay,
    in_hbm,
    out_hbm,
    attn_hbm,
    qkv_hbm,
    mixed_hbm,
    tokens_hbm,
    weight_hbm,
    resid_hbm,
    logs_ref,
    seg_col_ref,
    seg_wide_ref,
    extra_ref,
    grad_ref,
    norm_ref,
    shared_ref,
    input_hbm,
    staged_in,
    staged_out,
    staged_attn,
    flat,
    part,
    from_sib,
    from_x,
    from_y,
    diag_x,
    diag_y,
    from_z,
    total,
    stats,
    extras,
    tail,
    qkv,
    mixed,
    tokens,
    qkv_grad,
    key_acc,
    value_acc,
    weight,
    resid,
    load_sem,
    row_sem,
    ss_sem,
    sr_sem,
    xs_sem,
    xr_sem,
    ys_sem,
    yr_sem,
    dx_sem,
    dy_sem,
    zs_sem,
    zr_sem,
    bs_sem,
    br_sem,
    is_sem,
    ir_sem,
):
    at = Place()
    other_half = 1 - at.half
    width = 3 * lay.head_cols
    first_line = lay.mats[1][0]

    def load_in(half):
        cols = pl.ds(pl.multiple_of(half * lay.ffn_cols, LANES), lay.ffn_cols)
        return pltpu.make_async_copy(in_hbm.at[:, cols], staged_in, load_sem.at[0])

    def load_out(half):
        rows = pl.ds(pl.multiple_of(half * lay.ffn_cols, LANES), lay.ffn_cols)
        return pltpu.make_async_copy(out_hbm.at[rows, :], staged_out, load_sem.at[1])

    def load_attn(half):
        rows = pl.ds(pl.multiple_of(half * lay.head_cols, LANES), lay.head_cols)
        return pltpu.make_async_copy(attn_hbm.at[rows, :], staged_attn, load_sem.at[2])

    head_space = staged_attn.at[pl.ds(0, LANES)]

    def load_head(half):
        rows = pl.ds(pl.multiple_of(half * lay.head_cols, LANES), LANES)
        return pltpu.make_async_copy(attn_hbm.at[rows, :], head_space, load_sem.at[2])

    def load_row(row):
        rows = pl.ds(row * ROW, ROW)
        return [
            pltpu.make_async_copy(qkv_hbm.at[rows, :], qkv, row_sem.at[0]),
            pltpu.make_async_copy(mixed_hbm.at[rows, :], mixed, row_sem.at[1]),
        ]

    load_tokens = pltpu.make_async_copy(tokens_hbm, tokens, row_sem.at[2])

    def load_back(chunk):
        cols = pl.ds(chunk * 2 * LANES, 2 * LANES)
        return [
            pltpu.make_async_copy(weight_hbm.at[cols, :], weight, row_sem.at[3]),
            pltpu.make_async_copy(resid_hbm.at[:, cols], resid, row_sem.at[4]),
        ]

    def back_place(chunk, half):
        rows = pl.ds(pl.multiple_of(half * resid.shape[0], 16), resid.shape[0])
        return input_hbm.at[rows, pl.ds(chunk * 2 * LANES, 2 * LANES)]

    def store_back(chunk):
        return pltpu.make_async_copy(resid, back_place(chunk, at.half), row_sem.at[5])

    def share_back(chunk):
        return remote(
            resid, back_place(chunk, at.half), is_sem.at[chunk], ir_sem.at[chunk], at.sib
        )

    load_in(other_half).start()
    load_out(other_half).start()
    load_attn(other_half).start()
    for copy in load_row(0):
        copy.start()
    load_tokens.start()

    bar = pltpu.get_barrier_semaphore()
    me = at.dp * MP + at.half
    count = 16 * MP

    def peer(step):
        other = lax.rem(me + step, count)
        return (other // MP, lax.rem(other, MP))

    def greet(step, carry):
        pl.semaphore_signal(bar, inc=1, device_id=peer(step), device_id_type=MESH)
        return carry

    lax.fori_loop(1, count, greet, 0)
    sends = []

    def remote(src, dst, send_sem, recv_sem, dev):
        return pltpu.make_async_remote_copy(
            src_ref=src,
            dst_ref=dst,
            send_sem=send_sem,
            recv_sem=recv_sem,
            device_id=dev,
            device_id_type=MESH,
        )

    def later(cond, copy):
        sends.append((cond, lambda: copy().wait_send()))

    def lay_out(ref, offset, height, cols, base):
        def body(step, carry):
            row = pl.multiple_of(step * LANES, LANES)
            for col in range(cols):
                block = ref[pl.ds(row, LANES), col * LANES : (col + 1) * LANES]
                flat[pl.ds(offset - base + row * cols + col, LANES, stride=cols), :] = (
                    block.astype(jnp.float32)
                )
            return carry

        lax.fori_loop(0, height // LANES, body, 0)

    tail_from = lay.need // 16 * 16
    spare = lay.need - tail_from

    def emit(half, index, base):
        start = lay.starts[index] - base
        first, number = extra_lines(index)
        if number == 0:
            part[half, index] = flat[start : start + lay.length, :].astype(jnp.bfloat16)
            return
        part[half, index, :tail_from] = flat[start : start + tail_from, :].astype(jnp.bfloat16)
        tail[0:spare, :] = flat[start + tail_from : start + lay.need, :]
        tail[spare : spare + number, :] = extras[half, first : first + number, :]
        part[half, index, tail_from : tail_from + 16] = tail[...].astype(jnp.bfloat16)
        part[half, index, tail_from + 16 :] = jnp.zeros(
            (lay.length - tail_from - 16, LANES), jnp.bfloat16
        )

    def to_sib(index):
        return remote(
            part.at[other_half, index],
            from_sib.at[index],
            ss_sem.at[index],
            sr_sem.at[index],
            at.sib,
        )

    def emit_all(half, indices, base, share):
        for index in indices:
            emit(half, index, base)
            if share:
                to_sib(index).start()
                later(None, lambda index=index: to_sib(index))

    extras[...] = extra_ref[...]
    early = list(range(12, 16)) + list(range(8, 12)) + list(range(SPLIT, 8))
    late = list(range(SPLIT))
    tail[...] = jnp.zeros_like(tail)
    rows = flat.shape[0] - (lay.bias_start - first_line)
    for half, share in ((other_half, True), (at.half, False)):
        load_in(half).wait()
        lay_out(staged_in, *lay.mats[2], first_line)
        if share:
            load_in(at.half).start()
        load_out(half).wait()
        lay_out(staged_out, *lay.mats[3], first_line)
        if share:
            load_out(at.half).start()
            pl.semaphore_wait(bar, count - 1)
        load_attn(half).wait()
        lay_out(staged_attn, *lay.mats[1], first_line)
        if share:
            load_attn(at.half).start()
        flat[lay.bias_start - first_line :, :] = jnp.zeros((rows, LANES), jnp.float32)
        emit_all(half, early, first_line, share)
    load_head(other_half).start()

    my_part = part.at[at.half]

    def wait_sib(index):
        to_sib(index).wait_recv()

    def wide(ref, rows):
        return ref[rows, :].astype(jnp.float32)

    def add_span(dst, terms, begin, size):
        def body(step, carry):
            off = step * lay.step
            spans = [
                pl.ds(pl.multiple_of(first + off, 16), lay.step) for _, first in terms
            ]
            value = wide(terms[0][0], spans[0])
            for (ref, _), span in zip(terms[1:], spans[1:]):
                value = value + wide(ref, span)
            dst[pl.ds(pl.multiple_of(begin + off, 16), lay.step), :] = value.astype(dst.dtype)
            return carry

        lax.fori_loop(0, size // lay.step, body, 0)

    def diag_out(z, index, axis):
        mine = my_part.at[index]
        if axis == 0:
            return remote(
                mine.at[pl.ds(0, lay.cut)], diag_y.at[z], dy_sem.at[z, 0], dy_sem.at[z, 1], at.yn
            )
        return remote(
            mine.at[pl.ds(lay.cut, lay.cut)],
            diag_x.at[z],
            dx_sem.at[z, 0],
            dx_sem.at[z, 1],
            at.xn,
        )

    def diagonal(z):
        index = at.shard(z, 1 - at.y, 1 - at.x)
        wait_sib(index)
        mine = my_part.at[index]
        add_span(mine, [(mine, 0), (from_sib.at[index], 0)], 0, lay.length)
        for axis in range(2):
            diag_out(z, index, axis).start()
            later(None, lambda axis=axis: diag_out(z, index, axis))

    def plane_out(z, index, piece, to_y):
        rows = pl.ds(piece * lay.piece, lay.piece)
        if to_y:
            return remote(
                my_part.at[index, rows],
                from_y.at[z, rows],
                ys_sem.at[z, piece],
                yr_sem.at[z, piece],
                at.yn,
            )
        return remote(
            my_part.at[index, rows],
            from_x.at[z, rows],
            xs_sem.at[z, piece],
            xr_sem.at[z, piece],
            at.xn,
        )

    def plane(z):
        for to_y in range(2):
            y = 1 - at.y if to_y else at.y
            x = at.x if to_y else 1 - at.x
            index = at.shard(z, y, x)
            mine, sib = my_part.at[index], from_sib.at[index]
            wait_sib(index)
            diag_out(z, index, 1 if to_y else 0).wait_recv()
            for piece in range(PIECES):
                begin = piece * lay.piece
                terms = [(mine, begin), (sib, begin)]
                if to_y and begin >= lay.cut:
                    terms.append((diag_x.at[z], begin - lay.cut))
                if not to_y and begin < lay.cut:
                    terms.append((diag_y.at[z], begin))
                add_span(mine, terms, begin, lay.piece)
                plane_out(z, index, piece, to_y).start()
                later(
                    None,
                    lambda index=index, piece=piece, to_y=to_y: plane_out(
                        z, index, piece, to_y
                    ),
                )

    def chain_out(z, index, piece, dev, slot):
        rows = pl.ds(piece * lay.piece, lay.piece)
        return remote(
            my_part.at[index, rows],
            from_z.at[slot, rows],
            zs_sem.at[z, piece],
            zr_sem.at[slot, piece],
            dev,
        )

    def chain_in(slot, piece):
        return chain_out(0, at.dp, piece, at.sib, slot)

    def gather_terms(z, index, piece):
        plane_out(z, index, piece, 0).wait_recv()
        plane_out(z, index, piece, 1).wait_recv()
        begin = piece * lay.piece
        return [
            (my_part.at[index], begin),
            (from_sib.at[index], begin),
            (from_x.at[z], begin),
            (from_y.at[z], begin),
        ]

    def chain(z, hop):
        index = at.shard(z, at.y, at.x)
        for down in range(2):
            spot = 3 - hop if down else hop
            if (spot <= z) if down else (spot >= z):
                continue
            dev = at.down if down else at.up
            slot = 4 if down and spot - 1 == z else z
            cond = at.z == spot

            def work(dev=dev, slot=slot):
                wait_sib(index)
                for piece in range(PIECES):
                    terms = gather_terms(z, index, piece)
                    begin = piece * lay.piece
                    if hop > 0:
                        chain_in(z, piece).wait_recv()
                        terms.append((from_z.at[z], begin))
                    add_span(my_part.at[index], terms, begin, lay.piece)
                    chain_out(z, index, piece, dev, slot).start()

            guarded(cond, work)
            for piece in range(PIECES):
                later(
                    cond,
                    lambda piece=piece, dev=dev, slot=slot: chain_out(
                        z, index, piece, dev, slot
                    ),
                )

    tiles = lay.head_cols // LANES

    def attention(row, half):
        cols = pl.ds(half * width, width)
        attend_back_row(
            tiles,
            qkv.at[:, cols],
            mixed.at[:, pl.ds(half * lay.head_cols, lay.head_cols)],
            logs_ref.at[half, pl.ds(row * ROW, ROW)],
            seg_col_ref.at[pl.ds(row * ROW, ROW)],
            seg_wide_ref.at[row],
            qkv_grad.at[pl.ds(row * ROW, ROW), cols],
            key_acc,
            value_acc,
        )

    core_rows = qkv_grad.shape[0]

    def weights(half, share):
        ones = jnp.ones((16, core_rows), jnp.bfloat16)
        for section in range(3):
            cols = pl.ds(
                pl.multiple_of(half * width + section * lay.head_cols, LANES), lay.head_cols
            )
            grads = qkv_grad[:, cols]
            result = jnp.dot(tokens[...], grads, preferred_element_type=jnp.float32)
            for tile in range(tiles):
                flat[pl.ds(section * tiles + tile, lay.features, stride=3 * tiles), :] = (
                    result[:, tile * LANES : (tile + 1) * LANES]
                )
            if section != 1:
                sums = jnp.dot(ones, grads, preferred_element_type=jnp.float32)
                first = 0 if section == 0 else tiles
                for tile in range(tiles):
                    extras[half, first + tile : first + tile + 1, :] = sums[
                        0:1, tile * LANES : (tile + 1) * LANES
                    ]
        load_head(half).wait()
        lay_out(head_space, lay.mats[1][0], LANES, lay.mats[1][2], 0)
        if share:
            load_head(at.half).start()
        emit_all(half, late, 0, share)

    def back(chunk):
        for copy in load_back(chunk):
            copy.wait()
        for row in range(core_rows // ROW):
            rows = pl.ds(row * ROW, ROW)
            resid[rows, :] += lax.dot_general(
                qkv_grad[rows, :], weight[...], LAST, preferred_element_type=jnp.float32
            )
        store_back(chunk).start()
        share_back(chunk).start()

    diagonal(3)
    diagonal(2)
    diagonal(1)
    for copy in load_row(0):
        copy.wait()
    attention(0, 0)
    plane(3)
    attention(0, 1)
    for copy in load_row(1):
        copy.start()
    plane(2)
    for copy in load_row(1):
        copy.wait()
    attention(1, 0)
    plane(1)
    chain(3, 0)
    attention(1, 1)
    load_tokens.wait()
    chain(3, 1)
    chain(2, 0)
    weights(other_half, True)
    for copy in load_back(0):
        copy.start()
    weights(at.half, False)
    diagonal(0)
    chain(3, 2)
    chain(1, 0)
    chain(2, 1)
    back(0)
    plane(0)
    store_back(0).wait()
    share_back(0).wait_send()
    for copy in load_back(1):
        copy.start()
    chain(1, 1)
    back(1)
    chain(0, 0)
    store_back(1).wait()
    share_back(1).wait_send()
    for copy in load_back(2):
        copy.start()
    chain(0, 1)
    back(2)
    chain(0, 2)

    index = at.dp
    wait_sib(index)
    for piece in range(PIECES):
        begin = piece * lay.piece
        add_span(total, gather_terms(at.z, index, piece), begin, lay.piece)
    for down in range(2):
        slot = 4 if down else at.z

        @pl.when((at.z < 3) if down else (at.z > 0))
        def _(slot=slot):
            for piece in range(PIECES):
                chain_in(slot, piece).wait_recv()
                begin = piece * lay.piece
                add_span(total, [(total, begin), (from_z.at[slot], begin)], begin, lay.piece)

    scale = 1.0 / LOSS_SCALE
    phase = lax.rem(lax.axis_index("dp") * lay.shard, LANES)
    keep = lay.length - 8
    lanes = lane_ids(keep)
    spots = lax.broadcasted_iota(jnp.int32, (keep, LANES), 0) * LANES + lanes - phase
    lines = jnp.where((spots >= 0) & (spots < lay.shard), total[:keep, :] * scale, 0.0)
    extra = total[lay.need : lay.need + 3, :] * scale
    number = jnp.where(at.dp < SPLIT, 2, 3)
    for index in range(16):
        if extra_lines(index)[1] == 0:
            number = jnp.where(at.dp == index, 0, number)
    extra_rows = lax.broadcasted_iota(jnp.int32, (3, LANES), 0)
    stats[me, 0:1] = jnp.sum(lines * lines, 0, keepdims=True)
    stats[me, 1:4] = jnp.where(extra_rows < number, extra, 0.0)

    def tell(step):
        return remote(stats.at[me], stats.at[me], bs_sem.at[step], br_sem.at[step], peer(step))

    def hear(step):
        other = lax.rem(me + count - step, count)
        return remote(
            stats.at[other], stats.at[other], bs_sem.at[step], br_sem.at[step], peer(step)
        )

    def start_tell(step, carry):
        tell(step).start()
        return carry

    def finish(step, carry):
        hear(step).wait_recv()
        tell(step).wait_send()
        return carry

    lax.fori_loop(1, count, start_tell, 0)
    store_back(2).wait()
    share_back(2).wait_send()
    for chunk in range(3):
        share_back(chunk).wait_recv()
    for cond, work in sends:
        guarded(cond, work)
    lax.fori_loop(1, count, finish, 0)
    everyone = stats[...]
    squares = jnp.sum(everyone[:, 0])
    for row in range(3):
        squares = squares + jnp.sum(everyone[:, 1 + row] * everyone[:, 1 + row])
    norm_ref[...] = jnp.full((1, LANES), squares, jnp.float32)

    def extra_line(half, place):
        shard, row = extra_place(place)
        return stats.at[shard * MP + half, pl.ds(row, 1)]

    across = lay.features // LANES
    lines_half = 6 * across // MP
    for line in range(6 * across):
        half, place = line // lines_half, line % lines_half
        row, col = line // across, line % across
        shared_ref[row : row + 1, col * LANES : (col + 1) * LANES] = extra_line(
            half, lay.bias_lines + place
        )[...]

    @pl.when(at.dp == 15)
    def _():
        first = lay.bias_start - lay.starts[15]
        for place in range(lay.bias_lines):
            total[first + place : first + place + 1, :] = (
                extra_line(at.half, place)[...] * LOSS_SCALE
            )

    back_shift = lax.rem(LANES - phase, LANES)
    total[...] = pltpu.roll(total[...] * scale, back_shift, 1)
    grad_ref[:keep, :] = jnp.where(
        lanes < LANES - phase, total[:keep, :], total[1 : keep + 1, :]
    )
    grad_ref[keep:, :] = jnp.zeros((8, LANES), jnp.float32)


def finish_step(
    lay,
    ffn_grads,
    w_attn_grad,
    qkv,
    mixed_grad,
    tokens_turned,
    w_qkv,
    resid_grad,
    logs,
    seg_col,
    seg_row,
    in_sums,
    shared_step,
):
    across = lay.features // LANES
    lines_half = 6 * across // MP
    assert lay.starts[SPLIT] >= lay.mats[1][0] > lay.starts[SPLIT - 1]
    assert lay.starts[SPLIT - 1] + lay.length <= lay.mats[1][0] + LANES * lay.mats[1][2]
    assert lay.bias_lines + lines_half == 36 and 2 * lay.head_cols // LANES == LATE_LINES
    assert lay.need % 16 + 3 <= 16 and lay.length * LANES - lay.shard >= 8 * LANES
    heads = 2 * lay.head_cols // LANES
    extra = jnp.concatenate(
        [
            jnp.zeros((MP, heads, LANES), jnp.float32),
            in_sums.reshape(MP, -1, LANES),
            shared_step.reshape(MP, lines_half, LANES),
            jnp.zeros((MP, 4, LANES), jnp.float32),
        ],
        1,
    )
    flat_rows = -(-(lay.starts[15] + lay.length - lay.mats[1][0]) // 8) * 8
    core_rows = qkv.shape[0]
    size = (lay.length, LANES)
    low, full = jnp.bfloat16, jnp.float32
    vmem = pl.BlockSpec(memory_space=pltpu.VMEM)
    anywhere = pl.BlockSpec(memory_space=pl.ANY)
    scratch = pltpu.VMEM
    lines, squares, shared_grad, input_grad = pl.pallas_call(
        partial(finish_kernel, lay),
        out_shape=[
            jax.ShapeDtypeStruct(size, full),
            jax.ShapeDtypeStruct((1, LANES), full),
            jax.ShapeDtypeStruct(shared_step.shape, full),
            jax.ShapeDtypeStruct((MP * core_rows, lay.features), full),
        ],
        in_specs=[anywhere] * 8 + [vmem] * 4,
        out_specs=[vmem] * 3 + [anywhere],
        scratch_shapes=[
            scratch((lay.features, lay.ffn_cols), low),
            scratch((lay.ffn_cols, lay.features), low),
            scratch((lay.head_cols, lay.features), low),
            scratch((flat_rows, LANES), full),
            scratch((MP, 16) + size, low),
            scratch((16,) + size, low),
            scratch((4,) + size, low),
            scratch((4,) + size, low),
            scratch((4, lay.cut, LANES), low),
            scratch((4, lay.cut, LANES), low),
            scratch((5,) + size, low),
            scratch(size, full),
            scratch((16 * MP, STAT_ROWS, LANES), full),
            scratch((MP, 40, LANES), full),
            scratch((16, LANES), full),
            scratch((ROW, qkv.shape[1]), low),
            scratch((ROW, lay.features), low),
            scratch((lay.features, core_rows), low),
            scratch(qkv.shape, low),
            scratch((ROW, lay.head_cols), full),
            scratch((ROW, lay.head_cols), full),
            scratch((2 * LANES, qkv.shape[1]), low),
            scratch((core_rows, 2 * LANES), full),
            DMA((3,)),
            DMA((6,)),
            DMA((16,)),
            DMA((16,)),
            DMA((4, PIECES)),
            DMA((4, PIECES)),
            DMA((4, PIECES)),
            DMA((4, PIECES)),
            DMA((4, 2)),
            DMA((4, 2)),
            DMA((4, PIECES)),
            DMA((5, PIECES)),
            DMA((16 * MP,)),
            DMA((16 * MP,)),
            DMA((3,)),
            DMA((3,)),
        ],
        compiler_params=pltpu.CompilerParams(
            collective_id=1, has_side_effects=True, vmem_limit_bytes=VMEM_MOST
        ),
        name="finish_step",
    )(
        *ffn_grads,
        w_attn_grad,
        qkv,
        mixed_grad,
        tokens_turned,
        w_qkv,
        resid_grad,
        logs,
        seg_col,
        window_segments(seg_row),
        extra,
    )
    return input_grad, lines.reshape(1, -1), squares[0, 0], shared_grad


def scatter_gradients(lay, grads, bias_grad, shared_step):
    phase = (lax.axis_index("dp") * lay.shard) % LANES
    packed = pack_gradients(lay, grads, bias_grad)
    flat = packed.reshape(MP * lay.dp_count * lay.length, LANES)
    lines = lax.psum_scatter(flat, ("mp", "dp"), scatter_dimension=0, tiled=True)
    lines = lines.astype(jnp.float32).reshape(-1) / LOSS_SCALE
    lines = jnp.roll(lines, -phase)
    lines = jnp.where(jnp.arange(lines.size) < lay.shard, lines, 0.0)
    shared_grad = lax.psum(shared_step, ("dp", "mp")) / LOSS_SCALE
    squares = lax.psum(jnp.sum(lines * lines), ("dp", "mp"))
    squares = squares + jnp.sum(shared_grad * shared_grad)
    return lines.reshape(1, -1), squares, shared_grad


def ffn_back_kernel(
    grad_ref,
    hidden_ref,
    resid_ref,
    w_out_ref,
    w_in_ref,
    act_ref,
    slope_ref,
    out_grad_ref,
    in_grad_ref,
    sums_ref,
    total_ref,
    turned,
):
    first = pl.program_id(0) == 0

    @pl.when(first)
    def _():
        turned[...] = hidden_ref[...].T
        total_ref[...] = resid_ref[...]

    grad = grad_ref[...]
    act_grad = lax.dot_general(grad, w_out_ref[...], LAST, preferred_element_type=jnp.float32)
    up_grad = (act_grad * slope_ref[...].astype(jnp.float32)).astype(jnp.bfloat16)
    out_grad_ref[...] = lax.dot_general(
        act_ref[...], grad, FIRST, preferred_element_type=jnp.float32
    ).astype(jnp.bfloat16)
    in_grad_ref[...] = jnp.dot(
        turned[...], up_grad, preferred_element_type=jnp.float32
    ).astype(jnp.bfloat16)
    ones = jnp.ones((16, up_grad.shape[0]), jnp.bfloat16)
    sums_ref[...] = jnp.dot(ones, up_grad, preferred_element_type=jnp.float32)[0:8]
    total_ref[...] += lax.dot_general(
        up_grad, w_in_ref[...], LAST, preferred_element_type=jnp.float32
    )


def ffn_back(grad, hidden, resid, w_out, w_in, act, slope):
    rows, features = grad.shape
    units = act.shape[1]
    block = 512
    fixed = pl.BlockSpec(
        (rows, features), lambda i: (0, 0), pipeline_mode=pl.Buffered(1)
    )
    kept = pl.BlockSpec((rows, features), lambda i: (0, 0))
    across = pl.BlockSpec((rows, block), lambda i: (0, i))
    tall = pl.BlockSpec((block, features), lambda i: (i, 0))
    wide = pl.BlockSpec((features, block), lambda i: (0, i))
    shape = jax.ShapeDtypeStruct
    low, full = jnp.bfloat16, jnp.float32
    out_grad, in_grad, sums, total = pl.pallas_call(
        ffn_back_kernel,
        grid=(units // block,),
        in_specs=[fixed, fixed, fixed, tall, wide, across, across],
        out_specs=[tall, wide, pl.BlockSpec((8, block), lambda i: (0, i)), kept],
        out_shape=[
            shape((units, features), low),
            shape((features, units), low),
            shape((8, units), full),
            shape((rows, features), full),
        ],
        scratch_shapes=[pltpu.VMEM((features, rows), low)],
        compiler_params=pltpu.CompilerParams(vmem_limit_bytes=44 << 20),
        name="ffn_back",
    )(grad, hidden, resid, w_out, w_in, act, slope)
    return out_grad, in_grad, sums[0], total


def back_norm(values_in, scale_vec, grad):
    center = jnp.mean(values_in, -1, keepdims=True)
    centered = values_in - center
    inverse = lax.rsqrt(jnp.mean(centered * centered, -1, keepdims=True) + NORM_EPS)
    unit = centered * inverse
    scaled = grad * scale_vec
    out = inverse * (
        scaled
        - jnp.mean(scaled, -1, keepdims=True)
        - unit * jnp.mean(scaled * unit, -1, keepdims=True)
    )
    return out, jnp.sum(grad * unit, 0), jnp.sum(grad, 0)


def per_device(
    tokens,
    segments,
    sentence_dest,
    pair_source,
    labels,
    params,
    first,
    second,
    shared,
    shared_first,
    shared_second,
):
    features = tokens.shape[1]
    dp_count = lax.axis_size("dp")
    dp_index = lax.axis_index("dp")
    mp_index = lax.axis_index("mp")
    shard = params.shape[1]
    lay = Layout(features, shard, dp_count)
    head_cols = lay.head_cols
    sent_slots = ROWS_DEV * SEG
    slot_capacity = max(2, sent_slots // dp_count)
    params_total = MP * shard * dp_count + 6 * features
    core_rows = ROWS_CORE * ROW

    own = jnp.pad(params, ((0, 0), (0, lay.length * LANES - shard))).reshape(lay.length, LANES)
    tokens_core = lax.dynamic_slice_in_dim(tokens, mp_index * core_rows, core_rows, 0)
    segments_core = lax.dynamic_slice_in_dim(segments, mp_index * core_rows, core_rows, 0)
    seg_col = segments_core.reshape(core_rows, 1)
    seg_row = segments_core.reshape(ROWS_CORE, 1, ROW)
    head_lines = head_cols // LANES

    if dp_count == 16:
        w_qkv, w_attn, w_in, w_out, biases, qkv, mixed, logs = start_step(
            lay, own, tokens, seg_col, seg_row
        )
    else:
        w_qkv, w_attn, w_in, w_out, biases = unpack_weights(lay, gather_lines(lay, own))
        b_query = biases[:, :head_lines].reshape(MP, head_cols)
        b_value = biases[:, head_lines : 2 * head_lines].reshape(MP, head_cols)
        b_qkv = jnp.concatenate([b_query, jnp.zeros_like(b_query), b_value], 1).reshape(-1)
        qkv = jnp.dot(tokens_core, w_qkv, preferred_element_type=jnp.float32)
        qkv = (qkv + b_qkv).astype(jnp.bfloat16)
        mixed, logs = attend(qkv, seg_col, seg_row, head_cols)
    b_in = biases[:, 2 * head_lines : lay.bias_lines].reshape(MP * lay.ffn_cols)
    attn_out = jnp.dot(mixed, w_attn, preferred_element_type=jnp.float32) + shared[4]
    resid_one = tokens_core.astype(jnp.float32) + attn_out
    hidden = normalize(resid_one, shared[0], shared[1])
    hidden_low = hidden.astype(jnp.bfloat16)
    up_proj = jnp.dot(hidden_low, w_in, preferred_element_type=jnp.float32) + b_in
    cdf = 0.5 * (1.0 + lax.erf(up_proj * (0.5**0.5)))
    activated = (up_proj * cdf).astype(jnp.bfloat16)
    slope = (
        cdf + up_proj * jnp.exp(-0.5 * up_proj * up_proj) * ((2.0 * math.pi) ** -0.5)
    ).astype(jnp.bfloat16)
    ffn_out = jnp.dot(activated, w_out, preferred_element_type=jnp.float32) + shared[5]
    resid_two = hidden + ffn_out
    encoded_core = normalize(resid_two, shared[2], shared[3])

    slot_ids = jnp.arange(SEG, dtype=jnp.int32)
    onehot = (seg_row == slot_ids[None, :, None]).astype(jnp.float32)
    weight = onehot / jnp.sum(onehot, 2, keepdims=True)
    pooled_core = jnp.einsum(
        "kvf,kfo->kvo",
        weight,
        encoded_core.reshape(ROWS_CORE, ROW, features),
        precision=TOP_PRECISION,
    ).astype(jnp.bfloat16)
    pooled_grad, encoded = exchange(
        pooled_core.reshape(ROWS_CORE * SEG, features),
        encoded_core.astype(jnp.bfloat16),
        sentence_dest,
        pair_source,
        labels,
        dp_count,
        slot_capacity,
    )

    encoded_grad = jnp.einsum(
        "jix,jip->jxp",
        weight,
        pooled_grad.reshape(ROWS_CORE, SEG, features),
        precision=TOP_PRECISION,
    ).reshape(core_rows, features)
    resid_two_grad, scale_two, shift_two = back_norm(resid_two, shared[2], encoded_grad)
    ffn_grad = resid_two_grad.astype(jnp.bfloat16)
    w_out_grad, w_in_grad, in_sums, hidden_grad = ffn_back(
        ffn_grad, hidden_low, resid_two_grad, w_out, w_in, activated, slope
    )
    resid_one_grad, scale_one, shift_one = back_norm(resid_one, shared[0], hidden_grad)
    attn_grad = resid_one_grad.astype(jnp.bfloat16)
    w_attn_grad = lax.dot_general(mixed, attn_grad, FIRST, preferred_element_type=jnp.float32)
    mixed_grad = lax.dot_general(
        attn_grad, w_attn, LAST, preferred_element_type=jnp.float32
    ).astype(jnp.bfloat16)
    shared_step = jnp.stack(
        [
            scale_one,
            shift_one,
            scale_two,
            shift_two,
            jnp.sum(attn_grad.astype(jnp.float32), 0),
            jnp.sum(ffn_grad.astype(jnp.float32), 0),
        ]
    )
    ffn_grads = [w_in_grad, w_out_grad]
    w_attn_grad = w_attn_grad.astype(jnp.bfloat16)
    if dp_count == 16:
        input_grad, grad_lines, total_squares, shared_grad = finish_step(
            lay,
            ffn_grads,
            w_attn_grad,
            qkv,
            mixed_grad,
            tokens_core.T,
            w_qkv,
            resid_one_grad,
            logs,
            seg_col,
            seg_row,
            in_sums,
            shared_step,
        )
    else:
        qkv_grad = attend_back(qkv, mixed_grad, logs, seg_col, seg_row, head_cols)
        w_qkv_grad = lax.dot_general(
            tokens_core, qkv_grad, FIRST, preferred_element_type=jnp.float32
        ).astype(jnp.bfloat16)
        input_term = lax.dot_general(qkv_grad, w_qkv, LAST, preferred_element_type=jnp.float32)
        input_core = resid_one_grad + input_term
        qkv_sums = jnp.sum(qkv_grad.astype(jnp.float32), 0).reshape(MP, 3, head_lines, LANES)
        bias_grad = jnp.concatenate(
            [qkv_sums[:, 0], qkv_sums[:, 2], in_sums.reshape(MP, -1, LANES)], 1
        )
        bias_grad = jnp.pad(bias_grad, ((0, 0), (0, lay.bias_rows - lay.bias_lines), (0, 0)))
        grad_lines, total_squares, shared_grad = scatter_gradients(
            lay, [w_qkv_grad, w_attn_grad] + ffn_grads, bias_grad, shared_step
        )
        input_grad = lax.all_gather(input_core, "mp", axis=0, tiled=True)
    flat_grad = grad_lines[:, :shard]
    norm_value = jnp.sqrt(total_squares)
    factor = jnp.minimum(1.0, CLIP_NORM / norm_value)
    step_count = STEP_COUNT
    params_new, first_new, second_new = adamw(
        params, first, second, flat_grad, factor, step_count, LEARN_RATE
    )
    shared_new, shared_first_new, shared_second_new = adamw(
        shared, shared_first, shared_second, shared_grad, factor, step_count, SHARED_RATE
    )
    grad_unit = math.sqrt(params_total) / CLIP_NORM
    params_grad = flat_grad * factor * grad_unit
    shared_grad_out = shared_grad * factor * grad_unit
    return (
        encoded,
        input_grad,
        norm_value.reshape(1),
        params_new,
        first_new,
        second_new,
        params_new.astype(jnp.bfloat16),
        shared_new,
        shared_first_new,
        shared_second_new,
        params_grad,
        shared_grad_out,
    )


def solution(mesh):
    in_specs = (
        P("dp", None),
        P("dp"),
        P("dp", None),
        P("dp", None),
        P("dp"),
        P("mp", "dp"),
        P("mp", "dp"),
        P("mp", "dp"),
        P(),
        P(),
        P(),
    )
    out_specs = (
        P("dp", None),
        P("dp", None),
        P(),
        P("mp", "dp"),
        P("mp", "dp"),
        P("mp", "dp"),
        P("mp", "dp"),
        P(),
        P(),
        P(),
        P("mp", "dp"),
        P(),
    )
    return jax.shard_map(
        per_device, mesh=mesh, in_specs=in_specs, out_specs=out_specs, check_vma=False
    )
```
